32 devices in a mesh: dp: 32 (over z, y, x, core).
Axes of the slice: x: 2, y: 2, z: 4, core: 2. Of those that a mesh axis runs over, the one named last changes fastest.
Arguments:
- hidden_in: bfloat16 [4096, 1024], P('dp'), may hold values from -6 to 6
- seq_start: int32 [4096], P('dp'), may hold values from 0 to 1, as said below
- mixer_gain: bfloat16 [1, 1024], P(None, 'dp'), may hold values from 0.5 to 1.5
- in_weight: bfloat16 [1, 1024, 3072], P(None, 'dp'), may hold values from -0.1875 to 0.1875
- conv_weight: bfloat16 [1, 1024, 3], P(None, 'dp'), may hold values from -3.5 to 3.5
- out_weight: bfloat16 [1, 1024, 1024], P(None, 'dp'), may hold values from -0.1875 to 0.1875
- ffn_gain: bfloat16 [1, 1024], P(None, 'dp'), may hold values from 0.5 to 1.5
- gate_weight: bfloat16 [1, 1024, 4608], P(None, 'dp'), may hold values from -0.1875 to 0.1875
- up_weight: bfloat16 [1, 1024, 4608], P(None, 'dp'), may hold values from -0.1875 to 0.1875
- down_weight: bfloat16 [1, 4608, 1024], P(None, 'dp'), may hold values from -0.09375 to 0.09375
- cotangent: bfloat16 [4096, 1024], P('dp'), may hold values from -6 to 6
Outputs:
- hidden_out: bfloat16 [4096, 1024], P('dp')
- grad_hidden: float32 [4096, 1024], P('dp')
- grad_mixer_gain: float32 [1, 1024], P(None, 'dp')
- grad_in_weight: float32 [1, 1024, 3072], P(None, 'dp')
- grad_conv_weight: float32 [1, 1024, 3], P(None, 'dp')
- grad_out_weight: float32 [1, 1024, 1024], P(None, 'dp')
- grad_ffn_gain: float32 [1, 1024], P(None, 'dp')
- grad_gate_weight: float32 [1, 1024, 4608], P(None, 'dp')
- grad_up_weight: float32 [1, 1024, 4608], P(None, 'dp')
- grad_down_weight: float32 [1, 4608, 1024], P(None, 'dp')
The draws below stay inside these ranges and needn't reach their ends.
Inputs may be any that keep to these rules, and one draw needn't show every extreme that they name: `seq_start`: 1 marks the first token of a sequence; token 0 is marked, and 4 tokens are marked in all.
All inputs are finite; a program needn't handle non-finite values.
Results may differ from the reference program's by a relative error of at most 0.0098.
Values may be sent and summed in bfloat16 or wider, within the bound.
No kernel may reach another device: no remote copies, remote signals or barrier semaphores. Data moves between devices by JAX's collectives and lax.ppermute only.
A program may use at most 256 MiB of HBM per device.

```python
import jax
import jax.numpy as jnp
from jax import lax

D = 1024
FF = 4608
LAYERS = 1
SEQ = 1024
TOKENS = 4096


def draw_seq_start(key, part):
    shuffled = jax.random.permutation(key, TOKENS - 1) + 1
    marked = shuffled[:TOKENS // SEQ - 1]
    flag_rows = jnp.zeros((TOKENS,), jnp.int32).at[marked].set(1)
    return flag_rows.at[0].set(1)


def with_spikes(entries, rng, source, target, blocks, factor):
    owner, partner = [(jnp.arange(entries.shape[dim]) // (entries.shape[dim] // blocks)).reshape([-1 if axis == dim else 1 for axis in range(entries.ndim)]) for dim in (source, target)]
    chosen = jax.random.permutation(rng, blocks)[partner]
    strong = (owner == chosen) | (owner == (partner + blocks // 2) % blocks)
    return jnp.where(strong, factor * entries, entries)


def block_scale(rng, shape, split, least, top_value):
    def one(axis_at, blocks):
        heights = jax.random.uniform(jax.random.fold_in(jax.random.fold_in(rng, 6), axis_at), (blocks,), jnp.float32, least / len(split), top_value / len(split))
        return jnp.repeat(jnp.exp(heights), shape[axis_at] // blocks).reshape((-1,) + (1,) * (len(shape) - axis_at - 1))

    factor_of = one(*split[0])
    for cut in split[1:]:
        factor_of = factor_of * one(*cut)
    return factor_of


def gaussian(own_key, dims, width, most, cuts=(), kind=jnp.bfloat16):
    array = jax.random.normal(own_key, dims, jnp.float32) * width
    if len(cuts) > 0:
        array = block_scale(own_key, dims, cuts, -0.22, 0.18) * array
    return jnp.clip(array, min=-most, max=most).astype(kind)


def heavy_noise(rng, dims, spread, most, split, heavy, kind=jnp.bfloat16):
    drawn = spread * jax.random.normal(rng, dims, jnp.float32)
    if split:
        drawn = drawn * block_scale(rng, dims, split, -0.22, 0.18)
    return jnp.clip(with_spikes(drawn, jax.random.fold_in(rng, 3), *heavy), -most, most).astype(kind)


def setup_inputs(seed: int = 0) -> dict:
    splits = jax.random.split(jax.random.key(seed), 12)
    hidden_in = heavy_noise(splits[0], (TOKENS, D), 1.0, 6.0, ((0, 32),), (0, 1, 32, 2.75))
    seq_start = draw_seq_start(jax.random.fold_in(splits[11], 71), 0)
    mixer_gain = jnp.clip(1.0 + 0.1 * jax.random.normal(splits[2], (LAYERS, D), jnp.float32), 0.5, 1.5).astype(jnp.bfloat16)
    in_weight = gaussian(splits[3], (LAYERS, D, 3 * D), D ** -0.5, 0.1875, ((1, 32),))
    conv_weight = gaussian(splits[4], (LAYERS, D, 3), 3 ** -0.5, 3.5, ((1, 32),))
    out_weight = gaussian(splits[5], (LAYERS, D, D), D ** -0.5, 0.1875, ((1, 32),))
    ffn_gain = jnp.clip(1.0 + 0.1 * jax.random.normal(splits[6], (LAYERS, D), jnp.float32), 0.5, 1.5).astype(jnp.bfloat16)
    gate_weight = gaussian(splits[7], (LAYERS, D, FF), D ** -0.5, 0.1875, ((1, 32),))
    up_weight = gaussian(splits[8], (LAYERS, D, FF), D ** -0.5, 0.1875, ((1, 32),))
    down_weight = gaussian(splits[9], (LAYERS, FF, D), FF ** -0.5, 0.09375, ((1, 32),))
    cotangent = gaussian(splits[10], (TOKENS, D), 1.0, 6.0, ((0, 32),))
    return {"hidden_in": hidden_in, "seq_start": seq_start, "mixer_gain": mixer_gain, "in_weight": in_weight, "conv_weight": conv_weight, "out_weight": out_weight, "ffn_gain": ffn_gain, "gate_weight": gate_weight, "up_weight": up_weight, "down_weight": down_weight, "cotangent": cotangent}


epsilon = 1e-05

@jax.custom_vjp
def low(v):
    return lax.optimization_barrier(v.astype(jnp.bfloat16)).astype(jnp.float32)

@jax.custom_vjp
def low_back(v):
    return v

def low_keep(v):
    return (low(v), None)

def low_pass(kept, grad):
    return (grad,)

def back_keep(v):
    return (v, None)

def back_low(kept, grad):
    return (low(grad),)
low.defvjp(low_keep, low_pass)
low_back.defvjp(back_keep, back_low)

def product(left, right):
    return jnp.dot(left, right, precision=lax.Precision.HIGHEST, preferred_element_type=jnp.float32)

def rms_gain(values, gain):
    return values * lax.rsqrt(lax.optimization_barrier(jnp.mean(values * values, axis=1, keepdims=True)) + epsilon) * gain

def block_rows(weights, carried, values, flag_rows):
    mix_gain, in_proj, conv_taps, out_proj, ffn_scale, gate_proj, up_proj, down_proj = weights
    features = values.shape[1]
    normed_in = low(rms_gain(values, mix_gain))
    mixed = low_back(product(normed_in, in_proj))
    input_gate = mixed[:, :features]
    output_gate = mixed[:, features:2 * features]
    conv_input = mixed[:, 2 * features:]
    gated_in = low(input_gate * conv_input)
    current_saved = (1 - flag_rows).astype(jnp.float32)[:, None]
    previous_saved = jnp.concatenate([jnp.ones((1, 1), jnp.float32), current_saved[:-1]], 0)
    extended = jnp.concatenate([carried, gated_in], 0)
    conv_out = conv_taps[:, 2] * gated_in + conv_taps[:, 1] * (current_saved * extended[1:-1]) + conv_taps[:, 0] * (current_saved * previous_saved * extended[:-2])
    mixer_in = low(output_gate * conv_out)
    resid = values + low_back(product(mixer_in, out_proj))
    ffn_in = low(rms_gain(resid, ffn_scale))
    gate_val = low_back(product(ffn_in, gate_proj))
    up_val = low_back(product(ffn_in, up_proj))
    act_val = low(jax.nn.silu(gate_val) * up_val)
    result = resid + low_back(product(act_val, down_proj))
    next_carry = jnp.concatenate([gated_in[-2:-1] * current_saved[-1:], gated_in[-1:]], 0)
    return (next_carry, result)

def run_layer(values, weights, flag_rows):
    total_rows = values.shape[0]
    features = values.shape[1]
    block_size = min(4096, total_rows)
    block_count = total_rows // block_size

    def advance(carried, pieces):
        return block_rows(weights, carried, pieces[0], pieces[1])
    initial = jnp.zeros((2, features), jnp.float32)
    _, outputs = lax.scan(jax.checkpoint(advance), initial, (values.reshape(block_count, block_size, features), flag_rows.reshape(block_count, block_size)))
    return outputs.reshape(total_rows, features)

def reference(hidden_in, seq_start, mixer_gain, in_weight, conv_weight, out_weight, ffn_gain, gate_weight, up_weight, down_weight, cotangent):
    weights = (mixer_gain.astype(jnp.float32), in_weight.astype(jnp.float32), conv_weight.astype(jnp.float32), out_weight.astype(jnp.float32), ffn_gain.astype(jnp.float32), gate_weight.astype(jnp.float32), up_weight.astype(jnp.float32), down_weight.astype(jnp.float32))
    values = hidden_in.astype(jnp.float32)

    def forward(current, params):
        for layer_position in range(LAYERS):
            current = run_layer(current, tuple((item[layer_position] for item in params)), seq_start)
        return current
    result, pullback = jax.vjp(forward, values, weights)
    value_grad, weight_gradients = pullback(cotangent.astype(jnp.float32))
    return (result.astype(jnp.bfloat16), value_grad, weight_gradients[0], weight_gradients[1], weight_gradients[2], weight_gradients[3], weight_gradients[4], weight_gradients[5], weight_gradients[6], weight_gradients[7])
```

```python
import jax
import jax.numpy as jnp
from jax import lax
from jax.sharding import PartitionSpec as P

epsilon = 1e-05
TEAM = 8
HALO = 16
WIDE = jnp.float32
NARROW = jnp.bfloat16


def dot(left, right, contract):
    return lax.dot_general(left, right, (contract, ((), ())), preferred_element_type=WIDE)


class Layout:
    def __init__(self):
        self.count = lax.axis_size("dp")
        self.teams = self.count // TEAM
        index = lax.axis_index("dp")
        self.place = index % TEAM
        self.team = index // TEAM

    def swap(self, value, mask):
        return lax.ppermute(value, "dp", [(i, i ^ mask) for i in range(self.count)])

    def ring(self, value):
        return lax.ppermute(value, "dp", [(i, (i + TEAM) % self.count) for i in range(self.count)])

    def to_previous_team(self, value):
        return lax.ppermute(value, "dp", [(i, i - TEAM) for i in range(TEAM, self.count)])

    def team_blocks(self, value):
        half = value.shape[0] // 2
        across = self.swap(value, 2)
        along = self.swap(value, 4)
        twin = self.swap(value, 1)
        corner_top = self.swap(across[:half], 4)
        corner_low = self.swap(along[half:], 2)
        across_twin = self.swap(across, 1)
        along_twin = self.swap(along, 1)
        corner = jnp.concatenate([corner_top, corner_low], 0)
        corner_twin = self.swap(corner, 1)
        return [value, twin, across, across_twin, along, along_twin, corner, corner_twin]

    def team_rows(self, value):
        blocks = self.team_blocks(value)
        rows = value.shape[0]
        whole = jnp.zeros((TEAM * rows,) + value.shape[1:], value.dtype)
        for mask, block in enumerate(blocks):
            whole = lax.dynamic_update_slice(whole, block, ((self.place ^ mask) * rows, 0))
        return whole

    def team_sum(self, left, product):
        rows = left.shape[0] // TEAM
        half = rows // 2
        core = self.place % 2
        chip = self.place // 2
        split = left.reshape((TEAM // 2, 2, rows) + left.shape[1:])

        def side(which):
            part = lax.dynamic_index_in_dim(split, which, 1, keepdims=False)
            return product(part.reshape((TEAM // 2 * rows,) + left.shape[1:]))

        arrived = self.swap(side(1 - core).astype(NARROW), 1)
        both = side(core) + arrived.astype(WIDE)
        both = both.reshape((TEAM // 2, rows) + both.shape[1:])

        def block(mask):
            return lax.dynamic_index_in_dim(both, chip ^ mask, 0, keepdims=False)

        corner = block(3)
        by_across = self.swap(corner[:half].astype(NARROW), 2).astype(WIDE)
        by_along = self.swap(corner[half:].astype(NARROW), 4).astype(WIDE)
        to_across = block(1)
        to_along = block(2)
        to_across = jnp.concatenate([to_across[:half], to_across[half:] + by_along], 0)
        to_along = jnp.concatenate([to_along[:half] + by_across, to_along[half:]], 0)
        from_across = self.swap(to_across.astype(NARROW), 2)
        from_along = self.swap(to_along.astype(NARROW), 4)
        return block(0) + from_across.astype(WIDE) + from_along.astype(WIDE)

    def team_exchange(self, blocks):
        shape = blocks.shape
        view = blocks.reshape((2, 2, 2) + shape[1:])
        for dim, bit in ((1, 1), (0, 2), (2, 0)):
            mine = (self.place >> bit) & 1
            send = lax.dynamic_index_in_dim(view, 1 - mine, dim, keepdims=True)
            got = self.swap(send, 1 << bit)
            view = lax.dynamic_update_slice_in_dim(view, got, 1 - mine, dim)
        return view.reshape(shape)

    def across_teams(self, value, hold=None):
        rows = value.shape[0]
        whole = jnp.zeros((self.teams * rows,) + value.shape[1:], value.dtype)
        moving = value
        for step in range(self.teams):
            if step:
                moving = self.ring(moving)
            owner = (self.team - step) % self.teams
            whole = lax.dynamic_update_slice(whole, moving, (owner * rows, 0))
        return whole

    def sum_across_teams(self, value):
        rows = value.shape[0] // self.teams

        def share(step):
            owner = (self.team + step) % self.teams
            return lax.dynamic_slice(value, (owner * rows, 0), (rows, value.shape[1]))

        total = share(self.teams - 1)
        for step in range(self.teams - 2, -1, -1):
            total = share(step) + self.ring(total.astype(NARROW)).astype(WIDE)
        return total


def scale_of(values):
    return lax.rsqrt(jnp.mean(values * values, axis=1, keepdims=True) + epsilon)


def norm_back(upstream, normed, scaler, gain):
    scaled = upstream * gain
    return scaler * (scaled - normed * jnp.mean(scaled * normed, axis=1, keepdims=True))


def body(
    hidden_in,
    seq_start,
    mixer_gain,
    in_weight,
    conv_weight,
    out_weight,
    ffn_gain,
    gate_weight,
    up_weight,
    down_weight,
    cotangent,
):
    lay = Layout()
    teams = lay.teams
    rows, features = hidden_in.shape
    inner = gate_weight.shape[2]
    part = features // lay.count
    ffpart = inner // lay.count
    channels = features // TEAM
    ffown = inner // TEAM
    even = ffown // 128 * 128

    in_blocks = in_weight[0].reshape(part, 3, teams, TEAM, part)
    in_blocks = in_blocks.transpose(3, 0, 1, 2, 4).reshape(TEAM, part, 3 * channels)
    small = jnp.concatenate(
        [
            mixer_gain[0],
            ffn_gain[0],
            conv_weight[0].T.reshape(3 * part),
            seq_start.astype(NARROW),
        ]
    )
    small = jnp.pad(small, (0, 3 * channels - small.shape[0]))
    small_rows = jnp.zeros((TEAM, 8, 3 * channels), NARROW)
    small_rows = small_rows.at[:, 0].set(small)
    sent = jnp.concatenate([in_blocks, small_rows], 1)
    got = lay.team_exchange(sent)
    ring_in = jnp.concatenate(
        [
            got[:, :part].reshape(TEAM * part, 3 * channels),
            got[:, part],
            jnp.zeros((8, 3 * channels), NARROW),
        ],
        0,
    )
    in_rows = TEAM * part
    in_all = lay.across_teams(ring_in).reshape(teams, in_rows + 16, 3 * channels)
    in_own = in_all[:, :in_rows].reshape(features, 3 * channels)
    smalls = in_all[:, in_rows : in_rows + TEAM]

    def columns(weight):
        view = weight[0].reshape(part, teams, TEAM, ffpart)
        return view.transpose(2, 0, 1, 3).reshape(TEAM, part, ffown)

    gate_cols, up_cols = columns(gate_weight), columns(up_weight)
    pair = jnp.concatenate(
        [gate_cols[..., :even], up_cols[..., :even], gate_cols[..., even:], up_cols[..., even:]], 2
    )
    pair = lay.team_exchange(pair).reshape(TEAM * part, 2 * ffown)
    out_own = lay.across_teams(out_weight[0])
    down_own = lay.across_teams(down_weight[0])
    pair_own = lay.across_teams(pair)

    hidden = lay.team_rows(hidden_in)
    before = lay.ring(hidden[-HALO:])
    before = jnp.where(lay.team > 0, before, jnp.zeros_like(before))
    hidden = jnp.concatenate([before, hidden], 0).astype(WIDE)
    upstream = lay.team_blocks(cotangent)
    upstream = jnp.concatenate(upstream, 0)

    gains = smalls[:, :, : 2 * part].astype(WIDE)
    gain_one = gains[:, :, :part].reshape(1, features)
    gain_two = gains[:, :, part:].reshape(1, features)
    own_small = lax.dynamic_index_in_dim(smalls, lay.place, 1, keepdims=False).astype(WIDE)
    taps = own_small[:, 2 * part : 5 * part].reshape(teams, 3, part)
    taps = taps.transpose(1, 0, 2).reshape(3, channels)
    keep_all = 1.0 - smalls[:, :, 5 * part : 5 * part + rows].astype(WIDE)
    keep_own = lax.dynamic_index_in_dim(keep_all, lay.team, 0, keepdims=False)
    keep_last = lax.dynamic_index_in_dim(keep_all, (lay.team - 1) % teams, 0, keepdims=False)
    eye = jnp.eye(rows, dtype=WIDE)
    keep = jnp.sum(keep_own[:, None, :] * eye[None], axis=2).reshape(TEAM * rows, 1)
    keep_two = keep * jnp.concatenate([keep_last[-1:, -1:], keep[:-1]], 0)

    normed_one = hidden * scale_of(hidden)
    normed_in = (normed_one * gain_one).astype(NARROW)
    mixed = dot(normed_in, in_own, ((1,), (0,)))
    gated_in = (mixed[:, :channels] * mixed[:, 2 * channels :]).astype(NARROW).astype(WIDE)
    input_gate = mixed[HALO:, :channels]
    output_gate = mixed[HALO:, channels : 2 * channels]
    conv_input = mixed[HALO:, 2 * channels :]
    prior_one = keep * gated_in[HALO - 1 : -1]
    prior_two = keep_two * gated_in[HALO - 2 : -2]
    gated_in = gated_in[HALO:]
    conv_out = taps[2:3] * gated_in + taps[1:2] * prior_one + taps[0:1] * prior_two
    mixer_in = (output_gate * conv_out).astype(NARROW)
    own_hidden = hidden_in.astype(WIDE)
    resid = own_hidden + lay.team_sum(mixer_in, lambda x: dot(x, out_own, ((1,), (0,))))
    scale_two = scale_of(resid)
    normed_two = resid * scale_two
    ffn_in = (normed_two * gain_two).astype(NARROW)
    ffn_in = jnp.concatenate(lay.team_blocks(ffn_in), 0)

    gate_up = dot(ffn_in, pair_own, ((1,), (0,)))
    acts, gate_grads, up_grads = [], [], []
    act_grad = dot(upstream, down_own, ((1,), (1,)))
    spans = ((0, even, 0, even), (2 * even, even + ffown, even, ffown))
    for gate_at, up_at, start, stop in spans:
        width = stop - start
        gate_val = gate_up[:, gate_at : gate_at + width]
        up_val = gate_up[:, up_at : up_at + width]
        sigmoid = jax.nn.sigmoid(gate_val)
        acts.append((gate_val * sigmoid * up_val).astype(NARROW))
        grad = act_grad[:, start:stop]
        gate_grads.append(
            (grad * up_val * sigmoid * (1.0 + gate_val * (1.0 - sigmoid))).astype(NARROW)
        )
        up_grads.append((grad * gate_val * sigmoid).astype(NARROW))
    act_val = jnp.concatenate(acts, 1)
    pair_grad = jnp.concatenate([gate_grads[0], up_grads[0], gate_grads[1], up_grads[1]], 1)

    def by_place(blocks):
        view = blocks.reshape(TEAM, rows, blocks.shape[1])
        whole = jnp.zeros_like(view)
        for mask in range(TEAM):
            whole = lax.dynamic_update_slice(
                whole, view[mask : mask + 1], (lay.place ^ mask, 0, 0)
            )
        return whole.reshape(blocks.shape)

    ffn_grad = lay.team_sum(by_place(pair_grad), lambda x: dot(x, pair_own, ((1,), (1,))))
    own_upstream = cotangent.astype(WIDE)
    resid_grad = own_upstream + norm_back(ffn_grad, normed_two, scale_two, gain_two)
    mixer_out_grad = lay.team_rows(resid_grad.astype(NARROW))

    down_grad = lay.sum_across_teams(dot(act_val, upstream, ((0,), (0,))))
    pair_weight_grad = lay.sum_across_teams(dot(ffn_in, pair_grad, ((0,), (0,))))
    ffn_out = lay.team_sum(by_place(act_val), lambda x: dot(x, down_own, ((1,), (0,))))
    hidden_out = (resid + ffn_out).astype(NARROW)

    out_grad = dot(mixer_in, mixer_out_grad, ((0,), (0,)))
    mixer_in_grad = dot(mixer_out_grad, out_own, ((1,), (1,)))
    conv_grad = mixer_in_grad * output_gate
    output_gate_grad = mixer_in_grad * conv_out
    taps_grad = jnp.stack(
        [
            jnp.sum(conv_grad * prior_two, axis=0),
            jnp.sum(conv_grad * prior_one, axis=0),
            jnp.sum(conv_grad * gated_in, axis=0),
        ],
        0,
    )
    to_one = taps[1:2] * keep * conv_grad
    to_two = taps[0:1] * keep_two * conv_grad
    rim = jnp.concatenate([to_two[0:1], to_two[1:2] + to_one[0:1]], 0)
    returned = lay.to_previous_team(rim)
    from_one = jnp.concatenate([to_one[1:], jnp.zeros((1, channels), WIDE)], 0)
    from_two = jnp.concatenate([to_two[2:], returned], 0)
    gated_grad = taps[2:3] * conv_grad + from_one + from_two
    mixed_grad = jnp.concatenate(
        [gated_grad * conv_input, output_gate_grad, gated_grad * input_gate], 1
    ).astype(NARROW)
    normed_grad = lay.team_sum(mixed_grad, lambda x: dot(x, in_own, ((1,), (1,))))
    scale_one = scale_of(own_hidden)
    grad_hidden = resid_grad + norm_back(
        normed_grad, own_hidden * scale_one, scale_one, gain_one
    )

    taps_rows = taps_grad.reshape(3, teams, part).transpose(1, 0, 2)
    taps_rows = jnp.pad(taps_rows, ((0, 0), (0, 13), (0, features - part)))
    out_pack = jnp.concatenate([out_grad.reshape(teams, part, features), taps_rows], 1)
    out_pack = lay.sum_across_teams(out_pack.reshape(teams * (part + 16), features))
    grad_out = out_pack[:part]
    grad_conv = out_pack[part : part + 3, :part].T

    in_grad = lay.sum_across_teams(dot(normed_in[HALO:], mixed_grad, ((0,), (0,))))
    in_grad = lay.team_exchange(in_grad.astype(NARROW).reshape(TEAM, part, 3 * channels))
    in_grad = in_grad.astype(WIDE).reshape(TEAM, part, 3, teams, part)
    in_grad = in_grad.transpose(1, 2, 3, 0, 4).reshape(part, 3 * features)
    pair_back = lay.team_exchange(
        pair_weight_grad.astype(NARROW).reshape(TEAM, part, 2 * ffown)
    ).astype(WIDE)

    def uncolumns(cols):
        view = cols.reshape(TEAM, part, teams, ffpart)
        return view.transpose(1, 2, 0, 3).reshape(part, inner)

    grad_gate = uncolumns(
        jnp.concatenate([pair_back[..., :even], pair_back[..., 2 * even : even + ffown]], 2)
    )
    grad_up = uncolumns(
        jnp.concatenate([pair_back[..., even : 2 * even], pair_back[..., even + ffown :]], 2)
    )
    grad_mixer_gain = jnp.sum(in_weight[0].astype(WIDE) * in_grad, axis=1)
    grad_mixer_gain = grad_mixer_gain / mixer_gain[0].astype(WIDE)
    grad_ffn_gain = jnp.sum(
        gate_weight[0].astype(WIDE) * grad_gate + up_weight[0].astype(WIDE) * grad_up, axis=1
    )
    grad_ffn_gain = grad_ffn_gain / ffn_gain[0].astype(WIDE)
    return (
        hidden_out,
        grad_hidden,
        grad_mixer_gain[None],
        in_grad[None],
        grad_conv[None],
        grad_out[None],
        grad_ffn_gain[None],
        grad_gate[None],
        grad_up[None],
        down_grad[None],
    )


def solution(mesh):
    tokens, wide, deep = P("dp", None), P(None, "dp"), P(None, "dp", None)
    return jax.shard_map(
        body,
        mesh=mesh,
        in_specs=(tokens, P("dp"), wide, deep, deep, deep, wide, deep, deep, deep, tokens),
        out_specs=(tokens, tokens, wide, deep, deep, deep, wide, deep, deep, deep),
        check_vma=False,
    )
```

```python
import jax
import jax.numpy as jnp
from jax import lax
from jax.experimental import pallas as pl
from jax.experimental.pallas import tpu as pltpu
from jax.sharding import PartitionSpec as P

epsilon = 1e-05
TEAM = 8
HALO = 16
WIDE = jnp.float32
NARROW = jnp.bfloat16


def dot(left, right, contract):
    return lax.dot_general(left, right, (contract, ((), ())), preferred_element_type=WIDE)


def fetch(pairs, sems):
    copies = [pltpu.make_async_copy(a, b, sems.at[i]) for i, (a, b) in enumerate(pairs)]
    for copy in copies:
        copy.start()
    return copies


def shape(kind, *sizes):
    return jax.ShapeDtypeStruct(sizes, kind)


def call(kernel, name, out_shape, operands, scratch=(), flops=0, in_place=False):
    places = {}
    if in_place:
        places["in_specs"] = [pl.BlockSpec(memory_space=pl.ANY)] * len(operands)
    size = sum(x.size * x.dtype.itemsize for x in operands)
    return pl.pallas_call(
        kernel,
        out_shape=out_shape,
        scratch_shapes=list(scratch),
        compiler_params=pltpu.CompilerParams(vmem_limit_bytes=60 * 2**20),
        cost_estimate=pl.CostEstimate(flops=flops, bytes_accessed=size, transcendentals=0),
        name=name,
        **places,
    )(*operands)


def result_of(results, at):
    return lambda k: results[k][at]


class Job:
    def __init__(self, steps):
        self.steps = steps
        self.result = None
        self.open = True
        self.request = None
        self.held = False
        self.send(None)

    def send(self, value):
        try:
            self.request = self.steps.send(value)
        except StopIteration as stop:
            self.result, self.open, self.request = stop.value, False, None


class Net:
    def __init__(self):
        self.count = lax.axis_size("dp")
        self.teams = self.count // TEAM
        self.index = lax.axis_index("dp")
        self.place = self.index % TEAM
        self.team = self.index // TEAM
        self.core = self.index % 2
        self.peer = (self.index // 2) % 4
        self.jobs = []
        self.waiting = []
        self.gate = []
        self.extra = []

    def pairs(self, move):
        if move[0] == "swap":
            return [(i, i ^ move[1]) for i in range(self.count)]
        if move[0] == "ring":
            return [(i, (i + move[1] * TEAM) % self.count) for i in range(self.count)]
        if move[0] == "mixed":
            return [(i, i ^ (2 if i % 2 == 0 else 4)) for i in range(self.count)]
        return [(i, i - TEAM) for i in range(TEAM, self.count)]

    def do(self, call, *operands):
        def steps():
            (got,) = yield [(operands, ("call", call))]
            return got

        return self.spawn(steps())

    def spawn(self, steps):
        job = Job(steps)
        if job.open:
            self.jobs.append(job)
        return job

    def need(self, *values):
        self.extra.extend(values)

    def while_moving(self, values):
        mark = [got for move, got in self.raw if move == ("swap", 1)][0]
        return lax.optimization_barrier((values, mark))[0]

    def later(self, *values):
        return lax.optimization_barrier((values, self.gate))[0]

    def step(self, times=1):
        for _ in range(times):
            self.one_step()

    def one_step(self):
        ready = [job for job in self.jobs if job.request is not None and not job.held]
        values = [move[0] for job in ready for move in job.request]
        self.raw = []
        if values or self.waiting:
            values, _ = lax.optimization_barrier((values, (self.gate, self.extra)))
            self.extra = []
            at = 0
            for job in ready:
                span = 1
                got = []
                moves = job.request
                for move in moves:
                    if len(move) > 2:
                        span = move[2]
                    if move[1][0] == "call":
                        got.append(move[1][1](*values[at]))
                    else:
                        got.append(lax.ppermute(values[at], "dp", self.pairs(move[1])))
                    at += 1
                job.request = None
                self.raw.extend(zip([move[1] for move in moves], got))
                self.waiting.append([span, job, got])
        for entry in self.waiting:
            entry[0] -= 1
        done = [entry for entry in self.waiting if entry[0] <= 0]
        self.waiting = [entry for entry in self.waiting if entry[0] > 0]
        results = lax.optimization_barrier([entry[2] for entry in done])
        self.gate = results
        for (_, job, _), got in zip(done, results):
            job.send(got)
        self.jobs = [job for job in self.jobs if job.open]

    def until(self, *jobs):
        while any(job.open for job in jobs):
            self.one_step()
        return [job.result for job in jobs] if len(jobs) > 1 else jobs[0].result


    def blocks(self, value):
        across, along, twin = yield [
            (value, ("swap", 2)),
            (value, ("swap", 4)),
            (value, ("swap", 1)),
        ]
        corner, across_twin, along_twin = yield [
            (jnp.where(self.core == 0, along, across), ("mixed",)),
            (across, ("swap", 1)),
            (along, ("swap", 1)),
        ]
        (corner_twin,) = yield [(corner, ("swap", 1))]
        return [value, twin, across, across_twin, along, along_twin, corner, corner_twin]

    def team_sum(self, even, odd):
        arrived, even = yield [(odd, ("swap", 1)), (even[1], ("call", even[0]))]
        ((own, across, along, corner),) = yield [((even, arrived), ("call", fold_twin))]
        (by,) = yield [(corner, ("mixed",))]
        across, along = fold_corner(across, along, by)
        from_across, from_along = yield [(across, ("swap", 2)), (along, ("swap", 4))]
        return own, from_across, from_along

    def exchange(self, blocks):
        groups = [[base + q for q in range(TEAM)] for base in range(0, self.count, TEAM)]
        return lax.all_to_all(blocks, "dp", 0, 0, axis_index_groups=groups, tiled=True)

    def line_exchange(self, blocks):
        groups = [
            [TEAM * z + 2 * u + c for z in range(self.teams) for c in range(2)] for u in range(4)
        ]
        return lax.all_to_all(blocks, "dp", 0, 0, axis_index_groups=groups, tiled=True)

    def peer_groups(self):
        chips = range(0, self.count, TEAM)
        return [[base + c + 2 * u for u in range(4)] for base in chips for c in range(2)]

    def ring_blocks(self, value, found):
        moving = value
        for step in range(self.teams):
            moves = [(moving, ("swap", 1))]
            if step < self.teams - 1:
                moves.append((moving, ("ring", 1)))
            got = yield moves
            found.append((moving, got[0]))
            moving = got[-1]

    def ring_through(self, value, found, results, compute):
        teams = self.teams
        moving, total, twins = value, None, {}
        for step in range(teams + 3):
            moves, tags = [], []
            k, ready = (step - 2) % teams, (step - 1) % teams
            if step < teams:
                moves.append((moving, ("swap", 1)))
                tags.append("twin")
                if step < teams - 1:
                    moves.append((moving, ("ring", 1)))
                    tags.append("next")
            if step > 2:
                moves.append((results[k][3], ("swap", 1)))
                tags.append("back")
            hop = step - 3
            if 1 <= hop <= teams - 1:
                mine = results[hop][2] + twins[hop].astype(WIDE)
                if total is not None:
                    mine = mine + total.astype(WIDE)
                moves.append((mine.astype(NARROW), ("ring", 1)))
                tags.append("total")
            if 2 <= step <= teams + 1:
                call, operands = compute(ready, found[ready])
                moves.append((operands, ("call", call)))
                tags.append("work")
            got = dict(zip(tags, (yield moves)))
            if "twin" in got:
                found.append((moving, got["twin"]))
                moving = got.get("next")
            if "back" in got:
                twins[k] = got["back"]
            if "work" in got:
                results[ready] = got["work"]
            total = got.get("total", total)
        return results[0][2], twins[0], total

    def ring_sum(self, own, odd):
        order = list(range(1, self.teams)) + [0]
        total = None
        (twin,) = yield [(odd(order[0]), ("swap", 1))]
        for step, k in enumerate(order):
            if k == 0:
                return own(k), twin, total
            mine = own(k) + twin.astype(WIDE)
            if total is not None:
                mine = mine + total.astype(WIDE)
            total, twin = yield [
                (mine.astype(NARROW), ("ring", 1)),
                (odd(order[step + 1]), ("swap", 1)),
            ]

    def line_blocks(self, value):
        found = [value]
        for _ in range(1, self.teams):
            (value,) = yield [(value, ("ring", 1))]
            found.append(value)
        return found

    def line_send(self, parts, span=1):
        return (yield [(part, ("ring", k + 1), span) for k, part in enumerate(parts)])

    def line_sum(self, shares):
        total = shares[-1].astype(NARROW)
        for share in reversed(shares[:-1]):
            (got,) = yield [(total, ("ring", 1))]
            total = share + got.astype(WIDE)
            total = total if share is shares[0] else total.astype(NARROW)
        return total

    def line_all(self, value, span=1):
        return [value] + (yield from self.line_send([value] * (self.teams - 1), span))


def scale_of(values):
    return lax.rsqrt(jnp.mean(values * values, axis=1, keepdims=True) + epsilon)


def norm_back(upstream, normed, scaler, gain):
    scaled = upstream * gain
    return scaler * (scaled - normed * jnp.mean(scaled * normed, axis=1, keepdims=True))


def where_am_i():
    index = lax.axis_index("dp")
    return index % TEAM, index // TEAM


def at(start, size, step=16):
    return pl.ds(pl.multiple_of(start, step), size)


def fold_twin(even, arrived):
    rows, width = even.shape[0] // 4, even.shape[1]

    def kernel(even, arrived, own, across, along, corner):
        for k, out in enumerate((own, across, along, corner)):
            span = slice(k * rows, (k + 1) * rows)
            out[...] = (even[span, :] + arrived[span, :].astype(WIDE)).astype(out.dtype)

    outs = (shape(WIDE, rows, width),) * 3 + (shape(NARROW, rows, width),)
    return call(kernel, "fold_twin", outs, (even, arrived))


def fold_corner(across, along, by):
    def kernel(across, along, by, out_across, out_along):
        even_core = lax.axis_index("dp") % 2 == 0
        by = by[...].astype(WIDE)
        none = jnp.zeros_like(by)
        out_across[...] = (across[...] + jnp.where(even_core, none, by)).astype(NARROW)
        out_along[...] = (along[...] + jnp.where(even_core, by, none)).astype(NARROW)

    return call(kernel, "fold_corner", (shape(NARROW, *by.shape),) * 2, (across, along, by))


def pieces(ffpart, even, own):
    runs = []
    for u in range(4):
        for start, stop in ((0, even), (even, own)):
            low, high = max(u * ffpart, start), min((u + 1) * ffpart, stop)
            if low < high:
                at_gate = low if start == 0 else 2 * even + low - even
                at_up = even + low if start == 0 else own + low
                runs.append((u, low, high, at_gate, at_up))
    return runs


def in_prepare(weight, gains, marks, taps, teams):
    part, width = weight.shape
    features = width // 3
    channels = features // TEAM
    slots = max(128, TEAM * part) // part

    def kernel(weight, gain_one, gain_two, marks, taps, out, wide, small):
        index = lax.axis_index("dp")
        whole = weight[...].astype(WIDE)
        small[...] = jnp.zeros_like(small)
        for slot in range(slots):
            mine = lax.rem(index, slots) == slot
            for row, gain in enumerate((gain_one, gain_two)):
                value = gain[...].astype(WIDE)
                value = jnp.where(mine, value, jnp.zeros_like(value))
                small[row : row + 1, slot * part : (slot + 1) * part] = value
        small[0:1, 2 * channels :] = marks[...].astype(WIDE)
        for slot in range(teams):
            value = taps[...].astype(WIDE)
            value = jnp.where(index // TEAM == slot, value, jnp.zeros_like(value))
            for k in range(3):
                to = k * channels + slot * part
                small[2:3, to : to + part] = value[k : k + 1, :]
        for p in range(TEAM):
            for k in range(3):
                for z in range(teams):
                    source = k * features + (z * TEAM + p) * part
                    to = k * channels + z * part
                    wide[:, to : to + part] = whole[:, source : source + part]
            out[p, :part, :] = wide[...].astype(NARROW)
            out[p, part:, :] = small[...].astype(NARROW)

    return call(
        kernel,
        "in_prepare",
        shape(NARROW, TEAM, part + 8, 3 * channels),
        (weight, *gains, marks, taps),
        [pltpu.VMEM((part, 3 * channels), WIDE), pltpu.VMEM((8, 3 * channels), WIDE)],
    )


def in_finish(blocks, weight, gain, teams):
    part, width = weight.shape
    features = width // 3
    channels = features // TEAM

    def kernel(blocks, weight, gain, out, gain_grad):
        for p in range(TEAM):
            block = blocks[p].astype(WIDE)
            for k in range(3):
                for z in range(teams):
                    to = k * features + (z * TEAM + p) * part
                    source = k * channels + z * part
                    out[:, to : to + part] = block[:, source : source + part]
        product = jnp.sum(weight[...].astype(WIDE) * out[...], axis=1, keepdims=True)
        gain_grad[...] = product / gain[...].astype(WIDE)

    outs = (shape(WIDE, part, width), shape(WIDE, part, 1))
    return call(kernel, "in_finish", outs, (blocks, weight, gain))


def pair_prepare(gate, up, teams):
    part, inner = gate.shape
    ffpart = inner // (TEAM * teams)
    own = 4 * ffpart
    even = own // 128 * 128
    runs = pieces(ffpart, even, own)

    def kernel(gate, up, out, wide):
        gates, ups = gate[...].astype(WIDE), up[...].astype(WIDE)
        for z in range(teams):
            for c in range(2):
                for u, low, high, at_gate, at_up in runs:
                    source = ((z * 4 + u) * 2 + c) * ffpart + low - u * ffpart
                    size = high - low
                    wide[:, at_gate : at_gate + size] = gates[:, source : source + size]
                    wide[:, at_up : at_up + size] = ups[:, source : source + size]
                out[2 * z + c] = wide[...].astype(NARROW)

    out = shape(NARROW, 2 * teams, part, 2 * own)
    scratch = [pltpu.VMEM((part, 2 * own), WIDE)]
    return call(kernel, "pair_prepare", out, (gate, up), scratch)


def pair_finish(blocks, gate, up, gain, teams):
    part, inner = gate.shape
    ffpart = inner // (TEAM * teams)
    own = 4 * ffpart
    even = own // 128 * 128
    runs = pieces(ffpart, even, own)

    def kernel(blocks, gate, up, gain, gate_grad, up_grad, gain_grad):
        for z in range(teams):
            for c in range(2):
                block = blocks[2 * z + c].astype(WIDE)
                for u, low, high, at_gate, at_up in runs:
                    to = ((z * 4 + u) * 2 + c) * ffpart + low - u * ffpart
                    size = high - low
                    gate_grad[:, to : to + size] = block[:, at_gate : at_gate + size]
                    up_grad[:, to : to + size] = block[:, at_up : at_up + size]
        product = gate[...].astype(WIDE) * gate_grad[...] + up[...].astype(WIDE) * up_grad[...]
        gain_grad[...] = jnp.sum(product, axis=1, keepdims=True) / gain[...].astype(WIDE)

    outs = (shape(WIDE, part, inner), shape(WIDE, part, inner), shape(WIDE, part, 1))
    return call(kernel, "pair_finish", outs, (blocks, gate, up, gain))


def mixer_forward(blocks, before, weights):
    rows, features = blocks[0].shape
    tokens = TEAM * rows
    teams = len(weights)
    share = features // teams
    channels = weights[0].shape[2] // 3
    part = share // TEAM

    def kernel(*refs):
        blocks, refs = refs[:TEAM], refs[TEAM:]
        before, refs = refs[0], refs[1:]
        weights, refs = refs[:teams], refs[teams:]
        normed, mixed, gated, conv, mixer_in, in_own, gain, gain_two, taps, keeps = refs[:10]
        hs, small, sems = refs[10:]
        place, team = where_am_i()
        copies = []
        for k in range(teams):
            owner = lax.rem(team - k + teams, teams)
            for p in range(TEAM):
                to = in_own.at[at(owner * share + p * part, part, 8), :]
                copies.append((weights[k].at[p, :part, :], to))
            copies.append((weights[k].at[:, part:, :], small.at[k]))
        for m in range(TEAM):
            copies.append((blocks[m], hs.at[at(HALO + (place ^ m) * rows, rows), :]))
        copies.append((before, hs.at[:HALO, :]))
        for copy in fetch(copies, sems):
            copy.wait()
        first = hs[:HALO, :]
        hs[:HALO, :] = jnp.where(team > 0, first, jnp.zeros_like(first))
        total = jnp.zeros((1, 3 * channels), WIDE)
        gain[...] = jnp.zeros_like(gain)
        gain_two[...] = jnp.zeros_like(gain_two)
        span = max(share, 128)
        for k in range(teams):
            owner = lax.rem(team - k + teams, teams)
            both = sum(small[k, p].astype(WIDE) for p in range(TEAM))
            one, two = both[0:1], both[1:2]
            total = total + small[k, place].astype(WIDE)[2:3]
            to = at(owner * share // span * span, span, 128)
            gain[:, to] = gain[:, to] + one[:, :span]
            gain_two[:, to] = gain_two[:, to] + two[:, :span]
        taps[...] = jnp.zeros_like(taps)
        for k in range(3):
            taps[k : k + 1, :] = total[:, k * channels : (k + 1) * channels]
        marks = [1.0 - small[0, p].astype(WIDE)[0:1, 2 * channels :] for p in range(TEAM)]
        keep = jnp.concatenate([mark.reshape(rows, 1) for mark in marks], 0)
        keeps[8:, 0:1] = keep
        last = 1.0 - small[1, TEAM - 1].astype(WIDE)[0:1, 3 * channels - 1 :]
        keeps[7:8, 0:1] = last
        keeps[8:, 1:2] = keep * keeps[7 : 7 + tokens, 0:1]
        scale = gain[...]

        def norm(start, size):
            values = hs[at(start, size), :].astype(WIDE)
            values = values * scale_of(values) * scale
            normed[at(start, size), :] = values.astype(NARROW)

        norm(0, HALO)

        @pl.loop(0, TEAM)
        def _(step):
            norm(HALO + step * rows, rows)

        mixed[...] = dot(normed[...], in_own[...], ((1,), (0,)))
        gated[...] = (mixed[:, :channels] * mixed[:, 2 * channels :]).astype(NARROW).astype(WIDE)
        conv_out = (
            taps[2:3, :] * gated[HALO:, :]
            + taps[1:2, :] * (keeps[8:, 0:1] * gated[HALO - 1 : HALO - 1 + tokens, :])
            + taps[0:1, :] * (keeps[8:, 1:2] * gated[HALO - 2 : HALO - 2 + tokens, :])
        )
        conv[...] = conv_out
        mixer_in[...] = (mixed[HALO:, channels : 2 * channels] * conv_out).astype(NARROW)

    outs = (
        shape(NARROW, HALO + tokens, features),
        shape(WIDE, HALO + tokens, 3 * channels),
        shape(WIDE, HALO + tokens, channels),
        shape(WIDE, tokens, channels),
        shape(NARROW, tokens, channels),
        shape(NARROW, features, 3 * channels),
        shape(WIDE, 1, features),
        shape(WIDE, 1, features),
        shape(WIDE, 8, channels),
        shape(WIDE, 8 + tokens, 2),
    )
    return call(
        kernel,
        "mixer_forward",
        outs,
        (*blocks, before, *weights),
        [
            pltpu.VMEM((HALO + tokens, features), NARROW),
            pltpu.VMEM((teams, TEAM, 8, 3 * channels), NARROW),
            pltpu.SemaphoreType.DMA(((teams + 1) * (TEAM + 1),)),
        ],
        2 * tokens * features * 3 * channels,
        in_place=True,
    )


def out_project(mixer_local, out_blocks, hidden, gain):
    rows, features = hidden.shape

    def kernel(local, *refs):
        out_blocks, (hidden, gain, resid, ffn_in) = refs[:TEAM], refs[TEAM:]
        place, _ = where_am_i()
        total = hidden[...].astype(WIDE)
        for m in range(TEAM):
            total = total + dot(local[place ^ m], out_blocks[m][...], ((1,), (0,)))
        resid[...] = total
        ffn_in[...] = (total * scale_of(total) * gain[...]).astype(NARROW)

    outs = (shape(WIDE, rows, features), shape(NARROW, rows, features))
    return call(
        kernel,
        "out_project",
        outs,
        (mixer_local, *out_blocks, hidden, gain),
        flops=2 * rows * features * features,
    )


def ffn_parts(gate, up, grad):
    sigmoid = 1.0 / (1.0 + jnp.exp(-gate))
    scaled = gate * sigmoid
    gate_grad = grad * up * sigmoid * (1.0 + gate * (1.0 - sigmoid))
    return scaled * up, gate_grad, grad * scaled


def ffn_block(inputs, upstream, pair, down):
    rows, features = inputs[0].shape
    own = down.shape[0]
    even = own // 128 * 128
    width = own - even
    total = 2 * rows
    teams, size = pair.shape[1:3]

    def kernel(*refs):
        x0, x1, g0, g1, pair_in, down_in, act, grads, back0, back1, out0, out1 = refs[:12]
        xs, gs, pair, down, last, sems = refs[12:]
        first = [(x0, xs.at[:rows, :]), (x1, xs.at[rows:, :])]
        for u in range(4):
            for z in range(teams):
                to = (z * 4 + u) * size
                first.append((pair_in.at[u, z], pair.at[to : to + size, :]))
        second = [(g0, gs.at[:rows, :]), (g1, gs.at[rows:, :]), (down_in, down)]
        copies = fetch(first + second, sems)
        for copy in copies[: len(first)]:
            copy.wait()
        x = xs[...]
        gate = dot(x, pair[:, :even], ((1,), (0,)))
        up = dot(x, pair[:, even : 2 * even], ((1,), (0,)))
        for copy in copies[len(first) :]:
            copy.wait()
        g = gs[...]
        grad = dot(g, down[:even, :], ((1,), (1,)))
        value, gate_grad, up_grad = ffn_parts(gate, up, grad)
        act[:, :even] = value.astype(NARROW)
        grads[:, :even] = gate_grad.astype(NARROW)
        grads[:, even : 2 * even] = up_grad.astype(NARROW)
        if width == 64:
            last[:width, :] = down[even:, :]
            last[width:, :] = down[even:, :]
            both = dot(x, pair[:, 2 * even :], ((1,), (0,)))
            turned = pltpu.roll(both, width, 1)
            lower = lax.broadcasted_iota(jnp.int32, both.shape, 1) < width
            grad = dot(g, last[...], ((1,), (1,)))
            value, gate_grad, up_grad = ffn_parts(
                jnp.where(lower, both, turned), jnp.where(lower, turned, both), grad
            )
            act[:, even:] = value[:, :width].astype(NARROW)
            grads[:, 2 * even :] = jnp.where(lower, gate_grad, up_grad).astype(NARROW)
        else:
            gate = dot(x, pair[:, 2 * even : even + own], ((1,), (0,)))
            up = dot(x, pair[:, even + own :], ((1,), (0,)))
            grad = dot(g, down[even:, :], ((1,), (1,)))
            value, gate_grad, up_grad = ffn_parts(gate, up, grad)
            act[:, even:] = value.astype(NARROW)
            grads[:, 2 * even : even + own] = gate_grad.astype(NARROW)
            grads[:, even + own :] = up_grad.astype(NARROW)
        back = dot(grads[...], pair[...], ((1,), (1,)))
        back0[...] = back[:rows]
        back1[...] = back[rows:].astype(NARROW)
        out = dot(act[...], down[...], ((1,), (0,)))
        out0[...] = out[:rows]
        out1[...] = out[rows:].astype(NARROW)

    outs = (
        shape(NARROW, total, own),
        shape(NARROW, total, 2 * own),
        shape(WIDE, rows, features),
        shape(NARROW, rows, features),
        shape(WIDE, rows, features),
        shape(NARROW, rows, features),
    )
    return call(
        kernel,
        "ffn",
        outs,
        (*inputs, *upstream, pair, down),
        [
            pltpu.VMEM((total, features), NARROW),
            pltpu.VMEM((total, features), NARROW),
            pltpu.VMEM((features, 2 * own), NARROW),
            pltpu.VMEM((own, features), NARROW),
            pltpu.VMEM((2 * width, features), NARROW),
            pltpu.SemaphoreType.DMA((5 + 4 * teams,)),
        ],
        12 * total * features * own,
        in_place=True,
    )


def weight_grads(lefts, rights, groups, name):
    deep, wide = lefts[0].shape[1], rights[0].shape[1]
    tokens = sum(left.shape[0] for left in lefts)
    outer, inner, size = groups

    def kernel(*refs):
        ins, (out, left, right, sems) = refs[: len(lefts) + len(rights)], refs[-4:]
        pairs = []
        for blocks, whole in ((ins[: len(lefts)], left), (ins[len(lefts) :], right)):
            row = 0
            for block in blocks:
                pairs.append((block, whole.at[row : row + block.shape[0], :]))
                row += block.shape[0]
        for copy in fetch(pairs, sems):
            copy.wait()
        step = max(256 // (inner * size), 1) * inner * size
        step = step if step % 128 == 0 else deep
        step = 256 if size == deep else step
        for start in range(0, deep, step):
            stop = min(start + step, deep)
            total = dot(left[:, start:stop], right[...], ((0,), (0,))).astype(NARROW)
            if size == deep:
                out[start:stop, :] = total
                continue
            for row in range(start, stop, size):
                a, b = row // size // inner, row // size % inner
                to = (b * outer + a) * size
                out[to : to + size, :] = total[row - start : row - start + size]

    return call(
        kernel,
        name,
        shape(NARROW, deep, wide),
        (*lefts, *rights),
        [
            pltpu.VMEM((tokens, deep), NARROW),
            pltpu.VMEM((tokens, wide), NARROW),
            pltpu.SemaphoreType.DMA((len(lefts) + len(rights),)),
        ],
        2 * tokens * deep * wide,
        in_place=True,
    )


def resid_back(parts, resid, gain, upstream, out_blocks):
    rows, features = resid.shape
    channels = features // TEAM

    def kernel(own, across, along, resid, gain, upstream, *refs):
        out_blocks, (resid_grad, rounded, mixer_grad) = refs[:TEAM], refs[TEAM:]
        place, _ = where_am_i()
        grad = own[...] + across[...].astype(WIDE) + along[...].astype(WIDE)
        values = resid[...]
        scale = scale_of(values)
        grad = upstream[...].astype(WIDE) + norm_back(grad, values * scale, scale, gain[...])
        resid_grad[...] = grad
        rounded[...] = grad.astype(NARROW)
        for m in range(TEAM):
            product = dot(rounded[...], out_blocks[m][...], ((1,), (1,)))
            mixer_grad[place ^ m] = product.astype(NARROW)

    outs = (
        shape(WIDE, rows, features),
        shape(NARROW, rows, features),
        shape(NARROW, TEAM, rows, channels),
    )
    return call(
        kernel,
        "resid_back",
        outs,
        (*parts, resid, gain, upstream, *out_blocks),
        flops=2 * rows * features * features,
    )


def conv_back(mixer_grad, mixed, gated, conv, taps, keeps):
    tokens, channels = conv.shape

    def kernel(mixer_grad, mixed, gated, conv, taps, keeps, part, rim, taps_grad, ones, twos):
        grad = mixer_grad[...].astype(WIDE)
        conv_grad = grad * mixed[HALO:, channels : 2 * channels]
        one, two = keeps[8:, 0:1] * conv_grad, keeps[8:, 1:2] * conv_grad
        zeros = jnp.zeros((8, channels), WIDE)
        taps_grad[...] = zeros
        for k, (left, back) in enumerate(((two, 2), (one, 1), (conv_grad, 0))):
            product = left * gated[HALO - back : HALO - back + tokens, :]
            taps_grad[k : k + 1, :] = jnp.sum(product, axis=0, keepdims=True)
        ones[:tokens, :] = taps[1:2, :] * one
        twos[:tokens, :] = taps[0:1, :] * two
        ones[tokens:, :] = zeros
        twos[tokens:, :] = zeros
        rim[...] = zeros
        rim[6:7, :] = twos[0:1, :]
        rim[7:8, :] = twos[1:2, :] + ones[0:1, :]
        part[...] = taps[2:3, :] * conv_grad + ones[1 : tokens + 1, :] + twos[2 : tokens + 2, :]

    outs = (shape(WIDE, tokens, channels), shape(WIDE, 8, channels), shape(WIDE, 8, channels))
    scratch = [pltpu.VMEM((tokens + 8, channels), WIDE)] * 2
    return call(
        kernel, "conv_back", outs, (mixer_grad, mixed, gated, conv, taps, keeps), scratch
    )


def mixer_back(part, returned, mixer_grad, mixed, conv, normed, in_own, teams):
    tokens, channels = conv.shape
    features = in_own.shape[0]
    rows, share = tokens // TEAM, features // teams

    def kernel(*refs):
        part, returned, mixer_grad, mixed, conv, normed, in_own, grads, odd = refs[:9]
        shares, (side, whole, weight) = refs[9 : 9 + teams], refs[9 + teams :]
        place, team = where_am_i()
        whole[...] = part[...]
        whole[tokens - 8 :, :] = part[tokens - 8 :, :] + returned[...]
        gated_grad = whole[...]
        grads[:, :channels] = (gated_grad * mixed[HALO:, 2 * channels :]).astype(NARROW)
        grads[:, channels : 2 * channels] = (
            mixer_grad[...].astype(WIDE) * conv[...]
        ).astype(NARROW)
        grads[:, 2 * channels :] = (gated_grad * mixed[HALO:, :channels]).astype(NARROW)
        for chip in range(TEAM // 2):
            at_place = place ^ (2 * chip + 1)
            side[chip * rows : (chip + 1) * rows, :] = grads[at(at_place * rows, rows), :]
        step = features // 4
        for start in range(0, features, step):
            span = slice(start, start + step)
            weight[span, :] = dot(normed[HALO:, span], grads[...], ((0,), (0,)))
        for k in range(teams):
            owner = lax.rem(team + k, teams)
            shares[k][...] = weight[at(owner * share, share), :].astype(shares[k].dtype)
        odd[...] = dot(side[...], in_own[...], ((1,), (1,))).astype(NARROW)

    outs = (shape(NARROW, tokens, 3 * channels), shape(NARROW, tokens // 2, features))
    outs += tuple(
        shape(NARROW if k == teams - 1 else WIDE, share, 3 * channels) for k in range(teams)
    )
    grads, odd, *shares = call(
        kernel,
        "mixer_back",
        outs,
        (part, returned, mixer_grad, mixed, conv, normed, in_own),
        [
            pltpu.VMEM((tokens // 2, 3 * channels), NARROW),
            pltpu.VMEM((tokens, channels), WIDE),
            pltpu.VMEM((features, 3 * channels), WIDE),
        ],
        3 * tokens * features * 3 * channels,
    )
    return grads, odd, shares


def out_back(mixer_in, blocks, taps_grad, teams):
    rows, features = blocks[0].shape
    channels = mixer_in.shape[1]
    share = channels // teams
    low = (share + 15) // 16 * 16

    def kernel(*refs):
        mixer_in, blocks, taps_grad = refs[0], refs[1 : 1 + TEAM], refs[1 + TEAM]
        shares, (total,) = refs[2 + TEAM : 2 + TEAM + teams], refs[2 + TEAM + teams :]
        place, team = where_am_i()
        total[...] = sum(
            dot(mixer_in[at((place ^ m) * rows, rows), :], blocks[m][...], ((0,), (0,)))
            for m in range(TEAM)
        )
        for k in range(teams):
            owner = lax.rem(team + k, teams)
            kind = shares[k].dtype
            shares[k][...] = jnp.zeros_like(shares[k])
            shares[k][:share, :] = total[at(owner * share, share, 8), :].astype(kind)
            shares[k][low : low + 8, :channels] = taps_grad[...].astype(kind)

    outs = tuple(shape(NARROW if k else WIDE, low + 16, features) for k in range(teams))
    return call(
        kernel,
        "out_back",
        outs,
        (mixer_in, *blocks, taps_grad),
        [pltpu.VMEM((channels, features), WIDE)],
        2 * TEAM * rows * channels * features,
    ), low


def mixer_back_own(grads, in_own):
    tokens, width = grads.shape
    rows = tokens // TEAM

    def kernel(grads, in_own, even, side):
        place, _ = where_am_i()
        for chip in range(TEAM // 2):
            at_place = place ^ (2 * chip)
            side[chip * rows : (chip + 1) * rows, :] = grads[at(at_place * rows, rows), :]
        even[...] = dot(side[...], in_own[...], ((1,), (1,)))

    return call(
        kernel,
        "mixer_back_own",
        shape(WIDE, tokens // 2, in_own.shape[0]),
        (grads, in_own),
        [pltpu.VMEM((tokens // 2, width), NARROW)],
        tokens * in_own.size,
    )


def body(
    hidden_in,
    seq_start,
    mixer_gain,
    in_weight,
    conv_weight,
    out_weight,
    ffn_gain,
    gate_weight,
    up_weight,
    down_weight,
    cotangent,
):
    net = Net()
    teams = net.teams
    rows, features = hidden_in.shape
    inner = gate_weight.shape[2]
    part = features // net.count
    ffpart = inner // net.count
    channels = features // TEAM
    ffown = 4 * ffpart
    even = ffown // 128 * 128
    peers = net.peer_groups()

    down_own = lax.all_gather(down_weight[0], "dp", axis=0, tiled=True, axis_index_groups=peers)
    upstream, found, results = [], [], {}
    hidden_job = net.spawn(net.blocks(hidden_in))
    upstream_job = net.spawn(net.ring_blocks(cotangent, upstream))
    out_job = net.spawn(net.line_all(out_weight[0]))
    sent = in_prepare(
        in_weight[0],
        (mixer_gain, ffn_gain),
        seq_start.reshape(1, rows),
        conv_weight[0].T,
        teams,
    )
    net.need(sent)
    got_job = net.do(net.exchange, sent)
    pair_job = net.do(lambda *x: pair_prepare(*x, teams), gate_weight[0], up_weight[0])
    net.step()
    upstream_job.held = True
    pair_job = net.do(net.line_exchange, pair_job.result)
    in_job = net.spawn(net.line_blocks(got_job.result))
    net.until(pair_job)
    pair = pair_job.result.reshape(2 * teams * part, 2 * ffown)
    pair_own = lax.all_gather(pair, "dp", axis=0, tiled=True, axis_index_groups=peers)
    pair_own = pair_own.reshape(4, teams, 2 * part, 2 * ffown)
    out_own = jnp.zeros((channels, features), NARROW)
    for k, block in enumerate(out_job.result):
        out_own = lax.dynamic_update_slice(out_own, block, ((net.team - k) % teams * part, 0))
    net.until(hidden_job)

    def last_rows():
        last = hidden_job.result[0][-HALO:]
        for m in range(1, TEAM):
            block = hidden_job.result[m][-HALO:]
            last = jnp.where(net.place == (TEAM - 1) ^ m, block, last)
        (before,) = yield [(last, ("ring", 1))]
        return before

    halo_job = net.spawn(last_rows())
    out_job = net.spawn(net.blocks(out_own))
    before, weights = net.until(halo_job, in_job)

    upstream_job.held = False
    mix_job = net.do(lambda *x: mixer_forward(x[:TEAM], x[TEAM], x[TEAM + 1 :]),
                     *hidden_job.result, before, *weights)
    (normed, mixed, gated, conv, mixer_in, in_own, gain_one, gain_two, taps, keeps) = net.until(
        mix_job
    )
    mixer_local = net.until(net.do(net.exchange, mixer_in.reshape(TEAM, rows, channels)))
    out_blocks = net.until(out_job)
    resid, ffn_in = out_project(mixer_local, out_blocks, hidden_in, gain_two)

    def compute(k, inputs):
        operands = (*inputs, *upstream[k], pair_own, down_own)
        return (lambda *x: ffn_block(x[:2], x[2:4], *x[4:])), operands

    ffn_job = net.spawn(net.ring_through(ffn_in, found, results, compute))
    net.step(teams + 2)
    order = list(range(teams))
    acts, grads = [[results[k][i] for k in order] for i in (0, 1)]
    inputs, cots = [[block for k in order for block in b[k]] for b in (found, upstream)]

    def pair_grads(*blocks):
        count = 2 * teams
        return weight_grads(blocks[:count], blocks[count:], (teams, 4, 2 * part), "pair_grads")

    def down_grads(*blocks):
        return weight_grads(blocks[:teams], blocks[teams:], (1, 1, ffown), "down_grads")

    pair_job = net.do(pair_grads, *inputs, *grads)
    output_job = net.spawn(net.ring_sum(result_of(results, 4), result_of(results, 5)))
    ffn_grad = net.until(ffn_job)
    pair_sum = lax.psum_scatter(
        pair_job.result, "dp", scatter_dimension=0, tiled=True, axis_index_groups=peers
    )

    output_job.held = True
    back_job = net.do(
        lambda *x: resid_back(x[:3], *x[3:6], x[6:]),
        *ffn_grad, resid, gain_two, cotangent, *out_blocks,
    )
    resid_grad, rounded, mixer_grad = net.until(back_job)
    output_job.held = False
    down_job = net.do(down_grads, *acts, *cots)
    mixer_grad = net.until(net.do(net.exchange, mixer_grad)).reshape(TEAM * rows, channels)
    output_job.held = True
    down_sum = lax.psum_scatter(
        down_job.result, "dp", scatter_dimension=0, tiled=True, axis_index_groups=peers
    )
    gated_part, rim, taps_grad = net.until(
        net.do(conv_back, mixer_grad, mixed, gated, conv, taps, keeps)
    )

    def rim_steps():
        (returned,) = yield [(rim, ("back",))]
        return returned

    rounded_job = net.spawn(net.blocks(rounded))
    returned = net.until(net.spawn(rim_steps()))
    output_job.held = False
    mixed_grad, normed_odd, shares = net.until(
        net.do(
            lambda *x: mixer_back(*x, teams),
            gated_part, returned, mixer_grad, mixed, conv, normed, in_own,
        )
    )
    output_job.held = True
    in_job = net.spawn(net.line_sum(shares))
    normed_job = net.spawn(
        net.team_sum((mixer_back_own, (mixed_grad, in_own)), normed_odd)
    )
    net.until(rounded_job)
    low = (part + 15) // 16 * 16
    out_job = net.do(
        lambda *x: out_back(x[0], x[1 : 1 + TEAM], x[1 + TEAM], teams)[0],
        mixer_in, *rounded_job.result, taps_grad,
    )
    in_grad = net.until(in_job).astype(NARROW)
    in_job = net.do(net.exchange, in_grad.reshape(TEAM, part, 3 * channels))
    output_job.held = False
    in_grad = net.until(in_job)
    out_shares = net.until(out_job)
    out_job = net.spawn(net.line_send(out_shares[1:]))
    pair_job = net.do(net.line_exchange, pair_sum.reshape(teams * 2, part, 2 * ffown))
    in_job = net.do(
        lambda *x: in_finish(*x, teams), in_grad, in_weight[0], mixer_gain.reshape(part, 1)
    )
    normed_grad, ffn_out, arrived = net.until(normed_job, output_job, out_job)
    in_grad, grad_mixer_gain = net.until(in_job)
    grad_gate, grad_up, grad_ffn_gain = pair_finish(
        net.until(pair_job), gate_weight[0], up_weight[0], ffn_gain.reshape(part, 1), teams
    )
    out_pack = sum([part.astype(WIDE) for part in arrived], out_shares[0])

    def total(parts):
        return parts[0] + parts[1].astype(WIDE) + parts[2].astype(WIDE)

    own_hidden = hidden_in.astype(WIDE)
    scale_one = scale_of(own_hidden)
    grad_hidden = resid_grad + norm_back(
        total(normed_grad), own_hidden * scale_one, scale_one, gain_one
    )
    hidden_out = (resid + total(ffn_out)).astype(NARROW)
    grad_out = out_pack[:part]
    grad_conv = lax.dynamic_slice(out_pack, (low, net.team * part), (3, part)).T
    return (
        hidden_out,
        grad_hidden,
        grad_mixer_gain.reshape(1, part),
        in_grad[None],
        grad_conv[None],
        grad_out[None],
        grad_ffn_gain.reshape(1, part),
        grad_gate[None],
        grad_up[None],
        down_sum.astype(WIDE)[None],
    )


def solution(mesh):
    tokens, wide, deep = P("dp", None), P(None, "dp"), P(None, "dp", None)
    return jax.shard_map(
        body,
        mesh=mesh,
        in_specs=(tokens, P("dp"), wide, deep, deep, deep, wide, deep, deep, deep, tokens),
        out_specs=(tokens, tokens, wide, deep, deep, deep, wide, deep, deep, deep),
        check_vma=False,
    )
```

```python
import jax
import jax.numpy as jnp
from jax import lax
from jax.experimental import pallas as pl
from jax.experimental.pallas import tpu as pltpu
from jax.sharding import PartitionSpec as P

epsilon = 1e-05
TEAM = 8
HALO = 16
WIDE = jnp.float32
NARROW = jnp.bfloat16


def dot(left, right, contract):
    return lax.dot_general(left, right, (contract, ((), ())), preferred_element_type=WIDE)


def fetch(pairs, sems):
    copies = [pltpu.make_async_copy(a, b, sems.at[i]) for i, (a, b) in enumerate(pairs)]
    for copy in copies:
        copy.start()
    return copies


def shape(kind, *sizes):
    return jax.ShapeDtypeStruct(sizes, kind)


def call(kernel, name, out_shape, operands, scratch=(), flops=0, in_place=False):
    places = {}
    if in_place:
        spec = pl.BlockSpec(memory_space=pl.ANY)
        places["in_specs"] = [spec] * len(operands) if in_place is True else in_place
    size = sum(x.size * x.dtype.itemsize for x in operands)
    return pl.pallas_call(
        kernel,
        out_shape=out_shape,
        scratch_shapes=list(scratch),
        compiler_params=pltpu.CompilerParams(vmem_limit_bytes=60 * 2**20),
        cost_estimate=pl.CostEstimate(flops=flops, bytes_accessed=size, transcendentals=0),
        name=name,
        **places,
    )(*operands)


class Job:
    def __init__(self, steps):
        self.steps = steps
        self.result = None
        self.open = True
        self.request = None
        self.held = False
        self.send(None)

    def send(self, value):
        try:
            self.request = self.steps.send(value)
        except StopIteration as stop:
            self.result, self.open, self.request = stop.value, False, None


class Net:
    def __init__(self):
        self.count = lax.axis_size("dp")
        self.teams = self.count // TEAM
        self.index = lax.axis_index("dp")
        self.place = self.index % TEAM
        self.team = self.index // TEAM
        self.core = self.index % 2
        self.peer = (self.index // 2) % 4
        self.jobs = []
        self.waiting = []
        self.gate = []
        self.extra = []

    def pairs(self, move):
        if move[0] == "swap":
            return [(i, i ^ move[1]) for i in range(self.count)]
        if move[0] == "ring":
            return [(i, (i + move[1] * TEAM) % self.count) for i in range(self.count)]
        if move[0] == "mixed":
            return [(i, i ^ (2 if i % 2 == 0 else 4)) for i in range(self.count)]
        return [(i, i - TEAM) for i in range(TEAM, self.count)]

    def do(self, call, *operands):
        def steps():
            (got,) = yield [(operands, ("call", call))]
            return got

        return self.spawn(steps())

    def spawn(self, steps):
        job = Job(steps)
        if job.open:
            self.jobs.append(job)
        return job

    def need(self, *values):
        self.extra.extend(values)

    def later(self, value):
        return lax.optimization_barrier((value, self.gate))[0]

    def step(self, times=1):
        for _ in range(times):
            self.one_step()

    def one_step(self):
        ready = [job for job in self.jobs if job.request is not None and not job.held]
        values = [move[0] for job in ready for move in job.request]
        self.raw = []
        if values or self.waiting:
            values, _ = lax.optimization_barrier((values, (self.gate, self.extra)))
            self.extra = []
            at = 0
            for job in ready:
                span = 1
                got = []
                moves = job.request
                for move in moves:
                    if len(move) > 2:
                        span = move[2]
                    if move[1][0] == "call":
                        got.append(move[1][1](*values[at]))
                    else:
                        got.append(lax.ppermute(values[at], "dp", self.pairs(move[1])))
                    at += 1
                job.request = None
                self.raw.extend(zip([move[1] for move in moves], got))
                self.waiting.append([span, job, got])
        for entry in self.waiting:
            entry[0] -= 1
        done = [entry for entry in self.waiting if entry[0] <= 0]
        self.waiting = [entry for entry in self.waiting if entry[0] > 0]
        results = lax.optimization_barrier([entry[2] for entry in done])
        self.gate = results
        for (_, job, _), got in zip(done, results):
            job.send(got)
        self.jobs = [job for job in self.jobs if job.open]

    def until(self, *jobs):
        while any(job.open for job in jobs):
            self.one_step()
        return [job.result for job in jobs] if len(jobs) > 1 else jobs[0].result


    def blocks(self, value):
        across, along, twin = yield [
            (value, ("swap", 2)),
            (value, ("swap", 4)),
            (value, ("swap", 1)),
        ]
        corner, across_twin, along_twin = yield [
            (jnp.where(self.core == 0, along, across), ("mixed",)),
            (across, ("swap", 1)),
            (along, ("swap", 1)),
        ]
        (corner_twin,) = yield [(corner, ("swap", 1))]
        return [value, twin, across, across_twin, along, along_twin, corner, corner_twin]

    def blocks_direct(self, value):
        found = yield [(value, ("swap", mask)) for mask in (2, 4, 6, 1)]
        twins = yield [(block, ("swap", 1)) for block in found[:3]]
        return [value, found[3], found[0], twins[0], found[1], twins[1], found[2], twins[2]]

    def team_sum(self, odd, fold, span=1):
        (arrived,) = yield [(odd, ("swap", 1))]
        call, operands = fold(arrived)
        (parts,) = yield [(operands, ("call", call))]
        moved = yield [(part, ("swap", mask), span) for part, mask in zip(parts[1:], (6, 2, 4))]
        return [parts[0]] + moved

    def exchange(self, blocks):
        groups = [[base + q for q in range(TEAM)] for base in range(0, self.count, TEAM)]
        return lax.all_to_all(blocks, "dp", 0, 0, axis_index_groups=groups, tiled=True)

    def line_both(self, value):
        teams = self.teams
        found, up, down = {0: value}, value, value
        for step in range(1, teams // 2 + 1):
            moves = [(up, ("ring", 1))]
            if step < teams - step:
                moves.append((down, ("ring", teams - 1)))
            got = yield moves
            found[step], up = got[0], got[0]
            if len(got) > 1:
                found[teams - step], down = got[1], got[1]
        return jnp.concatenate([found[k] for k in range(teams)], 0)

    def line_send(self, parts, span=1):
        return (yield [(part, ("ring", k + 1), span) for k, part in enumerate(parts)])

    def line_sum(self, shares):
        total = shares[-1].astype(NARROW)
        for share in reversed(shares[:-1]):
            (got,) = yield [(total, ("ring", 1))]
            total = share + got.astype(WIDE)
            total = total if share is shares[0] else total.astype(NARROW)
        return total


def scale_of(values):
    return lax.rsqrt(jnp.mean(values * values, axis=1, keepdims=True) + epsilon)


def norm_back(upstream, normed, scaler, gain):
    scaled = upstream * gain
    return scaler * (scaled - normed * jnp.mean(scaled * normed, axis=1, keepdims=True))


def where_am_i():
    index = lax.axis_index("dp")
    return index % TEAM, index // TEAM


def at(start, size, step=16):
    return pl.ds(pl.multiple_of(start, step), size)


def summed_parts(left, right, arrived, turned, name, relative=False):
    rows, width = arrived.shape[0] // 4, arrived.shape[1]
    deep = left.shape[1]
    contract = ((1,), (1,)) if turned else ((1,), (0,))

    def kernel(left_in, right_in, arrived_in, own, corner, across, along, left, right, arrived, sems):
        place, _ = where_am_i()
        copies = [(right_in, right), (arrived_in, arrived)]
        for k in range(4):
            source = left_in
            if relative:
                source = left_in.at[at((place ^ (2 * k)) * rows, rows), :]
            else:
                source = left_in.at[k * rows : (k + 1) * rows, :]
            copies.append((source, left.at[k * rows : (k + 1) * rows, :]))
        for copy in fetch(copies, sems):
            copy.wait()
        total = dot(left[...], right[...], contract) + arrived[...].astype(WIDE)
        for k, out in ((3, corner), (1, across), (2, along), (0, own)):
            out[...] = total[k * rows : (k + 1) * rows].astype(out.dtype)

    outs = (shape(WIDE, rows, width),) + (shape(NARROW, rows, width),) * 3
    return call(
        kernel,
        name,
        outs,
        (left, right, arrived),
        [
            pltpu.VMEM((4 * rows, deep), NARROW),
            pltpu.VMEM(right.shape, NARROW),
            pltpu.VMEM(arrived.shape, NARROW),
            pltpu.SemaphoreType.DMA((6,)),
        ],
        8 * rows * deep * width,
        in_place=True,
    )


def pieces(ffpart, even, own):
    runs = []
    for z in range(own // ffpart):
        for start, stop in ((0, even), (even, own)):
            low, high = max(z * ffpart, start), min((z + 1) * ffpart, stop)
            if low < high:
                at_gate = low if start == 0 else 2 * even + low - even
                at_up = even + low if start == 0 else own + low
                runs.append((z, low, high, at_gate, at_up))
    return runs


def in_prepare(weight, gains, marks, taps, teams):
    part, width = weight.shape
    features = width // 3
    channels = features // TEAM
    slots = max(128, TEAM * part) // part

    def kernel(weight, gain_one, gain_two, marks, taps, out, wide, small):
        index = lax.axis_index("dp")
        whole = weight[...].astype(WIDE)
        small[...] = jnp.zeros_like(small)
        for slot in range(slots):
            mine = lax.rem(index, slots) == slot
            for row, gain in enumerate((gain_one, gain_two)):
                value = gain[...].astype(WIDE)
                value = jnp.where(mine, value, jnp.zeros_like(value))
                small[row : row + 1, slot * part : (slot + 1) * part] = value
        small[0:1, 2 * channels :] = marks[...].astype(WIDE)
        for slot in range(teams):
            value = taps[...].astype(WIDE)
            value = jnp.where(index // TEAM == slot, value, jnp.zeros_like(value))
            for k in range(3):
                to = k * channels + slot * part
                small[2:3, to : to + part] = value[k : k + 1, :]
        for p in range(TEAM):
            for k in range(3):
                for z in range(teams):
                    source = k * features + (z * TEAM + p) * part
                    to = k * channels + z * part
                    wide[:, to : to + part] = whole[:, source : source + part]
            out[p, :part, :] = wide[...].astype(NARROW)
            out[p, part:, :] = small[...].astype(NARROW)

    return call(
        kernel,
        "in_prepare",
        shape(NARROW, TEAM, part + 8, 3 * channels),
        (weight, *gains, marks, taps),
        [pltpu.VMEM((part, 3 * channels), WIDE), pltpu.VMEM((8, 3 * channels), WIDE)],
    )


def in_finish(blocks, weight, gain, teams):
    part, width = weight.shape
    features = width // 3
    channels = features // TEAM

    def kernel(blocks, weight, gain, out, gain_grad):
        for p in range(TEAM):
            block = blocks[p].astype(WIDE)
            for k in range(3):
                for z in range(teams):
                    to = k * features + (z * TEAM + p) * part
                    source = k * channels + z * part
                    out[:, to : to + part] = block[:, source : source + part]
        product = jnp.sum(weight[...].astype(WIDE) * out[...], axis=1, keepdims=True)
        gain_grad[...] = product / gain[...].astype(WIDE)

    outs = (shape(WIDE, part, width), shape(WIDE, part, 1))
    return call(kernel, "in_finish", outs, (blocks, weight, gain))


def pair_prepare(gate, up, teams):
    part, inner = gate.shape
    own = inner // TEAM
    ffpart = own // teams
    even = own // 128 * 128
    runs = pieces(ffpart, even, own)

    def kernel(gate, up, out, wide):
        gates, ups = gate[...].astype(WIDE), up[...].astype(WIDE)
        for p in range(TEAM):
            for z, low, high, at_gate, at_up in runs:
                source = (z * TEAM + p) * ffpart + low - z * ffpart
                size = high - low
                wide[:, at_gate : at_gate + size] = gates[:, source : source + size]
                wide[:, at_up : at_up + size] = ups[:, source : source + size]
            out[p] = wide[...].astype(NARROW)

    out = shape(NARROW, TEAM, part, 2 * own)
    scratch = [pltpu.VMEM((part, 2 * own), WIDE)]
    return call(kernel, "pair_prepare", out, (gate, up), scratch)


def pair_finish(blocks, gate, up, gain, teams):
    part, inner = gate.shape
    own = inner // TEAM
    ffpart = own // teams
    even = own // 128 * 128
    runs = pieces(ffpart, even, own)

    def kernel(blocks, gate, up, gain, gate_grad, up_grad, gain_grad):
        for p in range(TEAM):
            block = blocks[p].astype(WIDE)
            for z, low, high, at_gate, at_up in runs:
                to = (z * TEAM + p) * ffpart + low - z * ffpart
                size = high - low
                gate_grad[:, to : to + size] = block[:, at_gate : at_gate + size]
                up_grad[:, to : to + size] = block[:, at_up : at_up + size]
        product = gate[...].astype(WIDE) * gate_grad[...] + up[...].astype(WIDE) * up_grad[...]
        gain_grad[...] = jnp.sum(product, axis=1, keepdims=True) / gain[...].astype(WIDE)

    outs = (shape(WIDE, part, inner), shape(WIDE, part, inner), shape(WIDE, part, 1))
    return call(kernel, "pair_finish", outs, (blocks, gate, up, gain))


def mixer_forward(blocks, before, weights):
    rows, features = blocks[0].shape
    tokens = TEAM * rows
    count, _, channels = weights.shape
    channels = channels // 3
    teams = count // TEAM
    share, part = features // teams, features // count

    def kernel(*refs):
        blocks, (before, weights), refs = refs[:TEAM], refs[TEAM : TEAM + 2], refs[TEAM + 2 :]
        normed, mixed, gated, conv, mixer_in, in_own, gain, gain_two, taps, keeps = refs[:10]
        hs, small, sems = refs[10:]
        place, team = where_am_i()
        copies = [(weights.at[:, part:, :], small)]
        for d in range(count):
            to = in_own.at[d * part : (d + 1) * part, :]
            copies.append((weights.at[d, :part, :], to))
        for m in range(TEAM):
            copies.append((blocks[m], hs.at[at(HALO + (place ^ m) * rows, rows), :]))
        copies.append((before, hs.at[:HALO, :]))
        for copy in fetch(copies, sems):
            copy.wait()
        first = hs[:HALO, :]
        hs[:HALO, :] = jnp.where(team > 0, first, jnp.zeros_like(first))
        total = jnp.zeros((1, 3 * channels), WIDE)
        gain[...] = jnp.zeros_like(gain)
        gain_two[...] = jnp.zeros_like(gain_two)
        span = max(share, 128)
        for z in range(teams):
            both = sum(small[z * TEAM + p].astype(WIDE) for p in range(TEAM))
            one, two = both[0:1], both[1:2]
            total = total + small[z * TEAM + place].astype(WIDE)[2:3]
            to = slice(z * share // span * span, z * share // span * span + span)
            gain[:, to] = gain[:, to] + one[:, :span]
            gain_two[:, to] = gain_two[:, to] + two[:, :span]
        taps[...] = jnp.zeros_like(taps)
        for k in range(3):
            taps[k : k + 1, :] = total[:, k * channels : (k + 1) * channels]
        marks = [
            1.0 - small[team * TEAM + p].astype(WIDE)[0:1, 2 * channels :] for p in range(TEAM)
        ]
        keep = jnp.concatenate([mark.reshape(rows, 1) for mark in marks], 0)
        keeps[8:, 0:1] = keep
        before_team = lax.rem(team + teams - 1, teams) * TEAM + TEAM - 1
        last = 1.0 - small[before_team].astype(WIDE)[0:1, 3 * channels - 1 :]
        keeps[7:8, 0:1] = last
        keeps[8:, 1:2] = keep * keeps[7 : 7 + tokens, 0:1]
        scale = gain[...]

        def norm(start, size):
            values = hs[at(start, size), :].astype(WIDE)
            values = values * scale_of(values) * scale
            normed[at(start, size), :] = values.astype(NARROW)

        norm(0, HALO)

        @pl.loop(0, TEAM)
        def _(step):
            norm(HALO + step * rows, rows)

        mixed[...] = dot(normed[...], in_own[...], ((1,), (0,)))
        gated[...] = (mixed[:, :channels] * mixed[:, 2 * channels :]).astype(NARROW).astype(WIDE)
        conv_out = (
            taps[2:3, :] * gated[HALO:, :]
            + taps[1:2, :] * (keeps[8:, 0:1] * gated[HALO - 1 : HALO - 1 + tokens, :])
            + taps[0:1, :] * (keeps[8:, 1:2] * gated[HALO - 2 : HALO - 2 + tokens, :])
        )
        conv[...] = conv_out
        mixer_in[...] = (mixed[HALO:, channels : 2 * channels] * conv_out).astype(NARROW)

    outs = (
        shape(NARROW, HALO + tokens, features),
        shape(WIDE, HALO + tokens, 3 * channels),
        shape(WIDE, HALO + tokens, channels),
        shape(WIDE, tokens, channels),
        shape(NARROW, tokens, channels),
        shape(NARROW, features, 3 * channels),
        shape(WIDE, 1, features),
        shape(WIDE, 1, features),
        shape(WIDE, 8, channels),
        shape(WIDE, 8 + tokens, 2),
    )
    return call(
        kernel,
        "mixer_forward",
        outs,
        (*blocks, before, weights),
        [
            pltpu.VMEM((HALO + tokens, features), NARROW),
            pltpu.VMEM((count, 8, 3 * channels), NARROW),
            pltpu.SemaphoreType.DMA((count + TEAM + 2,)),
        ],
        2 * tokens * features * 3 * channels,
        in_place=True,
    )


def out_rows(blocks, whole, teams):
    place, team = where_am_i()
    channels = blocks[0].shape[0]
    share = channels // teams
    copies = []
    for m, block in enumerate(blocks):
        for k in range(teams):
            to = (place ^ m) * channels + lax.rem(team - k + teams, teams) * share
            copies.append((block.at[k * share : (k + 1) * share, :], whole.at[at(to, share, 8), :]))
    return copies


def out_project(mixer_blocks, out_blocks, hidden_blocks, gain, teams):
    rows, features = hidden_blocks[0].shape
    tokens, channels = mixer_blocks[0].shape

    def kernel(*refs):
        mixer_in, out_in, hidden_in = [refs[k * TEAM : (k + 1) * TEAM] for k in range(3)]
        gain, resid, odd, even, mixer, turned, out, hidden, sems = refs[3 * TEAM :]
        place, _ = where_am_i()
        copies = out_rows(out_in, out, teams)
        for m in range(TEAM):
            to = mixer.at[:, at((place ^ m) * channels, channels, 128)]
            copies.append((mixer_in[m], to))
            copies.append((hidden_in[m], hidden.at[m]))
        for copy in fetch(copies, sems):
            copy.wait()
        for half, side in ((1, odd), (0, even)):
            for k in range(TEAM // 2):
                source = mixer[at((place ^ (2 * k + half)) * rows, rows), :]
                turned[k * rows : (k + 1) * rows, :] = source
            product = dot(turned[...], out[...], ((1,), (0,)))
            for k in range(TEAM // 2):
                span = slice(k * rows, (k + 1) * rows)
                total = hidden[2 * k + half].astype(WIDE) + product[span]
                side[span, :] = (total * scale_of(total) * gain[...]).astype(NARROW)
                if k + half == 0:
                    resid[...] = total

    outs = (shape(WIDE, rows, features),) + (shape(NARROW, tokens // 2, features),) * 2
    any_place, in_vmem = pl.BlockSpec(memory_space=pl.ANY), pl.BlockSpec(memory_space=pltpu.VMEM)
    return call(
        kernel,
        "out_project",
        outs,
        (*mixer_blocks, *out_blocks, *hidden_blocks, gain),
        [
            pltpu.VMEM((tokens, features), NARROW),
            pltpu.VMEM((tokens // 2, features), NARROW),
            pltpu.VMEM((features, features), NARROW),
            pltpu.VMEM((TEAM, rows, features), NARROW),
            pltpu.SemaphoreType.DMA((TEAM * teams + 2 * TEAM,)),
        ],
        2 * tokens * features * features,
        in_place=[any_place] * (3 * TEAM) + [in_vmem],
    )


def ffn_parts(gate, up, grad):
    sigmoid = 1.0 / (1.0 + jnp.exp(-gate))
    scaled = gate * sigmoid
    gate_grad = grad * up * sigmoid * (1.0 + gate * (1.0 - sigmoid))
    return scaled * up, gate_grad, grad * scaled


def ffn_block(inputs, upstream, pair, down, send):
    count = len(upstream)
    rows, features = upstream[0].shape
    own = down.shape[0]
    even = own // 128 * 128
    width = own - even
    total = count * rows

    def kernel(*refs):
        x_in, g_in, refs = refs[0], refs[1 : 1 + count], refs[1 + count :]
        pair_in, down_in, act, grads = refs[:4]
        xs, gs, pair, down, last, sems = refs[-6:]
        first = [(x_in, xs), (pair_in, pair)]
        second = [(g_in[k], gs.at[k * rows : (k + 1) * rows, :]) for k in range(count)]
        second.append((down_in, down))
        copies = fetch(first + second, sems)
        for copy in copies[:2]:
            copy.wait()
        x = xs[...]
        gate = dot(x, pair[:, :even], ((1,), (0,)))
        up = dot(x, pair[:, even : 2 * even], ((1,), (0,)))
        for copy in copies[2:]:
            copy.wait()
        g = gs[...]
        grad = dot(g, down[:even, :], ((1,), (1,)))
        value, gate_grad, up_grad = ffn_parts(gate, up, grad)
        act[:, :even] = value.astype(NARROW)
        grads[:, :even] = gate_grad.astype(NARROW)
        grads[:, even : 2 * even] = up_grad.astype(NARROW)
        last[:width, :] = down[even:, :]
        last[width:, :] = down[even:, :]
        both = dot(x, pair[:, 2 * even :], ((1,), (0,)))
        turned = pltpu.roll(both, width, 1)
        lower = lax.broadcasted_iota(jnp.int32, both.shape, 1) < width
        grad = dot(g, last[...], ((1,), (1,)))
        value, gate_grad, up_grad = ffn_parts(
            jnp.where(lower, both, turned), jnp.where(lower, turned, both), grad
        )
        act[:, even:] = value[:, :width].astype(NARROW)
        grads[:, 2 * even :] = jnp.where(lower, gate_grad, up_grad).astype(NARROW)
        if send:
            refs[4][...] = dot(grads[...], pair[...], ((1,), (1,))).astype(NARROW)

    outs = (shape(NARROW, total, own), shape(NARROW, total, 2 * own))
    if send:
        outs += (shape(NARROW, total, features),)
    return call(
        kernel,
        "ffn",
        outs,
        (inputs, *upstream, pair, down),
        [
            pltpu.VMEM((total, features), NARROW),
            pltpu.VMEM((total, features), NARROW),
            pltpu.VMEM((features, 2 * own), NARROW),
            pltpu.VMEM((own, features), NARROW),
            pltpu.VMEM((2 * width, features), NARROW),
            pltpu.SemaphoreType.DMA((count + 3,)),
        ],
        10 * total * features * own,
        in_place=True,
    )


def ffn_output(act, down):
    def kernel(act, down, out):
        out[...] = dot(act[...], down[...], ((1,), (0,))).astype(NARROW)

    rows, features = act.shape[0], down.shape[1]
    out = shape(NARROW, rows, features)
    return call(kernel, "ffn_output", out, (act, down), flops=2 * rows * features * down.shape[0])


def weight_grads(lefts, rights, name):
    deep, wide = lefts[0].shape[1], rights[0].shape[1]
    tokens = sum(left.shape[0] for left in lefts)

    def kernel(*refs):
        ins, (out, left, right, sems) = refs[: len(lefts) + len(rights)], refs[-4:]
        pairs = []
        for blocks, whole in ((ins[: len(lefts)], left), (ins[len(lefts) :], right)):
            row = 0
            for block in blocks:
                pairs.append((block, whole.at[row : row + block.shape[0], :]))
                row += block.shape[0]
        for copy in fetch(pairs, sems):
            copy.wait()
        for start in range(0, deep, 256):
            stop = min(start + 256, deep)
            total = dot(left[:, start:stop], right[...], ((0,), (0,)))
            out[start:stop, :] = total.astype(NARROW)

    return call(
        kernel,
        name,
        shape(NARROW, deep, wide),
        (*lefts, *rights),
        [
            pltpu.VMEM((tokens, deep), NARROW),
            pltpu.VMEM((tokens, wide), NARROW),
            pltpu.SemaphoreType.DMA((len(lefts) + len(rights),)),
        ],
        2 * tokens * deep * wide,
        in_place=True,
    )


def resid_back(parts, resid, gain, upstream, out_blocks, teams):
    rows, features = resid.shape
    channels = features // TEAM

    def kernel(own, corner, across, along, resid, gain, upstream, *refs):
        out_in, (resid_grad, rounded, mixer_grad, out, sems) = refs[:TEAM], refs[TEAM:]
        copies = fetch(out_rows(out_in, out, teams), sems)
        grad = own[...] + sum(part[...].astype(WIDE) for part in (corner, across, along))
        values = resid[...]
        scale = scale_of(values)
        grad = upstream[...].astype(WIDE) + norm_back(grad, values * scale, scale, gain[...])
        resid_grad[...] = grad
        rounded[...] = grad.astype(NARROW)
        for copy in copies:
            copy.wait()
        product = dot(rounded[...], out[...], ((1,), (1,))).astype(NARROW)
        for p in range(TEAM):
            mixer_grad[p] = product[:, p * channels : (p + 1) * channels]

    outs = (
        shape(WIDE, rows, features),
        shape(NARROW, rows, features),
        shape(NARROW, TEAM, rows, channels),
    )
    any_place, in_vmem = pl.BlockSpec(memory_space=pl.ANY), pl.BlockSpec(memory_space=pltpu.VMEM)
    return call(
        kernel,
        "resid_back",
        outs,
        (*parts, resid, gain, upstream, *out_blocks),
        [
            pltpu.VMEM((features, features), NARROW),
            pltpu.SemaphoreType.DMA((TEAM * teams,)),
        ],
        2 * rows * features * features,
        in_place=[in_vmem] * 7 + [any_place] * TEAM,
    )


def conv_back(mixer_grad, mixed, gated, conv, taps, keeps):
    tokens, channels = conv.shape

    def kernel(mixer_grad, mixed, gated, conv, taps, keeps, part, rim, taps_grad, ones, twos):
        grad = mixer_grad[...].astype(WIDE)
        conv_grad = grad * mixed[HALO:, channels : 2 * channels]
        one, two = keeps[8:, 0:1] * conv_grad, keeps[8:, 1:2] * conv_grad
        zeros = jnp.zeros((8, channels), WIDE)
        taps_grad[...] = zeros
        for k, (left, back) in enumerate(((two, 2), (one, 1), (conv_grad, 0))):
            product = left * gated[HALO - back : HALO - back + tokens, :]
            taps_grad[k : k + 1, :] = jnp.sum(product, axis=0, keepdims=True)
        ones[:tokens, :] = taps[1:2, :] * one
        twos[:tokens, :] = taps[0:1, :] * two
        ones[tokens:, :] = zeros
        twos[tokens:, :] = zeros
        rim[...] = zeros
        rim[6:7, :] = twos[0:1, :]
        rim[7:8, :] = twos[1:2, :] + ones[0:1, :]
        part[...] = taps[2:3, :] * conv_grad + ones[1 : tokens + 1, :] + twos[2 : tokens + 2, :]

    outs = (shape(WIDE, tokens, channels), shape(WIDE, 8, channels), shape(WIDE, 8, channels))
    scratch = [pltpu.VMEM((tokens + 8, channels), WIDE)] * 2
    return call(
        kernel, "conv_back", outs, (mixer_grad, mixed, gated, conv, taps, keeps), scratch
    )


def mixer_back(part, returned, mixer_grad, mixed, conv, normed, in_own, teams):
    tokens, channels = conv.shape
    features = in_own.shape[0]
    rows, share = tokens // TEAM, features // teams

    def kernel(*refs):
        part, returned, mixer_grad, mixed, conv, normed, in_own, grads, odd = refs[:9]
        shares, (side, whole, weight) = refs[9 : 9 + teams], refs[9 + teams :]
        place, team = where_am_i()
        whole[...] = part[...]
        whole[tokens - 8 :, :] = part[tokens - 8 :, :] + returned[...]
        gated_grad = whole[...]
        grads[:, :channels] = (gated_grad * mixed[HALO:, 2 * channels :]).astype(NARROW)
        grads[:, channels : 2 * channels] = (
            mixer_grad[...].astype(WIDE) * conv[...]
        ).astype(NARROW)
        grads[:, 2 * channels :] = (gated_grad * mixed[HALO:, :channels]).astype(NARROW)
        for chip in range(TEAM // 2):
            at_place = place ^ (2 * chip + 1)
            side[chip * rows : (chip + 1) * rows, :] = grads[at(at_place * rows, rows), :]
        step = features // 4
        for start in range(0, features, step):
            span = slice(start, start + step)
            weight[span, :] = dot(normed[HALO:, span], grads[...], ((0,), (0,)))
        for k in range(teams):
            owner = lax.rem(team + k, teams)
            shares[k][...] = weight[at(owner * share, share), :].astype(shares[k].dtype)
        odd[...] = dot(side[...], in_own[...], ((1,), (1,))).astype(NARROW)

    outs = (shape(NARROW, tokens, 3 * channels), shape(NARROW, tokens // 2, features))
    outs += tuple(
        shape(NARROW if k == teams - 1 else WIDE, share, 3 * channels) for k in range(teams)
    )
    grads, odd, *shares = call(
        kernel,
        "mixer_back",
        outs,
        (part, returned, mixer_grad, mixed, conv, normed, in_own),
        [
            pltpu.VMEM((tokens // 2, 3 * channels), NARROW),
            pltpu.VMEM((tokens, channels), WIDE),
            pltpu.VMEM((features, 3 * channels), WIDE),
        ],
        3 * tokens * features * 3 * channels,
    )
    return grads, odd, shares


def out_back(mixer_in, blocks, taps_grad, teams):
    rows, features = blocks[0].shape
    channels = mixer_in.shape[1]
    share = channels // teams
    low = (share + 15) // 16 * 16

    def kernel(*refs):
        mixer_in, blocks, taps_grad = refs[0], refs[1 : 1 + TEAM], refs[1 + TEAM]
        shares, (total,) = refs[2 + TEAM : 2 + TEAM + teams], refs[2 + TEAM + teams :]
        place, team = where_am_i()
        total[...] = sum(
            dot(mixer_in[at((place ^ m) * rows, rows), :], blocks[m][...], ((0,), (0,)))
            for m in range(TEAM)
        )
        for k in range(teams):
            owner = lax.rem(team + k, teams)
            kind = shares[k].dtype
            shares[k][...] = jnp.zeros_like(shares[k])
            shares[k][:share, :] = total[at(owner * share, share, 8), :].astype(kind)
            shares[k][low : low + 8, :channels] = taps_grad[...].astype(kind)

    outs = tuple(
        shape(NARROW if k == teams - 1 else WIDE, low + 16, features) for k in range(teams)
    )
    return call(
        kernel,
        "out_back",
        outs,
        (mixer_in, *blocks, taps_grad),
        [pltpu.VMEM((channels, features), WIDE)],
        2 * TEAM * rows * channels * features,
    ), low


def body(
    hidden_in,
    seq_start,
    mixer_gain,
    in_weight,
    conv_weight,
    out_weight,
    ffn_gain,
    gate_weight,
    up_weight,
    down_weight,
    cotangent,
):
    net = Net()
    teams = net.teams
    rows, features = hidden_in.shape
    inner = gate_weight.shape[2]
    part = features // net.count
    ffpart = inner // net.count
    channels = features // TEAM
    ffown = inner // TEAM
    line = [[p + TEAM * z for z in range(teams)] for p in range(TEAM)]


    def gather(value):
        return lax.all_gather(value, "dp", axis=0, tiled=True, axis_index_groups=line)

    def reduce(value):
        return lax.psum_scatter(
            value, "dp", scatter_dimension=0, tiled=True, axis_index_groups=line
        )

    down_own = gather(down_weight[0])
    hidden_job = net.spawn(net.blocks_direct(hidden_in))
    sent = in_prepare(
        in_weight[0],
        (mixer_gain, ffn_gain),
        seq_start.reshape(1, rows),
        conv_weight[0].T,
        teams,
    )
    net.need(sent)
    got_job = net.do(net.exchange, sent)
    pair_job = net.do(lambda *x: pair_prepare(*x, teams), gate_weight[0], up_weight[0])
    net.step()
    out_job = net.spawn(net.line_both(out_weight[0]))
    pair_job = net.do(net.exchange, pair_job.result)
    in_job = net.do(gather, got_job.result.reshape(TEAM * (part + 8), 3 * channels))
    net.until(pair_job, in_job, hidden_job)

    def last_rows():
        last = hidden_job.result[0][-HALO:]
        for m in range(1, TEAM):
            block = hidden_job.result[m][-HALO:]
            last = jnp.where(net.place == (TEAM - 1) ^ m, block, last)
        (before,) = yield [(last, ("ring", 1))]
        return before

    halo_job = net.spawn(last_rows())
    before, out_rows_here = net.until(halo_job, out_job)
    weights = in_job.result.reshape(net.count, part + 8, 3 * channels)
    pair_own = gather(net.later(pair_job.result.reshape(TEAM * part, 2 * ffown)))
    out_job = net.spawn(net.blocks(out_rows_here))

    mix_job = net.do(
        lambda *x: mixer_forward(x[:TEAM], x[TEAM], x[TEAM + 1]),
        *hidden_job.result, before, weights,
    )
    (normed, mixed, gated, conv, mixer_in, in_own, gain_one, gain_two, taps, keeps) = net.until(
        mix_job
    )
    mixer_job = net.spawn(net.blocks(mixer_in))
    net.step()
    upstream_job = net.spawn(net.blocks(cotangent))
    mixer_blocks, out_blocks = net.until(mixer_job, out_job)
    project_job = net.do(
        lambda *x: out_project(
            x[:TEAM], x[TEAM : 2 * TEAM], x[2 * TEAM : 3 * TEAM], x[3 * TEAM], teams
        ),
        *mixer_blocks, *out_blocks, *hidden_job.result, gain_two,
    )
    resid, in_odd, in_even = net.until(project_job)
    upstream = net.until(upstream_job)

    def ffn(inputs, which, send):
        operands = (inputs, *upstream[which::2], pair_own, down_own)
        return (lambda *x: ffn_block(x[0], x[1:5], x[5], x[6], send)), operands

    call, operands = ffn(in_odd, 1, True)
    act_odd, grads_odd, back_odd = net.until(net.do(call, *operands))
    call, operands = ffn(in_even, 0, False)
    even_job = net.do(call, *operands)
    ffn_job = net.spawn(
        net.team_sum(
            back_odd,
            lambda arrived: (
                lambda *x: summed_parts(*x, True, "ffn_back"),
                (even_job.result[1], pair_own, arrived),
            ),
        )
    )
    act_even, grads_even = net.until(even_job)
    net.step()
    pair_job = net.do(
        lambda *x: weight_grads(x[:2], x[2:], "pair_grads"),
        in_odd, in_even, grads_odd, grads_even,
    )
    odd_job = net.do(ffn_output, act_odd, down_own)
    ffn_grad = net.until(ffn_job)
    pair_sum = reduce(pair_job.result)

    back_job = net.do(
        lambda *x: resid_back(x[:4], *x[4:7], x[7:], teams),
        *ffn_grad, resid, gain_two, cotangent, *out_blocks,
    )
    resid_grad, rounded, mixer_grad = net.until(back_job)
    down_job = net.do(
        lambda *x: weight_grads(x[:2], x[2:], "down_grads"),
        act_odd, act_even, *upstream[1::2], *upstream[0::2],
    )
    rounded_job = net.spawn(net.blocks(rounded))
    mixer_grad = net.until(net.do(net.exchange, mixer_grad)).reshape(TEAM * rows, channels)
    rounded_job.held = True
    down_sum = reduce(down_job.result)
    output_job = net.spawn(
        net.team_sum(
            odd_job.result,
            lambda arrived: (
                lambda *x: summed_parts(*x, False, "ffn_output_sum"),
                (act_even, down_own, arrived),
            ),
            2,
        )
    )
    gated_part, rim, taps_grad = net.until(
        net.do(conv_back, mixer_grad, mixed, gated, conv, taps, keeps)
    )
    rounded_job.held = False

    def rim_steps():
        (returned,) = yield [(rim, ("back",))]
        return returned

    returned = net.until(net.spawn(rim_steps()))
    mixed_grad, normed_odd, shares = net.until(
        net.do(
            lambda *x: mixer_back(*x, teams),
            gated_part, returned, mixer_grad, mixed, conv, normed, in_own,
        )
    )
    in_job = net.spawn(net.line_sum(shares))
    normed_job = net.spawn(
        net.team_sum(
            normed_odd,
            lambda arrived: (
                lambda *x: summed_parts(*x, True, "mixer_back_sum", True),
                (mixed_grad, in_own, arrived),
            ),
            2,
        )
    )
    low = (part + 15) // 16 * 16
    out_job = net.do(
        lambda *x: out_back(x[0], x[1 : 1 + TEAM], x[1 + TEAM], teams)[0],
        mixer_in, *net.until(rounded_job), taps_grad,
    )
    net.until(out_job)
    out_job = net.spawn(net.line_sum(out_job.result))
    pair_job = net.do(net.exchange, pair_sum.reshape(TEAM, part, 2 * ffown))
    in_grad = net.until(in_job).astype(NARROW)
    in_job = net.do(net.exchange, in_grad.reshape(TEAM, part, 3 * channels))
    finish_job = net.do(
        lambda *x: pair_finish(*x, teams),
        net.until(pair_job), gate_weight[0], up_weight[0], ffn_gain.reshape(part, 1),
    )
    in_grad = net.until(in_job)
    grad_gate, grad_up, grad_ffn_gain = net.until(finish_job)
    normed_grad, ffn_out, out_pack = net.until(normed_job, output_job, out_job)
    in_grad, grad_mixer_gain = in_finish(
        in_grad, in_weight[0], mixer_gain.reshape(part, 1), teams
    )

    def total(parts):
        return sum([part.astype(WIDE) for part in parts[1:]], parts[0])

    own_hidden = hidden_in.astype(WIDE)
    scale_one = scale_of(own_hidden)
    grad_hidden = resid_grad + norm_back(
        total(normed_grad), own_hidden * scale_one, scale_one, gain_one
    )
    hidden_out = (resid + total(ffn_out)).astype(NARROW)
    grad_out = out_pack[:part]
    grad_conv = lax.dynamic_slice(out_pack, (low, net.team * part), (3, part)).T
    return (
        hidden_out,
        grad_hidden,
        grad_mixer_gain.reshape(1, part),
        in_grad[None],
        grad_conv[None],
        grad_out[None],
        grad_ffn_gain.reshape(1, part),
        grad_gate[None],
        grad_up[None],
        down_sum.astype(WIDE)[None],
    )


def solution(mesh):
    tokens, wide, deep = P("dp", None), P(None, "dp"), P(None, "dp", None)
    return jax.shard_map(
        body,
        mesh=mesh,
        in_specs=(tokens, P("dp"), wide, deep, deep, deep, wide, deep, deep, deep, tokens),
        out_specs=(tokens, tokens, wide, deep, deep, deep, wide, deep, deep, deep),
        check_vma=False,
    )
```

```python
import jax
import jax.numpy as jnp
from jax import lax
from jax.experimental import pallas as pl
from jax.experimental.pallas import tpu as pltpu
from jax.sharding import PartitionSpec as P

epsilon = 1e-05
TEAM = 8
HALO = 16
WIDE = jnp.float32
NARROW = jnp.bfloat16


def dot(left, right, contract):
    return lax.dot_general(left, right, (contract, ((), ())), preferred_element_type=WIDE)


def fetch(pairs, sems):
    copies = [pltpu.make_async_copy(a, b, sems.at[i]) for i, (a, b) in enumerate(pairs)]
    for copy in copies:
        copy.start()
    return copies


def shape(kind, *sizes):
    return jax.ShapeDtypeStruct(sizes, kind)


def call(kernel, name, out_shape, operands, scratch=(), flops=0, in_place=False):
    places = {}
    if in_place:
        spec = pl.BlockSpec(memory_space=pl.ANY)
        places["in_specs"] = [spec] * len(operands) if in_place is True else in_place
    size = sum(x.size * x.dtype.itemsize for x in operands)
    return pl.pallas_call(
        kernel,
        out_shape=out_shape,
        scratch_shapes=list(scratch),
        compiler_params=pltpu.CompilerParams(vmem_limit_bytes=60 * 2**20),
        cost_estimate=pl.CostEstimate(flops=flops, bytes_accessed=size, transcendentals=0),
        name=name,
        **places,
    )(*operands)


class Job:
    def __init__(self, steps):
        self.steps = steps
        self.result = None
        self.open = True
        self.request = None
        self.held = False
        self.send(None)

    def send(self, value):
        try:
            self.request = self.steps.send(value)
        except StopIteration as stop:
            self.result, self.open, self.request = stop.value, False, None


class Net:
    def __init__(self):
        self.count = lax.axis_size("dp")
        self.teams = self.count // TEAM
        self.index = lax.axis_index("dp")
        self.place = self.index % TEAM
        self.team = self.index // TEAM
        self.core = self.index % 2
        self.peer = (self.index // 2) % 4
        self.jobs = []
        self.waiting = []
        self.gate = []
        self.extra = []

    def pairs(self, move):
        if move[0] == "swap":
            return [(i, i ^ move[1]) for i in range(self.count)]
        if move[0] == "ring":
            return [(i, (i + move[1] * TEAM) % self.count) for i in range(self.count)]
        if move[0] == "mixed":
            return [(i, i ^ (2 if i % 2 == 0 else 4)) for i in range(self.count)]
        return [(i, i - TEAM) for i in range(TEAM, self.count)]

    def do(self, call, *operands):
        def steps():
            (got,) = yield [(operands, ("call", call))]
            return got

        return self.spawn(steps())

    def spawn(self, steps):
        job = Job(steps)
        if job.open:
            self.jobs.append(job)
        return job

    def need(self, *values):
        self.extra.extend(values)

    def later(self, value):
        return lax.optimization_barrier((value, self.gate))[0]

    def step(self, times=1):
        for _ in range(times):
            self.one_step()

    def one_step(self):
        ready = [job for job in self.jobs if job.request is not None and not job.held]
        values = [move[0] for job in ready for move in job.request]
        self.raw = []
        if values or self.waiting:
            values, _ = lax.optimization_barrier((values, (self.gate, self.extra)))
            self.extra = []
            at = 0
            for job in ready:
                span = 1
                got = []
                moves = job.request
                for move in moves:
                    if len(move) > 2:
                        span = move[2]
                    if move[1][0] == "call":
                        got.append(move[1][1](*values[at]))
                    else:
                        got.append(lax.ppermute(values[at], "dp", self.pairs(move[1])))
                    at += 1
                job.request = None
                self.raw.extend(zip([move[1] for move in moves], got))
                self.waiting.append([span, job, got])
        for entry in self.waiting:
            entry[0] -= 1
        done = [entry for entry in self.waiting if entry[0] <= 0]
        self.waiting = [entry for entry in self.waiting if entry[0] > 0]
        results = lax.optimization_barrier([entry[2] for entry in done])
        self.gate = results
        for (_, job, _), got in zip(done, results):
            job.send(got)
        self.jobs = [job for job in self.jobs if job.open]

    def until(self, *jobs):
        while any(job.open for job in jobs):
            self.one_step()
        return [job.result for job in jobs] if len(jobs) > 1 else jobs[0].result


    def blocks(self, value):
        across, along, twin = yield [
            (value, ("swap", 2)),
            (value, ("swap", 4)),
            (value, ("swap", 1)),
        ]
        corner, across_twin, along_twin = yield [
            (jnp.where(self.core == 0, along, across), ("mixed",)),
            (across, ("swap", 1)),
            (along, ("swap", 1)),
        ]
        (corner_twin,) = yield [(corner, ("swap", 1))]
        return [value, twin, across, across_twin, along, along_twin, corner, corner_twin]

    def blocks_direct(self, value):
        found = yield [(value, ("swap", mask)) for mask in (2, 4, 6, 1)]
        twins = yield [(block, ("swap", 1)) for block in found[:3]]
        return [value, found[3], found[0], twins[0], found[1], twins[1], found[2], twins[2]]

    def team_sum(self, odd, fold, split=False, span=1):
        (arrived,) = yield [(odd, ("swap", 1))]
        call, operands = fold(arrived)
        (parts,) = yield [(operands, ("call", call))]
        sends = [(part, ("swap", mask), span) for part, mask in zip(parts[1:], (6, 2, 4))]
        if split:
            sides = yield sends[1:]
            return [parts[0]] + (yield sends[:1]) + sides
        moved = yield sends
        return [parts[0]] + moved

    def exchange(self, blocks):
        groups = [[base + q for q in range(TEAM)] for base in range(0, self.count, TEAM)]
        return lax.all_to_all(blocks, "dp", 0, 0, axis_index_groups=groups, tiled=True)

    def line_both(self, value):
        teams = self.teams
        found, up, down = {0: value}, value, value
        for step in range(1, teams // 2 + 1):
            moves = [(up, ("ring", 1))]
            if step < teams - step:
                moves.append((down, ("ring", teams - 1)))
            got = yield moves
            found[step], up = got[0], got[0]
            if len(got) > 1:
                found[teams - step], down = got[1], got[1]
        return jnp.concatenate([found[k] for k in range(teams)], 0)

    def line_send(self, parts, span=1):
        return (yield [(part, ("ring", k + 1), span) for k, part in enumerate(parts)])

    def line_sum(self, shares):
        total = shares[-1].astype(NARROW)
        for share in reversed(shares[:-1]):
            (got,) = yield [(total, ("ring", 1))]
            total = share + got.astype(WIDE)
            total = total if share is shares[0] else total.astype(NARROW)
        return total


def scale_of(values):
    return lax.rsqrt(jnp.mean(values * values, axis=1, keepdims=True) + epsilon)


def norm_back(upstream, normed, scaler, gain):
    scaled = upstream * gain
    return scaler * (scaled - normed * jnp.mean(scaled * normed, axis=1, keepdims=True))


def where_am_i():
    index = lax.axis_index("dp")
    return index % TEAM, index // TEAM


def at(start, size, step=16):
    return pl.ds(pl.multiple_of(start, step), size)


def summed_parts(left, right, arrived, turned, name, relative=False):
    rows, width = arrived.shape[0] // 4, arrived.shape[1]
    deep = left.shape[1]
    contract = ((1,), (1,)) if turned else ((1,), (0,))

    def kernel(left_in, right_in, arrived_in, own, corner, across, along, left, right, arrived, sems):
        place, _ = where_am_i()
        copies = [(right_in, right), (arrived_in, arrived)]
        for k in range(4):
            source = left_in
            if relative:
                source = left_in.at[at((place ^ (2 * k)) * rows, rows), :]
            else:
                source = left_in.at[k * rows : (k + 1) * rows, :]
            copies.append((source, left.at[k * rows : (k + 1) * rows, :]))
        for copy in fetch(copies, sems):
            copy.wait()
        total = dot(left[...], right[...], contract) + arrived[...].astype(WIDE)
        for k, out in ((3, corner), (1, across), (2, along), (0, own)):
            out[...] = total[k * rows : (k + 1) * rows].astype(out.dtype)

    outs = (shape(WIDE, rows, width),) + (shape(NARROW, rows, width),) * 3
    return call(
        kernel,
        name,
        outs,
        (left, right, arrived),
        [
            pltpu.VMEM((4 * rows, deep), NARROW),
            pltpu.VMEM(right.shape, NARROW),
            pltpu.VMEM(arrived.shape, NARROW),
            pltpu.SemaphoreType.DMA((6,)),
        ],
        8 * rows * deep * width,
        in_place=True,
    )


def pieces(ffpart, even, own):
    runs = []
    for z in range(own // ffpart):
        for start, stop in ((0, even), (even, own)):
            low, high = max(z * ffpart, start), min((z + 1) * ffpart, stop)
            if low < high:
                at_gate = low if start == 0 else 2 * even + low - even
                at_up = even + low if start == 0 else own + low
                runs.append((z, low, high, at_gate, at_up))
    return runs


def in_prepare(weight, gains, marks, taps, teams):
    part, width = weight.shape
    features = width // 3
    channels = features // TEAM
    slots = max(128, TEAM * part) // part

    def kernel(weight, gain_one, gain_two, marks, taps, out, wide, small):
        index = lax.axis_index("dp")
        whole = weight[...].astype(WIDE)
        small[...] = jnp.zeros_like(small)
        for slot in range(slots):
            mine = lax.rem(index, slots) == slot
            for row, gain in enumerate((gain_one, gain_two)):
                value = gain[...].astype(WIDE)
                value = jnp.where(mine, value, jnp.zeros_like(value))
                small[row : row + 1, slot * part : (slot + 1) * part] = value
        small[0:1, 2 * channels :] = marks[...].astype(WIDE)
        for slot in range(teams):
            value = taps[...].astype(WIDE)
            value = jnp.where(index // TEAM == slot, value, jnp.zeros_like(value))
            for k in range(3):
                to = k * channels + slot * part
                small[2:3, to : to + part] = value[k : k + 1, :]
        for p in range(TEAM):
            for k in range(3):
                for z in range(teams):
                    source = k * features + (z * TEAM + p) * part
                    to = k * channels + z * part
                    wide[:, to : to + part] = whole[:, source : source + part]
            out[p, :part, :] = wide[...].astype(NARROW)
            out[p, part:, :] = small[...].astype(NARROW)

    return call(
        kernel,
        "in_prepare",
        shape(NARROW, TEAM, part + 8, 3 * channels),
        (weight, *gains, marks, taps),
        [pltpu.VMEM((part, 3 * channels), WIDE), pltpu.VMEM((8, 3 * channels), WIDE)],
    )


def in_finish(blocks, weight, gain, teams):
    part, width = weight.shape
    features = width // 3
    channels = features // TEAM

    def kernel(blocks, weight, gain, out, gain_grad):
        for p in range(TEAM):
            block = blocks[p].astype(WIDE)
            for k in range(3):
                for z in range(teams):
                    to = k * features + (z * TEAM + p) * part
                    source = k * channels + z * part
                    out[:, to : to + part] = block[:, source : source + part]
        product = jnp.sum(weight[...].astype(WIDE) * out[...], axis=1, keepdims=True)
        gain_grad[...] = (product / gain[...].astype(WIDE)).reshape(1, part)

    outs = (shape(WIDE, part, width), shape(WIDE, 1, part))
    return call(kernel, "in_finish", outs, (blocks, weight, gain))


def pair_prepare(gate, up, teams):
    part, inner = gate.shape
    own = inner // TEAM
    ffpart = own // teams
    even = own // 128 * 128
    runs = pieces(ffpart, even, own)

    def kernel(gate, up, out, wide):
        gates, ups = gate[...].astype(WIDE), up[...].astype(WIDE)
        for p in range(TEAM):
            for z, low, high, at_gate, at_up in runs:
                source = (z * TEAM + p) * ffpart + low - z * ffpart
                size = high - low
                wide[:, at_gate : at_gate + size] = gates[:, source : source + size]
                wide[:, at_up : at_up + size] = ups[:, source : source + size]
            out[p] = wide[...].astype(NARROW)

    out = shape(NARROW, TEAM, part, 2 * own)
    scratch = [pltpu.VMEM((part, 2 * own), WIDE)]
    return call(kernel, "pair_prepare", out, (gate, up), scratch)


def pair_finish(blocks, gate, up, gain, teams):
    part, inner = gate.shape
    own = inner // TEAM
    ffpart = own // teams
    even = own // 128 * 128
    runs = pieces(ffpart, even, own)

    def kernel(blocks, gate, up, gain, gate_grad, up_grad, gain_grad):
        for p in range(TEAM):
            block = blocks[p].astype(WIDE)
            for z, low, high, at_gate, at_up in runs:
                to = (z * TEAM + p) * ffpart + low - z * ffpart
                size = high - low
                gate_grad[:, to : to + size] = block[:, at_gate : at_gate + size]
                up_grad[:, to : to + size] = block[:, at_up : at_up + size]
        product = gate[...].astype(WIDE) * gate_grad[...] + up[...].astype(WIDE) * up_grad[...]
        total = jnp.sum(product, axis=1, keepdims=True) / gain[...].astype(WIDE)
        gain_grad[...] = total.reshape(1, part)

    outs = (shape(WIDE, part, inner), shape(WIDE, part, inner), shape(WIDE, 1, part))
    return call(kernel, "pair_finish", outs, (blocks, gate, up, gain))


def mixer_forward(blocks, before, weights):
    rows, features = blocks[0].shape
    tokens = TEAM * rows
    count, _, channels = weights.shape
    channels = channels // 3
    teams = count // TEAM
    share, part = features // teams, features // count

    def kernel(*refs):
        blocks, (before, weights), refs = refs[:TEAM], refs[TEAM : TEAM + 2], refs[TEAM + 2 :]
        normed, mixed, gated, conv, mixer_in, in_own, gain, gain_two, taps, keeps = refs[:10]
        hs, small, sems = refs[10:]
        place, team = where_am_i()
        copies = [(weights.at[:, part:, :], small)]
        for d in range(count):
            to = in_own.at[d * part : (d + 1) * part, :]
            copies.append((weights.at[d, :part, :], to))
        for m in range(TEAM):
            copies.append((blocks[m], hs.at[at(HALO + (place ^ m) * rows, rows), :]))
        copies.append((before, hs.at[:HALO, :]))
        for copy in fetch(copies, sems):
            copy.wait()
        first = hs[:HALO, :]
        hs[:HALO, :] = jnp.where(team > 0, first, jnp.zeros_like(first))
        total = jnp.zeros((1, 3 * channels), WIDE)
        gain[...] = jnp.zeros_like(gain)
        gain_two[...] = jnp.zeros_like(gain_two)
        span = max(share, 128)
        for z in range(teams):
            both = sum(small[z * TEAM + p].astype(WIDE) for p in range(TEAM))
            one, two = both[0:1], both[1:2]
            total = total + small[z * TEAM + place].astype(WIDE)[2:3]
            to = slice(z * share // span * span, z * share // span * span + span)
            gain[:, to] = gain[:, to] + one[:, :span]
            gain_two[:, to] = gain_two[:, to] + two[:, :span]
        taps[...] = jnp.zeros_like(taps)
        for k in range(3):
            taps[k : k + 1, :] = total[:, k * channels : (k + 1) * channels]
        marks = [
            1.0 - small[team * TEAM + p].astype(WIDE)[0:1, 2 * channels :] for p in range(TEAM)
        ]
        keep = jnp.concatenate([mark.reshape(rows, 1) for mark in marks], 0)
        keeps[8:, 0:1] = keep
        before_team = lax.rem(team + teams - 1, teams) * TEAM + TEAM - 1
        last = 1.0 - small[before_team].astype(WIDE)[0:1, 3 * channels - 1 :]
        keeps[7:8, 0:1] = last
        keeps[8:, 1:2] = keep * keeps[7 : 7 + tokens, 0:1]
        scale = gain[...]

        def norm(start, size):
            values = hs[at(start, size), :].astype(WIDE)
            values = values * scale_of(values) * scale
            normed[at(start, size), :] = values.astype(NARROW)

        norm(0, HALO)

        @pl.loop(0, TEAM)
        def _(step):
            norm(HALO + step * rows, rows)

        mixed[...] = dot(normed[...], in_own[...], ((1,), (0,)))
        gated[...] = (mixed[:, :channels] * mixed[:, 2 * channels :]).astype(NARROW).astype(WIDE)
        conv_out = (
            taps[2:3, :] * gated[HALO:, :]
            + taps[1:2, :] * (keeps[8:, 0:1] * gated[HALO - 1 : HALO - 1 + tokens, :])
            + taps[0:1, :] * (keeps[8:, 1:2] * gated[HALO - 2 : HALO - 2 + tokens, :])
        )
        conv[...] = conv_out
        mixer_in[...] = (mixed[HALO:, channels : 2 * channels] * conv_out).astype(NARROW)

    outs = (
        shape(NARROW, HALO + tokens, features),
        shape(WIDE, HALO + tokens, 3 * channels),
        shape(WIDE, HALO + tokens, channels),
        shape(WIDE, tokens, channels),
        shape(NARROW, tokens, channels),
        shape(NARROW, features, 3 * channels),
        shape(WIDE, 1, features),
        shape(WIDE, 1, features),
        shape(WIDE, 8, channels),
        shape(WIDE, 8 + tokens, 2),
    )
    return call(
        kernel,
        "mixer_forward",
        outs,
        (*blocks, before, weights),
        [
            pltpu.VMEM((HALO + tokens, features), NARROW),
            pltpu.VMEM((count, 8, 3 * channels), NARROW),
            pltpu.SemaphoreType.DMA((count + TEAM + 2,)),
        ],
        2 * tokens * features * 3 * channels,
        in_place=True,
    )


def out_rows(blocks, whole, teams):
    place, team = where_am_i()
    channels = blocks[0].shape[0]
    share = channels // teams
    copies = []
    for m, block in enumerate(blocks):
        for k in range(teams):
            to = (place ^ m) * channels + lax.rem(team - k + teams, teams) * share
            copies.append((block.at[k * share : (k + 1) * share, :], whole.at[at(to, share, 8), :]))
    return copies


def out_project(mixer_blocks, out_blocks, hidden_blocks, gain, teams):
    rows, features = hidden_blocks[0].shape
    tokens, channels = mixer_blocks[0].shape

    def kernel(*refs):
        mixer_in, out_in, hidden_in = [refs[k * TEAM : (k + 1) * TEAM] for k in range(3)]
        gain, resid, odd, even, mixer, turned, out, hidden, sems = refs[3 * TEAM :]
        place, _ = where_am_i()
        copies = out_rows(out_in, out, teams)
        for m in range(TEAM):
            to = mixer.at[:, at((place ^ m) * channels, channels, 128)]
            copies.append((mixer_in[m], to))
            copies.append((hidden_in[m], hidden.at[m]))
        for copy in fetch(copies, sems):
            copy.wait()
        for half, side in ((1, odd), (0, even)):
            for k in range(TEAM // 2):
                source = mixer[at((place ^ (2 * k + half)) * rows, rows), :]
                turned[k * rows : (k + 1) * rows, :] = source
            product = dot(turned[...], out[...], ((1,), (0,)))
            for k in range(TEAM // 2):
                span = slice(k * rows, (k + 1) * rows)
                total = hidden[2 * k + half].astype(WIDE) + product[span]
                side[span, :] = (total * scale_of(total) * gain[...]).astype(NARROW)
                if k + half == 0:
                    resid[...] = total

    outs = (shape(WIDE, rows, features),) + (shape(NARROW, tokens // 2, features),) * 2
    any_place, in_vmem = pl.BlockSpec(memory_space=pl.ANY), pl.BlockSpec(memory_space=pltpu.VMEM)
    return call(
        kernel,
        "out_project",
        outs,
        (*mixer_blocks, *out_blocks, *hidden_blocks, gain),
        [
            pltpu.VMEM((tokens, features), NARROW),
            pltpu.VMEM((tokens // 2, features), NARROW),
            pltpu.VMEM((features, features), NARROW),
            pltpu.VMEM((TEAM, rows, features), NARROW),
            pltpu.SemaphoreType.DMA((TEAM * teams + 2 * TEAM,)),
        ],
        2 * tokens * features * features,
        in_place=[any_place] * (3 * TEAM) + [in_vmem],
    )


def ffn_parts(gate, up, grad):
    sigmoid = 1.0 / (1.0 + jnp.exp(-gate))
    scaled = gate * sigmoid
    gate_grad = grad * up * sigmoid * (1.0 + gate * (1.0 - sigmoid))
    return scaled * up, gate_grad, grad * scaled


def ffn_block(odd, even, upstream, pair, down):
    count = len(upstream)
    rows, features = upstream[0].shape
    own = down.shape[0]
    units = own // 128 * 128
    width = own - units
    half = odd.shape[0]

    def kernel(odd_in, even_in, *refs):
        g_in, (pair_in, down_in), refs = refs[:count], refs[count : count + 2], refs[count + 2 :]
        acts, grads, weight = refs[:2], refs[2:4], refs[4]
        xs, gs, pair, down, last, all_grads, sems = refs[5:]
        first = [(odd_in, xs.at[:half, :]), (pair_in, pair)]
        second = [(g_in[k], gs.at[k * rows : (k + 1) * rows, :]) for k in range(count)]
        second += [(down_in, down), (even_in, xs.at[half:, :])]
        copies = fetch(first + second, sems)
        for copy in copies[:2]:
            copy.wait()
        for side in range(2):
            span = slice(side * half, (side + 1) * half)
            act, grad_out = acts[side], grads[side]
            x = xs[span, :]
            gate = dot(x, pair[:, :units], ((1,), (0,)))
            up = dot(x, pair[:, units : 2 * units], ((1,), (0,)))
            if side == 0:
                for copy in copies[2:]:
                    copy.wait()
                last[:width, :] = down[units:, :]
                last[width:, :] = down[units:, :]
            g = gs[span, :]
            grad = dot(g, down[:units, :], ((1,), (1,)))
            value, gate_grad, up_grad = ffn_parts(gate, up, grad)
            act[:, :units] = value.astype(NARROW)
            all_grads[span, :units] = gate_grad.astype(NARROW)
            all_grads[span, units : 2 * units] = up_grad.astype(NARROW)
            both = dot(x, pair[:, 2 * units :], ((1,), (0,)))
            turned = pltpu.roll(both, width, 1)
            lower = lax.broadcasted_iota(jnp.int32, both.shape, 1) < width
            grad = dot(g, last[...], ((1,), (1,)))
            value, gate_grad, up_grad = ffn_parts(
                jnp.where(lower, both, turned), jnp.where(lower, turned, both), grad
            )
            act[:, units:] = value[:, :width].astype(NARROW)
            all_grads[span, 2 * units :] = jnp.where(lower, gate_grad, up_grad).astype(NARROW)
            grad_out[...] = all_grads[span, :]
        for start in range(0, features, 256):
            total = dot(xs[:, start : start + 256], all_grads[...], ((0,), (0,)))
            weight[start : start + 256, :] = total.astype(NARROW)

    outs = (shape(NARROW, half, own),) * 2 + (shape(NARROW, half, 2 * own),) * 2
    return call(
        kernel,
        "ffn",
        outs + (shape(NARROW, features, 2 * own),),
        (odd, even, *upstream, pair, down),
        [
            pltpu.VMEM((2 * half, features), NARROW),
            pltpu.VMEM((2 * half, features), NARROW),
            pltpu.VMEM((features, 2 * own), NARROW),
            pltpu.VMEM((own, features), NARROW),
            pltpu.VMEM((2 * width, features), NARROW),
            pltpu.VMEM((2 * half, 2 * own), NARROW),
            pltpu.SemaphoreType.DMA((count + 4,)),
        ],
        20 * half * features * own,
        in_place=True,
    )


def product(left, right, turned, name):
    contract = ((1,), (1,)) if turned else ((1,), (0,))

    def kernel(left, right, out):
        out[...] = dot(left[...], right[...], contract).astype(NARROW)

    rows, wide = left.shape[0], right.shape[0 if turned else 1]
    return call(kernel, name, shape(NARROW, rows, wide), (left, right), flops=2 * rows * right.size)


def weight_grads(lefts, rights, name):
    deep, wide = lefts[0].shape[1], rights[0].shape[1]
    tokens = sum(left.shape[0] for left in lefts)

    def kernel(*refs):
        ins, (out, left, right, sems) = refs[: len(lefts) + len(rights)], refs[-4:]
        pairs = []
        for blocks, whole in ((ins[: len(lefts)], left), (ins[len(lefts) :], right)):
            row = 0
            for block in blocks:
                pairs.append((block, whole.at[row : row + block.shape[0], :]))
                row += block.shape[0]
        for copy in fetch(pairs, sems):
            copy.wait()
        for start in range(0, deep, 256):
            stop = min(start + 256, deep)
            total = dot(left[:, start:stop], right[...], ((0,), (0,)))
            out[start:stop, :] = total.astype(NARROW)

    return call(
        kernel,
        name,
        shape(NARROW, deep, wide),
        (*lefts, *rights),
        [
            pltpu.VMEM((tokens, deep), NARROW),
            pltpu.VMEM((tokens, wide), NARROW),
            pltpu.SemaphoreType.DMA((len(lefts) + len(rights),)),
        ],
        2 * tokens * deep * wide,
        in_place=True,
    )


def resid_back(parts, resid, gain, upstream, out_blocks, teams):
    rows, features = resid.shape
    channels = features // TEAM

    def kernel(own, corner, across, along, resid, gain, upstream, *refs):
        out_in, (resid_grad, rounded, mixer_grad, out, sems) = refs[:TEAM], refs[TEAM:]
        copies = fetch(out_rows(out_in, out, teams), sems)
        grad = own[...] + sum(part[...].astype(WIDE) for part in (corner, across, along))
        values = resid[...]
        scale = scale_of(values)
        grad = upstream[...].astype(WIDE) + norm_back(grad, values * scale, scale, gain[...])
        resid_grad[...] = grad
        rounded[...] = grad.astype(NARROW)
        for copy in copies:
            copy.wait()
        product = dot(rounded[...], out[...], ((1,), (1,))).astype(NARROW)
        for p in range(TEAM):
            mixer_grad[p] = product[:, p * channels : (p + 1) * channels]

    outs = (
        shape(WIDE, rows, features),
        shape(NARROW, rows, features),
        shape(NARROW, TEAM, rows, channels),
    )
    any_place, in_vmem = pl.BlockSpec(memory_space=pl.ANY), pl.BlockSpec(memory_space=pltpu.VMEM)
    return call(
        kernel,
        "resid_back",
        outs,
        (*parts, resid, gain, upstream, *out_blocks),
        [
            pltpu.VMEM((features, features), NARROW),
            pltpu.SemaphoreType.DMA((TEAM * teams,)),
        ],
        2 * rows * features * features,
        in_place=[in_vmem] * 7 + [any_place] * TEAM,
    )


def conv_back(mixer_grad, mixed, gated, conv, taps, keeps):
    tokens, channels = conv.shape

    def kernel(mixer_grad, mixed, gated, conv, taps, keeps, part, rim, taps_grad, ones, twos):
        grad = mixer_grad[...].astype(WIDE)
        conv_grad = grad * mixed[HALO:, channels : 2 * channels]
        one, two = keeps[8:, 0:1] * conv_grad, keeps[8:, 1:2] * conv_grad
        zeros = jnp.zeros((8, channels), WIDE)
        taps_grad[...] = zeros
        for k, (left, back) in enumerate(((two, 2), (one, 1), (conv_grad, 0))):
            product = left * gated[HALO - back : HALO - back + tokens, :]
            taps_grad[k : k + 1, :] = jnp.sum(product, axis=0, keepdims=True)
        ones[:tokens, :] = taps[1:2, :] * one
        twos[:tokens, :] = taps[0:1, :] * two
        ones[tokens:, :] = zeros
        twos[tokens:, :] = zeros
        rim[...] = zeros
        rim[6:7, :] = twos[0:1, :]
        rim[7:8, :] = twos[1:2, :] + ones[0:1, :]
        part[...] = taps[2:3, :] * conv_grad + ones[1 : tokens + 1, :] + twos[2 : tokens + 2, :]

    outs = (shape(WIDE, tokens, channels), shape(WIDE, 8, channels), shape(WIDE, 8, channels))
    scratch = [pltpu.VMEM((tokens + 8, channels), WIDE)] * 2
    return call(
        kernel, "conv_back", outs, (mixer_grad, mixed, gated, conv, taps, keeps), scratch
    )


def mixer_back(part, returned, mixer_grad, mixed, conv, normed, in_own, teams):
    tokens, channels = conv.shape
    features = in_own.shape[0]
    rows, share = tokens // TEAM, features // teams

    def kernel(*refs):
        part, returned, mixer_grad, mixed, conv, normed, in_own, grads, odd = refs[:9]
        shares, (side, whole, weight) = refs[9 : 9 + teams], refs[9 + teams :]
        place, team = where_am_i()
        whole[...] = part[...]
        whole[tokens - 8 :, :] = part[tokens - 8 :, :] + returned[...]
        gated_grad = whole[...]
        grads[:, :channels] = (gated_grad * mixed[HALO:, 2 * channels :]).astype(NARROW)
        grads[:, channels : 2 * channels] = (
            mixer_grad[...].astype(WIDE) * conv[...]
        ).astype(NARROW)
        grads[:, 2 * channels :] = (gated_grad * mixed[HALO:, :channels]).astype(NARROW)
        for chip in range(TEAM // 2):
            at_place = place ^ (2 * chip + 1)
            side[chip * rows : (chip + 1) * rows, :] = grads[at(at_place * rows, rows), :]
        step = features // 4
        for start in range(0, features, step):
            span = slice(start, start + step)
            weight[span, :] = dot(normed[HALO:, span], grads[...], ((0,), (0,)))
        for k in range(teams):
            owner = lax.rem(team + k, teams)
            shares[k][...] = weight[at(owner * share, share), :].astype(shares[k].dtype)
        odd[...] = dot(side[...], in_own[...], ((1,), (1,))).astype(NARROW)

    outs = (shape(NARROW, tokens, 3 * channels), shape(NARROW, tokens // 2, features))
    outs += tuple(
        shape(NARROW if k == teams - 1 else WIDE, share, 3 * channels) for k in range(teams)
    )
    grads, odd, *shares = call(
        kernel,
        "mixer_back",
        outs,
        (part, returned, mixer_grad, mixed, conv, normed, in_own),
        [
            pltpu.VMEM((tokens // 2, 3 * channels), NARROW),
            pltpu.VMEM((tokens, channels), WIDE),
            pltpu.VMEM((features, 3 * channels), WIDE),
        ],
        3 * tokens * features * 3 * channels,
    )
    return grads, odd, shares


def out_back(mixer_in, blocks, taps_grad, teams):
    rows, features = blocks[0].shape
    channels = mixer_in.shape[1]
    share = channels // teams
    low = (share + 15) // 16 * 16

    def kernel(*refs):
        mixer_in, blocks, taps_grad = refs[0], refs[1 : 1 + TEAM], refs[1 + TEAM]
        shares, (total,) = refs[2 + TEAM : 2 + TEAM + teams], refs[2 + TEAM + teams :]
        place, team = where_am_i()
        total[...] = sum(
            dot(mixer_in[at((place ^ m) * rows, rows), :], blocks[m][...], ((0,), (0,)))
            for m in range(TEAM)
        )
        for k in range(teams):
            owner = lax.rem(team + k, teams)
            kind = shares[k].dtype
            shares[k][...] = jnp.zeros_like(shares[k])
            shares[k][:share, :] = total[at(owner * share, share, 8), :].astype(kind)
            shares[k][low : low + 8, :channels] = taps_grad[...].astype(kind)

    outs = tuple(
        shape(NARROW if k == teams - 1 else WIDE, low + 16, features) for k in range(teams)
    )
    return call(
        kernel,
        "out_back",
        outs,
        (mixer_in, *blocks, taps_grad),
        [pltpu.VMEM((channels, features), WIDE)],
        2 * TEAM * rows * channels * features,
    ), low


def body(
    hidden_in,
    seq_start,
    mixer_gain,
    in_weight,
    conv_weight,
    out_weight,
    ffn_gain,
    gate_weight,
    up_weight,
    down_weight,
    cotangent,
):
    net = Net()
    teams = net.teams
    rows, features = hidden_in.shape
    inner = gate_weight.shape[2]
    part = features // net.count
    ffpart = inner // net.count
    channels = features // TEAM
    ffown = inner // TEAM
    line = [[p + TEAM * z for z in range(teams)] for p in range(TEAM)]


    def gather(value):
        return lax.all_gather(value, "dp", axis=0, tiled=True, axis_index_groups=line)

    def reduce(value):
        return lax.psum_scatter(
            value, "dp", scatter_dimension=0, tiled=True, axis_index_groups=line
        )

    down_own = gather(down_weight[0])
    hidden_job = net.spawn(net.blocks_direct(hidden_in))
    sent = in_prepare(
        in_weight[0],
        (mixer_gain, ffn_gain),
        seq_start.reshape(1, rows),
        conv_weight[0].T,
        teams,
    )
    net.need(sent)
    got_job = net.do(net.exchange, sent)
    pair_job = net.do(lambda *x: pair_prepare(*x, teams), gate_weight[0], up_weight[0])
    net.step()
    out_job = net.spawn(net.line_both(out_weight[0]))
    pair_job = net.do(net.exchange, pair_job.result)
    in_job = net.do(gather, got_job.result.reshape(TEAM * (part + 8), 3 * channels))
    net.until(pair_job, in_job, hidden_job)
    pair_own = gather(pair_job.result.reshape(TEAM * part, 2 * ffown))
    upstream_job = net.spawn(net.blocks(cotangent))

    def last_rows():
        last = hidden_job.result[0][-HALO:]
        for m in range(1, TEAM):
            block = hidden_job.result[m][-HALO:]
            last = jnp.where(net.place == (TEAM - 1) ^ m, block, last)
        (before,) = yield [(last, ("ring", 1))]
        return before

    halo_job = net.spawn(last_rows())
    before, out_rows_here = net.until(halo_job, out_job)
    upstream_job.held = True
    weights = in_job.result.reshape(net.count, part + 8, 3 * channels)
    out_job = net.spawn(net.blocks(out_rows_here))

    mix_job = net.do(
        lambda *x: mixer_forward(x[:TEAM], x[TEAM], x[TEAM + 1]),
        *hidden_job.result, before, weights,
    )
    (normed, mixed, gated, conv, mixer_in, in_own, gain_one, gain_two, taps, keeps) = net.until(
        mix_job
    )
    mixer_job = net.spawn(net.blocks(mixer_in))
    net.step(2)
    upstream_job.held = False
    mixer_blocks, out_blocks = net.until(mixer_job, out_job)
    project_job = net.do(
        lambda *x: out_project(
            x[:TEAM], x[TEAM : 2 * TEAM], x[2 * TEAM : 3 * TEAM], x[3 * TEAM], teams
        ),
        *mixer_blocks, *out_blocks, *hidden_job.result, gain_two,
    )
    resid, in_odd, in_even = net.until(project_job)
    upstream = net.until(upstream_job)

    ffn_job = net.do(
        lambda *x: ffn_block(x[0], x[1], x[2 : 2 + TEAM], x[2 + TEAM], x[3 + TEAM]),
        in_odd, in_even, *upstream[1::2], *upstream[0::2], pair_own, down_own,
    )
    act_odd, act_even, grads_odd, grads_even, pair_all = net.until(ffn_job)
    pair_sum = reduce(pair_all)
    back_odd = net.until(
        net.do(lambda *x: product(*x, True, "ffn_back_odd"), grads_odd, pair_own)
    )
    ffn_job = net.spawn(
        net.team_sum(
            back_odd,
            lambda arrived: (
                lambda *x: summed_parts(*x, True, "ffn_back"),
                (grads_even, pair_own, arrived),
            ),
        )
    )
    odd_job = net.do(lambda *x: product(*x, False, "ffn_output"), act_odd, down_own)
    net.step()
    output_job = net.spawn(
        net.team_sum(
            odd_job.result,
            lambda arrived: (
                lambda *x: summed_parts(*x, False, "ffn_output_sum"),
                (act_even, down_own, arrived),
            ),
            True,
        )
    )
    net.step()
    down_job = net.do(
        lambda *x: weight_grads(x[:2], x[2:], "down_grads"),
        act_odd, act_even, *upstream[1::2], *upstream[0::2],
    )
    ffn_grad = net.until(ffn_job)
    down_sum = reduce(down_job.result)

    back_job = net.do(
        lambda *x: resid_back(x[:4], *x[4:7], x[7:], teams),
        *ffn_grad, resid, gain_two, cotangent, *out_blocks,
    )
    resid_grad, rounded, mixer_grad = net.until(back_job)
    output_job.held = True
    rounded_job = net.spawn(net.blocks(rounded))
    mixer_grad = net.until(net.do(net.exchange, mixer_grad)).reshape(TEAM * rows, channels)
    rounded_job.held = True
    gated_part, rim, taps_grad = net.until(
        net.do(conv_back, mixer_grad, mixed, gated, conv, taps, keeps)
    )
    rounded_job.held = False
    output_job.held = False

    def rim_steps():
        (returned,) = yield [(rim, ("back",))]
        return returned

    returned = net.until(net.spawn(rim_steps()))
    mixed_grad, normed_odd, shares = net.until(
        net.do(
            lambda *x: mixer_back(*x, teams),
            gated_part, returned, mixer_grad, mixed, conv, normed, in_own,
        )
    )
    in_job = net.spawn(net.line_sum(shares))
    pair_job = net.do(net.exchange, pair_sum.reshape(TEAM, part, 2 * ffown))
    normed_job = net.spawn(
        net.team_sum(
            normed_odd,
            lambda arrived: (
                lambda *x: summed_parts(*x, True, "mixer_back_sum", True),
                (mixed_grad, in_own, arrived),
            ),
            span=2,
        )
    )
    low = (part + 15) // 16 * 16
    out_job = net.do(
        lambda *x: out_back(x[0], x[1 : 1 + TEAM], x[1 + TEAM], teams)[0],
        mixer_in, *net.until(rounded_job), taps_grad,
    )
    net.until(out_job)
    net.need(down_sum)
    out_job = net.spawn(net.line_sum(out_job.result))
    in_grad = net.until(in_job).astype(NARROW)
    in_job = net.do(net.exchange, in_grad.reshape(TEAM, part, 3 * channels))
    finish_job = net.do(
        lambda *x: pair_finish(*x, teams),
        net.until(pair_job), gate_weight[0], up_weight[0], ffn_gain.reshape(part, 1),
    )
    in_grad = net.until(in_job)
    grad_gate, grad_up, grad_ffn_gain = net.until(finish_job)
    normed_grad, ffn_out, out_pack = net.until(normed_job, output_job, out_job)
    in_grad, grad_mixer_gain = in_finish(
        in_grad, in_weight[0], mixer_gain.reshape(part, 1), teams
    )

    def total(parts):
        return sum([part.astype(WIDE) for part in parts[1:]], parts[0])

    own_hidden = hidden_in.astype(WIDE)
    scale_one = scale_of(own_hidden)
    grad_hidden = resid_grad + norm_back(
        total(normed_grad), own_hidden * scale_one, scale_one, gain_one
    )
    hidden_out = (resid + total(ffn_out)).astype(NARROW)
    grad_out = out_pack[:part]
    grad_conv = lax.dynamic_slice(out_pack, (low, net.team * part), (3, part)).T
    return (
        hidden_out,
        grad_hidden,
        grad_mixer_gain,
        in_grad[None],
        grad_conv[None],
        grad_out[None],
        grad_ffn_gain,
        grad_gate[None],
        grad_up[None],
        down_sum.astype(WIDE)[None],
    )


def solution(mesh):
    tokens, wide, deep = P("dp", None), P(None, "dp"), P(None, "dp", None)
    return jax.shard_map(
        body,
        mesh=mesh,
        in_specs=(tokens, P("dp"), wide, deep, deep, deep, wide, deep, deep, deep, tokens),
        out_specs=(tokens, tokens, wide, deep, deep, deep, wide, deep, deep, deep),
        check_vma=False,
    )
```

```python
import jax
import jax.numpy as jnp
from jax import lax
from jax.experimental import pallas as pl
from jax.experimental.pallas import tpu as pltpu
from jax.sharding import PartitionSpec as P

epsilon = 1e-05
TEAM = 8
HALO = 16
WIDE = jnp.float32
NARROW = jnp.bfloat16


def dot(left, right, contract):
    return lax.dot_general(left, right, (contract, ((), ())), preferred_element_type=WIDE)


def fetch(pairs, sems):
    copies = [pltpu.make_async_copy(a, b, sems.at[i]) for i, (a, b) in enumerate(pairs)]
    for copy in copies:
        copy.start()
    return copies


def shape(kind, *sizes):
    return jax.ShapeDtypeStruct(sizes, kind)


def call(kernel, name, out_shape, operands, scratch=(), flops=0, in_place=False):
    places = {}
    if in_place:
        spec = pl.BlockSpec(memory_space=pl.ANY)
        places["in_specs"] = [spec] * len(operands) if in_place is True else in_place
    size = sum(x.size * x.dtype.itemsize for x in operands)
    return pl.pallas_call(
        kernel,
        out_shape=out_shape,
        scratch_shapes=list(scratch),
        compiler_params=pltpu.CompilerParams(vmem_limit_bytes=60 * 2**20),
        cost_estimate=pl.CostEstimate(flops=flops, bytes_accessed=size, transcendentals=0),
        name=name,
        **places,
    )(*operands)


class Job:
    def __init__(self, steps):
        self.steps = steps
        self.result = None
        self.open = True
        self.request = None
        self.held = False
        self.send(None)

    def send(self, value):
        try:
            self.request = self.steps.send(value)
        except StopIteration as stop:
            self.result, self.open, self.request = stop.value, False, None


class Net:
    def __init__(self):
        self.count = lax.axis_size("dp")
        self.teams = self.count // TEAM
        self.index = lax.axis_index("dp")
        self.place = self.index % TEAM
        self.team = self.index // TEAM
        self.core = self.index % 2
        self.peer = (self.index // 2) % 4
        self.jobs = []
        self.waiting = []
        self.gate = []
        self.extra = []

    def pairs(self, move):
        if move[0] == "swap":
            return [(i, i ^ move[1]) for i in range(self.count)]
        if move[0] == "ring":
            return [(i, (i + move[1] * TEAM) % self.count) for i in range(self.count)]
        if move[0] == "mixed":
            return [(i, i ^ (2 if i % 2 == 0 else 4)) for i in range(self.count)]
        return [(i, i - TEAM) for i in range(TEAM, self.count)]

    def do(self, call, *operands):
        def steps():
            (got,) = yield [(operands, ("call", call))]
            return got

        return self.spawn(steps())

    def spawn(self, steps):
        job = Job(steps)
        if job.open:
            self.jobs.append(job)
        return job

    def need(self, *values):
        self.extra.extend(values)

    def later(self, value):
        return lax.optimization_barrier((value, self.gate))[0]

    def step(self, times=1):
        for _ in range(times):
            self.one_step()

    def one_step(self):
        ready = [job for job in self.jobs if job.request is not None and not job.held]
        values = [move[0] for job in ready for move in job.request]
        self.raw = []
        if values or self.waiting:
            values, _ = lax.optimization_barrier((values, (self.gate, self.extra)))
            self.extra = []
            at = 0
            for job in ready:
                span = 1
                got = []
                moves = job.request
                for move in moves:
                    if len(move) > 2:
                        span = move[2]
                    if move[1][0] == "call":
                        got.append(move[1][1](*values[at]))
                    else:
                        got.append(lax.ppermute(values[at], "dp", self.pairs(move[1])))
                    at += 1
                job.request = None
                self.raw.extend(zip([move[1] for move in moves], got))
                self.waiting.append([span, job, got])
        for entry in self.waiting:
            entry[0] -= 1
        done = [entry for entry in self.waiting if entry[0] <= 0]
        self.waiting = [entry for entry in self.waiting if entry[0] > 0]
        results = lax.optimization_barrier([entry[2] for entry in done])
        self.gate = results
        for (_, job, _), got in zip(done, results):
            job.send(got)
        self.jobs = [job for job in self.jobs if job.open]

    def until(self, *jobs):
        while any(job.open for job in jobs):
            self.one_step()
        return [job.result for job in jobs] if len(jobs) > 1 else jobs[0].result


    def blocks(self, value):
        across, along, twin = yield [
            (value, ("swap", 2)),
            (value, ("swap", 4)),
            (value, ("swap", 1)),
        ]
        corner, across_twin, along_twin = yield [
            (jnp.where(self.core == 0, along, across), ("mixed",)),
            (across, ("swap", 1)),
            (along, ("swap", 1)),
        ]
        (corner_twin,) = yield [(corner, ("swap", 1))]
        return [value, twin, across, across_twin, along, along_twin, corner, corner_twin]

    def blocks_direct(self, value):
        found = yield [(value, ("swap", mask)) for mask in (2, 4, 6, 1)]
        twins = yield [(block, ("swap", 1)) for block in found[:3]]
        return [value, found[3], found[0], twins[0], found[1], twins[1], found[2], twins[2]]

    def team_sum(self, odd, fold, split=False, span=1):
        (arrived,) = yield [(odd, ("swap", 1))]
        call, operands = fold(arrived)
        (parts,) = yield [(operands, ("call", call))]
        sends = [(part, ("swap", mask), span) for part, mask in zip(parts[1:], (6, 2, 4))]
        if split:
            corner = yield sends[:1]
            return [parts[0]] + corner + (yield sends[1:])
        moved = yield sends
        return [parts[0]] + moved

    def exchange(self, blocks):
        groups = [[base + q for q in range(TEAM)] for base in range(0, self.count, TEAM)]
        return lax.all_to_all(blocks, "dp", 0, 0, axis_index_groups=groups, tiled=True)

    def line_both(self, value):
        teams = self.teams
        found, up, down = {0: value}, value, value
        for step in range(1, teams // 2 + 1):
            moves = [(up, ("ring", 1))]
            if step < teams - step:
                moves.append((down, ("ring", teams - 1)))
            got = yield moves
            found[step], up = got[0], got[0]
            if len(got) > 1:
                found[teams - step], down = got[1], got[1]
        return jnp.concatenate([found[k] for k in range(teams)], 0)

    def line_send(self, parts, span=1):
        return (yield [(part, ("ring", k + 1), span) for k, part in enumerate(parts)])

    def line_sum(self, shares):
        total = shares[-1].astype(NARROW)
        for share in reversed(shares[:-1]):
            (got,) = yield [(total, ("ring", 1))]
            total = share + got.astype(WIDE)
            total = total if share is shares[0] else total.astype(NARROW)
        return total


def scale_of(values):
    return lax.rsqrt(jnp.mean(values * values, axis=1, keepdims=True) + epsilon)


def norm_back(upstream, normed, scaler, gain):
    scaled = upstream * gain
    return scaler * (scaled - normed * jnp.mean(scaled * normed, axis=1, keepdims=True))


def where_am_i():
    index = lax.axis_index("dp")
    return index % TEAM, index // TEAM


def at(start, size, step=16):
    return pl.ds(pl.multiple_of(start, step), size)


def summed_parts(left, right, arrived, turned, name, relative=False):
    rows, width = arrived.shape[0] // 4, arrived.shape[1]
    deep = left.shape[1]
    contract = ((1,), (1,)) if turned else ((1,), (0,))

    def kernel(left_in, right_in, arrived_in, own, corner, across, along, left, right, arrived, sems):
        place, _ = where_am_i()
        copies = [(right_in, right), (arrived_in, arrived)]
        for k in range(4):
            source = left_in
            if relative:
                source = left_in.at[at((place ^ (2 * k)) * rows, rows), :]
            else:
                source = left_in.at[k * rows : (k + 1) * rows, :]
            copies.append((source, left.at[k * rows : (k + 1) * rows, :]))
        for copy in fetch(copies, sems):
            copy.wait()
        total = dot(left[...], right[...], contract) + arrived[...].astype(WIDE)
        for k, out in ((3, corner), (1, across), (2, along), (0, own)):
            out[...] = total[k * rows : (k + 1) * rows].astype(out.dtype)

    outs = (shape(WIDE, rows, width),) + (shape(NARROW, rows, width),) * 3
    return call(
        kernel,
        name,
        outs,
        (left, right, arrived),
        [
            pltpu.VMEM((4 * rows, deep), NARROW),
            pltpu.VMEM(right.shape, NARROW),
            pltpu.VMEM(arrived.shape, NARROW),
            pltpu.SemaphoreType.DMA((6,)),
        ],
        8 * rows * deep * width,
        in_place=True,
    )


def pieces(ffpart, even, own):
    runs = []
    for z in range(own // ffpart):
        for start, stop in ((0, even), (even, own)):
            low, high = max(z * ffpart, start), min((z + 1) * ffpart, stop)
            if low < high:
                at_gate = low if start == 0 else 2 * even + low - even
                at_up = even + low if start == 0 else own + low
                runs.append((z, low, high, at_gate, at_up))
    return runs


def in_prepare(weight, gains, marks, taps, teams):
    part, width = weight.shape
    features = width // 3
    channels = features // TEAM
    slots = max(128, TEAM * part) // part

    def kernel(weight, gain_one, gain_two, marks, taps, out, wide, small):
        index = lax.axis_index("dp")
        whole = weight[...].astype(WIDE)
        small[...] = jnp.zeros_like(small)
        for slot in range(slots):
            mine = lax.rem(index, slots) == slot
            for row, gain in enumerate((gain_one, gain_two)):
                value = gain[...].astype(WIDE)
                value = jnp.where(mine, value, jnp.zeros_like(value))
                small[row : row + 1, slot * part : (slot + 1) * part] = value
        small[0:1, 2 * channels :] = marks[...].astype(WIDE)
        for slot in range(teams):
            value = taps[...].astype(WIDE)
            value = jnp.where(index // TEAM == slot, value, jnp.zeros_like(value))
            for k in range(3):
                to = k * channels + slot * part
                small[2:3, to : to + part] = value[k : k + 1, :]
        for p in range(TEAM):
            for k in range(3):
                for z in range(teams):
                    source = k * features + (z * TEAM + p) * part
                    to = k * channels + z * part
                    wide[:, to : to + part] = whole[:, source : source + part]
            out[p, :part, :] = wide[...].astype(NARROW)
            out[p, part:, :] = small[...].astype(NARROW)

    return call(
        kernel,
        "in_prepare",
        shape(NARROW, TEAM, part + 8, 3 * channels),
        (weight, *gains, marks, taps),
        [pltpu.VMEM((part, 3 * channels), WIDE), pltpu.VMEM((8, 3 * channels), WIDE)],
    )


def in_finish(blocks, weight, gain, teams):
    part, width = weight.shape
    features = width // 3
    channels = features // TEAM

    def kernel(blocks, weight, gain, out, gain_grad):
        for p in range(TEAM):
            block = blocks[p].astype(WIDE)
            for k in range(3):
                for z in range(teams):
                    to = k * features + (z * TEAM + p) * part
                    source = k * channels + z * part
                    out[:, to : to + part] = block[:, source : source + part]
        product = jnp.sum(weight[...].astype(WIDE) * out[...], axis=1, keepdims=True)
        gain_grad[...] = (product / gain[...].astype(WIDE)).reshape(1, part)

    outs = (shape(WIDE, part, width), shape(WIDE, 1, part))
    return call(kernel, "in_finish", outs, (blocks, weight, gain))


def pair_prepare(gate, up, teams):
    part, inner = gate.shape
    own = inner // TEAM
    ffpart = own // teams
    even = own // 128 * 128
    runs = pieces(ffpart, even, own)

    def kernel(gate, up, out, wide):
        gates, ups = gate[...].astype(WIDE), up[...].astype(WIDE)
        for p in range(TEAM):
            for z, low, high, at_gate, at_up in runs:
                source = (z * TEAM + p) * ffpart + low - z * ffpart
                size = high - low
                wide[:, at_gate : at_gate + size] = gates[:, source : source + size]
                wide[:, at_up : at_up + size] = ups[:, source : source + size]
            out[p] = wide[...].astype(NARROW)

    out = shape(NARROW, TEAM, part, 2 * own)
    scratch = [pltpu.VMEM((part, 2 * own), WIDE)]
    return call(kernel, "pair_prepare", out, (gate, up), scratch)


def pair_finish(blocks, gate, up, gain, teams):
    part, inner = gate.shape
    own = inner // TEAM
    ffpart = own // teams
    even = own // 128 * 128
    runs = pieces(ffpart, even, own)

    def kernel(blocks, gate, up, gain, gate_grad, up_grad, gain_grad):
        for p in range(TEAM):
            block = blocks[p].astype(WIDE)
            for z, low, high, at_gate, at_up in runs:
                to = (z * TEAM + p) * ffpart + low - z * ffpart
                size = high - low
                gate_grad[:, to : to + size] = block[:, at_gate : at_gate + size]
                up_grad[:, to : to + size] = block[:, at_up : at_up + size]
        product = gate[...].astype(WIDE) * gate_grad[...] + up[...].astype(WIDE) * up_grad[...]
        total = jnp.sum(product, axis=1, keepdims=True) / gain[...].astype(WIDE)
        gain_grad[...] = total.reshape(1, part)

    outs = (shape(WIDE, part, inner), shape(WIDE, part, inner), shape(WIDE, 1, part))
    return call(kernel, "pair_finish", outs, (blocks, gate, up, gain))


def mixer_forward(blocks, before, weights):
    rows, features = blocks[0].shape
    tokens = TEAM * rows
    count, _, channels = weights.shape
    channels = channels // 3
    teams = count // TEAM
    share, part = features // teams, features // count

    def kernel(*refs):
        blocks, (before, weights), refs = refs[:TEAM], refs[TEAM : TEAM + 2], refs[TEAM + 2 :]
        normed, mixed, gated, conv, mixer_in, in_own, gain, gain_two, taps, keeps = refs[:10]
        hs, small, sems = refs[10:]
        place, team = where_am_i()
        copies = [(weights.at[:, part:, :], small)]
        for d in range(count):
            to = in_own.at[d * part : (d + 1) * part, :]
            copies.append((weights.at[d, :part, :], to))
        for m in range(TEAM):
            copies.append((blocks[m], hs.at[at(HALO + (place ^ m) * rows, rows), :]))
        copies.append((before, hs.at[:HALO, :]))
        for copy in fetch(copies, sems):
            copy.wait()
        first = hs[:HALO, :]
        hs[:HALO, :] = jnp.where(team > 0, first, jnp.zeros_like(first))
        total = jnp.zeros((1, 3 * channels), WIDE)
        gain[...] = jnp.zeros_like(gain)
        gain_two[...] = jnp.zeros_like(gain_two)
        span = max(share, 128)
        for z in range(teams):
            both = sum(small[z * TEAM + p].astype(WIDE) for p in range(TEAM))
            one, two = both[0:1], both[1:2]
            total = total + small[z * TEAM + place].astype(WIDE)[2:3]
            to = slice(z * share // span * span, z * share // span * span + span)
            gain[:, to] = gain[:, to] + one[:, :span]
            gain_two[:, to] = gain_two[:, to] + two[:, :span]
        taps[...] = jnp.zeros_like(taps)
        for k in range(3):
            taps[k : k + 1, :] = total[:, k * channels : (k + 1) * channels]
        marks = [
            1.0 - small[team * TEAM + p].astype(WIDE)[0:1, 2 * channels :] for p in range(TEAM)
        ]
        keep = jnp.concatenate([mark.reshape(rows, 1) for mark in marks], 0)
        keeps[8:, 0:1] = keep
        before_team = lax.rem(team + teams - 1, teams) * TEAM + TEAM - 1
        last = 1.0 - small[before_team].astype(WIDE)[0:1, 3 * channels - 1 :]
        keeps[7:8, 0:1] = last
        keeps[8:, 1:2] = keep * keeps[7 : 7 + tokens, 0:1]
        scale = gain[...]

        def norm(start, size):
            values = hs[at(start, size), :].astype(WIDE)
            values = values * scale_of(values) * scale
            normed[at(start, size), :] = values.astype(NARROW)

        norm(0, HALO)

        @pl.loop(0, TEAM)
        def _(step):
            norm(HALO + step * rows, rows)

        mixed[...] = dot(normed[...], in_own[...], ((1,), (0,)))
        gated[...] = (mixed[:, :channels] * mixed[:, 2 * channels :]).astype(NARROW).astype(WIDE)
        conv_out = (
            taps[2:3, :] * gated[HALO:, :]
            + taps[1:2, :] * (keeps[8:, 0:1] * gated[HALO - 1 : HALO - 1 + tokens, :])
            + taps[0:1, :] * (keeps[8:, 1:2] * gated[HALO - 2 : HALO - 2 + tokens, :])
        )
        conv[...] = conv_out
        mixer_in[...] = (mixed[HALO:, channels : 2 * channels] * conv_out).astype(NARROW)

    outs = (
        shape(NARROW, HALO + tokens, features),
        shape(WIDE, HALO + tokens, 3 * channels),
        shape(WIDE, HALO + tokens, channels),
        shape(WIDE, tokens, channels),
        shape(NARROW, tokens, channels),
        shape(NARROW, features, 3 * channels),
        shape(WIDE, 1, features),
        shape(WIDE, 1, features),
        shape(WIDE, 8, channels),
        shape(WIDE, 8 + tokens, 2),
    )
    return call(
        kernel,
        "mixer_forward",
        outs,
        (*blocks, before, weights),
        [
            pltpu.VMEM((HALO + tokens, features), NARROW),
            pltpu.VMEM((count, 8, 3 * channels), NARROW),
            pltpu.SemaphoreType.DMA((count + TEAM + 2,)),
        ],
        2 * tokens * features * 3 * channels,
        in_place=True,
    )


def out_rows(blocks, whole, teams):
    place, team = where_am_i()
    channels = blocks[0].shape[0]
    share = channels // teams
    copies = []
    for m, block in enumerate(blocks):
        for k in range(teams):
            to = (place ^ m) * channels + lax.rem(team - k + teams, teams) * share
            copies.append((block.at[k * share : (k + 1) * share, :], whole.at[at(to, share, 8), :]))
    return copies


def out_project(mixer_blocks, out_blocks, hidden_blocks, gain, teams):
    rows, features = hidden_blocks[0].shape
    tokens, channels = mixer_blocks[0].shape

    def kernel(*refs):
        mixer_in, out_in, hidden_in = [refs[k * TEAM : (k + 1) * TEAM] for k in range(3)]
        gain, resid, odd, even, mixer, turned, out, hidden, sems = refs[3 * TEAM :]
        place, _ = where_am_i()
        copies = out_rows(out_in, out, teams)
        for m in range(TEAM):
            to = mixer.at[:, at((place ^ m) * channels, channels, 128)]
            copies.append((mixer_in[m], to))
        first = len(copies)
        copies += [(hidden_in[m], hidden.at[m]) for m in range(TEAM)]
        copies = fetch(copies, sems)
        for copy in copies[:first]:
            copy.wait()
        for half, side in ((1, odd), (0, even)):
            for k in range(TEAM // 2):
                source = mixer[at((place ^ (2 * k + half)) * rows, rows), :]
                turned[k * rows : (k + 1) * rows, :] = source
            product = dot(turned[...], out[...], ((1,), (0,)))
            if half == 1:
                for copy in copies[first:]:
                    copy.wait()
            for k in range(TEAM // 2):
                span = slice(k * rows, (k + 1) * rows)
                total = hidden[2 * k + half].astype(WIDE) + product[span]
                side[span, :] = (total * scale_of(total) * gain[...]).astype(NARROW)
                if k + half == 0:
                    resid[...] = total

    outs = (shape(WIDE, rows, features),) + (shape(NARROW, tokens // 2, features),) * 2
    any_place, in_vmem = pl.BlockSpec(memory_space=pl.ANY), pl.BlockSpec(memory_space=pltpu.VMEM)
    return call(
        kernel,
        "out_project",
        outs,
        (*mixer_blocks, *out_blocks, *hidden_blocks, gain),
        [
            pltpu.VMEM((tokens, features), NARROW),
            pltpu.VMEM((tokens // 2, features), NARROW),
            pltpu.VMEM((features, features), NARROW),
            pltpu.VMEM((TEAM, rows, features), NARROW),
            pltpu.SemaphoreType.DMA((TEAM * teams + 2 * TEAM,)),
        ],
        2 * tokens * features * features,
        in_place=[any_place] * (3 * TEAM) + [in_vmem],
    )


def ffn_parts(gate, up, grad):
    sigmoid = 1.0 / (1.0 + jnp.exp(-gate))
    scaled = gate * sigmoid
    gate_grad = grad * up * sigmoid * (1.0 + gate * (1.0 - sigmoid))
    return scaled * up, gate_grad, grad * scaled


def ffn_block(odd, even, upstream, pair, down):
    count = len(upstream)
    rows, features = upstream[0].shape
    own = down.shape[0]
    units = own // 128 * 128
    width = own - units
    half = odd.shape[0]

    def kernel(odd_in, even_in, *refs):
        g_in, (pair_in, down_in), refs = refs[:count], refs[count : count + 2], refs[count + 2 :]
        acts, grads, weight, back = refs[:2], refs[2:4], refs[4], refs[5]
        xs, gs, pair, down, last, all_grads, sems = refs[6:]
        first = [(odd_in, xs.at[:half, :]), (pair_in, pair)]
        second = [(g_in[k], gs.at[k * rows : (k + 1) * rows, :]) for k in range(count)]
        second += [(down_in, down), (even_in, xs.at[half:, :])]
        copies = fetch(first + second, sems)
        for copy in copies[:2]:
            copy.wait()
        for side in range(2):
            span = slice(side * half, (side + 1) * half)
            act, grad_out = acts[side], grads[side]
            x = xs[span, :]
            gate = dot(x, pair[:, :units], ((1,), (0,)))
            up = dot(x, pair[:, units : 2 * units], ((1,), (0,)))
            if side == 0:
                for copy in copies[2:]:
                    copy.wait()
                last[:width, :] = down[units:, :]
                last[width:, :] = down[units:, :]
            g = gs[span, :]
            grad = dot(g, down[:units, :], ((1,), (1,)))
            value, gate_grad, up_grad = ffn_parts(gate, up, grad)
            act[:, :units] = value.astype(NARROW)
            all_grads[span, :units] = gate_grad.astype(NARROW)
            all_grads[span, units : 2 * units] = up_grad.astype(NARROW)
            both = dot(x, pair[:, 2 * units :], ((1,), (0,)))
            turned = pltpu.roll(both, width, 1)
            lower = lax.broadcasted_iota(jnp.int32, both.shape, 1) < width
            grad = dot(g, last[...], ((1,), (1,)))
            value, gate_grad, up_grad = ffn_parts(
                jnp.where(lower, both, turned), jnp.where(lower, turned, both), grad
            )
            act[:, units:] = value[:, :width].astype(NARROW)
            all_grads[span, 2 * units :] = jnp.where(lower, gate_grad, up_grad).astype(NARROW)
            grad_out[...] = all_grads[span, :]
        back[...] = dot(all_grads[:half, :], pair[...], ((1,), (1,))).astype(NARROW)
        for start in range(0, features, 256):
            total = dot(xs[:, start : start + 256], all_grads[...], ((0,), (0,)))
            weight[start : start + 256, :] = total.astype(NARROW)

    outs = (shape(NARROW, half, own),) * 2 + (shape(NARROW, half, 2 * own),) * 2
    return call(
        kernel,
        "ffn",
        outs + (shape(NARROW, features, 2 * own), shape(NARROW, half, features)),
        (odd, even, *upstream, pair, down),
        [
            pltpu.VMEM((2 * half, features), NARROW),
            pltpu.VMEM((2 * half, features), NARROW),
            pltpu.VMEM((features, 2 * own), NARROW),
            pltpu.VMEM((own, features), NARROW),
            pltpu.VMEM((2 * width, features), NARROW),
            pltpu.VMEM((2 * half, 2 * own), NARROW),
            pltpu.SemaphoreType.DMA((count + 4,)),
        ],
        20 * half * features * own,
        in_place=True,
    )


def product(left, right, turned, name):
    contract = ((1,), (1,)) if turned else ((1,), (0,))

    def kernel(left, right, out):
        out[...] = dot(left[...], right[...], contract).astype(NARROW)

    rows, wide = left.shape[0], right.shape[0 if turned else 1]
    return call(kernel, name, shape(NARROW, rows, wide), (left, right), flops=2 * rows * right.size)


def weight_grads(lefts, rights, name):
    deep, wide = lefts[0].shape[1], rights[0].shape[1]
    tokens = sum(left.shape[0] for left in lefts)

    def kernel(*refs):
        ins, (out, left, right, sems) = refs[: len(lefts) + len(rights)], refs[-4:]
        pairs = []
        for blocks, whole in ((ins[: len(lefts)], left), (ins[len(lefts) :], right)):
            row = 0
            for block in blocks:
                pairs.append((block, whole.at[row : row + block.shape[0], :]))
                row += block.shape[0]
        for copy in fetch(pairs, sems):
            copy.wait()
        for start in range(0, deep, 256):
            stop = min(start + 256, deep)
            total = dot(left[:, start:stop], right[...], ((0,), (0,)))
            out[start:stop, :] = total.astype(NARROW)

    return call(
        kernel,
        name,
        shape(NARROW, deep, wide),
        (*lefts, *rights),
        [
            pltpu.VMEM((tokens, deep), NARROW),
            pltpu.VMEM((tokens, wide), NARROW),
            pltpu.SemaphoreType.DMA((len(lefts) + len(rights),)),
        ],
        2 * tokens * deep * wide,
        in_place=True,
    )


def resid_back(parts, resid, gain, upstream, out_blocks, teams):
    rows, features = resid.shape
    channels = features // TEAM

    def kernel(own, corner, across, along, resid, gain, upstream, *refs):
        out_in, (resid_grad, rounded, mixer_grad, out, sems) = refs[:TEAM], refs[TEAM:]
        copies = fetch(out_rows(out_in, out, teams), sems)
        grad = own[...] + sum(part[...].astype(WIDE) for part in (corner, across, along))
        values = resid[...]
        scale = scale_of(values)
        grad = upstream[...].astype(WIDE) + norm_back(grad, values * scale, scale, gain[...])
        resid_grad[...] = grad
        rounded[...] = grad.astype(NARROW)
        for copy in copies:
            copy.wait()
        product = dot(rounded[...], out[...], ((1,), (1,))).astype(NARROW)
        for p in range(TEAM):
            mixer_grad[p] = product[:, p * channels : (p + 1) * channels]

    outs = (
        shape(WIDE, rows, features),
        shape(NARROW, rows, features),
        shape(NARROW, TEAM, rows, channels),
    )
    any_place, in_vmem = pl.BlockSpec(memory_space=pl.ANY), pl.BlockSpec(memory_space=pltpu.VMEM)
    return call(
        kernel,
        "resid_back",
        outs,
        (*parts, resid, gain, upstream, *out_blocks),
        [
            pltpu.VMEM((features, features), NARROW),
            pltpu.SemaphoreType.DMA((TEAM * teams,)),
        ],
        2 * rows * features * features,
        in_place=[in_vmem] * 7 + [any_place] * TEAM,
    )


def conv_back(mixer_grad, mixed, gated, conv, taps, keeps):
    tokens, channels = conv.shape

    def kernel(mixer_grad, mixed, gated, conv, taps, keeps, part, rim, taps_grad, ones, twos):
        grad = mixer_grad[...].astype(WIDE)
        conv_grad = grad * mixed[HALO:, channels : 2 * channels]
        one, two = keeps[8:, 0:1] * conv_grad, keeps[8:, 1:2] * conv_grad
        zeros = jnp.zeros((8, channels), WIDE)
        taps_grad[...] = zeros
        for k, (left, back) in enumerate(((two, 2), (one, 1), (conv_grad, 0))):
            product = left * gated[HALO - back : HALO - back + tokens, :]
            taps_grad[k : k + 1, :] = jnp.sum(product, axis=0, keepdims=True)
        ones[:tokens, :] = taps[1:2, :] * one
        twos[:tokens, :] = taps[0:1, :] * two
        ones[tokens:, :] = zeros
        twos[tokens:, :] = zeros
        rim[...] = zeros
        rim[6:7, :] = twos[0:1, :]
        rim[7:8, :] = twos[1:2, :] + ones[0:1, :]
        part[...] = taps[2:3, :] * conv_grad + ones[1 : tokens + 1, :] + twos[2 : tokens + 2, :]

    outs = (shape(WIDE, tokens, channels), shape(WIDE, 8, channels), shape(WIDE, 8, channels))
    scratch = [pltpu.VMEM((tokens + 8, channels), WIDE)] * 2
    return call(
        kernel, "conv_back", outs, (mixer_grad, mixed, gated, conv, taps, keeps), scratch
    )


def mixer_back(part, returned, mixer_grad, mixed, conv, normed, in_own, teams):
    tokens, channels = conv.shape
    features = in_own.shape[0]
    rows, share = tokens // TEAM, features // teams

    def kernel(*refs):
        part, returned, mixer_grad, mixed, conv, normed, in_own, grads, odd = refs[:9]
        shares, (side, whole, weight) = refs[9 : 9 + teams], refs[9 + teams :]
        place, team = where_am_i()
        whole[...] = part[...]
        whole[tokens - 8 :, :] = part[tokens - 8 :, :] + returned[...]
        gated_grad = whole[...]
        grads[:, :channels] = (gated_grad * mixed[HALO:, 2 * channels :]).astype(NARROW)
        grads[:, channels : 2 * channels] = (
            mixer_grad[...].astype(WIDE) * conv[...]
        ).astype(NARROW)
        grads[:, 2 * channels :] = (gated_grad * mixed[HALO:, :channels]).astype(NARROW)
        for chip in range(TEAM // 2):
            at_place = place ^ (2 * chip + 1)
            side[chip * rows : (chip + 1) * rows, :] = grads[at(at_place * rows, rows), :]
        step = features // 4
        for start in range(0, features, step):
            span = slice(start, start + step)
            weight[span, :] = dot(normed[HALO:, span], grads[...], ((0,), (0,)))
        for k in range(teams):
            owner = lax.rem(team + k, teams)
            shares[k][...] = weight[at(owner * share, share), :].astype(shares[k].dtype)
        odd[...] = dot(side[...], in_own[...], ((1,), (1,))).astype(NARROW)

    outs = (shape(NARROW, tokens, 3 * channels), shape(NARROW, tokens // 2, features))
    outs += tuple(
        shape(NARROW if k == teams - 1 else WIDE, share, 3 * channels) for k in range(teams)
    )
    grads, odd, *shares = call(
        kernel,
        "mixer_back",
        outs,
        (part, returned, mixer_grad, mixed, conv, normed, in_own),
        [
            pltpu.VMEM((tokens // 2, 3 * channels), NARROW),
            pltpu.VMEM((tokens, channels), WIDE),
            pltpu.VMEM((features, 3 * channels), WIDE),
        ],
        3 * tokens * features * 3 * channels,
    )
    return grads, odd, shares


def out_back(mixer_in, blocks, taps_grad, teams):
    rows, features = blocks[0].shape
    channels = mixer_in.shape[1]
    share = channels // teams
    low = (share + 15) // 16 * 16

    def kernel(*refs):
        mixer_in, blocks, taps_grad = refs[0], refs[1 : 1 + TEAM], refs[1 + TEAM]
        shares, (total,) = refs[2 + TEAM : 2 + TEAM + teams], refs[2 + TEAM + teams :]
        place, team = where_am_i()
        total[...] = sum(
            dot(mixer_in[at((place ^ m) * rows, rows), :], blocks[m][...], ((0,), (0,)))
            for m in range(TEAM)
        )
        for k in range(teams):
            owner = lax.rem(team + k, teams)
            kind = shares[k].dtype
            shares[k][...] = jnp.zeros_like(shares[k])
            shares[k][:share, :] = total[at(owner * share, share, 8), :].astype(kind)
            shares[k][low : low + 8, :channels] = taps_grad[...].astype(kind)

    outs = tuple(
        shape(NARROW if k == teams - 1 else WIDE, low + 16, features) for k in range(teams)
    )
    return call(
        kernel,
        "out_back",
        outs,
        (mixer_in, *blocks, taps_grad),
        [pltpu.VMEM((channels, features), WIDE)],
        2 * TEAM * rows * channels * features,
    ), low


def body(
    hidden_in,
    seq_start,
    mixer_gain,
    in_weight,
    conv_weight,
    out_weight,
    ffn_gain,
    gate_weight,
    up_weight,
    down_weight,
    cotangent,
):
    net = Net()
    teams = net.teams
    rows, features = hidden_in.shape
    inner = gate_weight.shape[2]
    part = features // net.count
    ffpart = inner // net.count
    channels = features // TEAM
    ffown = inner // TEAM
    line = [[p + TEAM * z for z in range(teams)] for p in range(TEAM)]


    def gather(value):
        return lax.all_gather(value, "dp", axis=0, tiled=True, axis_index_groups=line)

    def reduce(value):
        return lax.psum_scatter(
            value, "dp", scatter_dimension=0, tiled=True, axis_index_groups=line
        )

    down_own = gather(down_weight[0])
    hidden_job = net.spawn(net.blocks_direct(hidden_in))
    sent = in_prepare(
        in_weight[0],
        (mixer_gain, ffn_gain),
        seq_start.reshape(1, rows),
        conv_weight[0].T,
        teams,
    )
    net.need(sent)
    got_job = net.do(net.exchange, sent)
    pair_job = net.do(lambda *x: pair_prepare(*x, teams), gate_weight[0], up_weight[0])
    net.step()
    out_job = net.spawn(net.line_both(out_weight[0]))
    pair_job = net.do(net.exchange, pair_job.result)
    in_job = net.do(gather, got_job.result.reshape(TEAM * (part + 8), 3 * channels))
    net.until(pair_job, in_job, hidden_job)
    pair_own = gather(pair_job.result.reshape(TEAM * part, 2 * ffown))
    upstream_job = net.spawn(net.blocks(cotangent))

    def last_rows():
        last = hidden_job.result[0][-HALO:]
        for m in range(1, TEAM):
            block = hidden_job.result[m][-HALO:]
            last = jnp.where(net.place == (TEAM - 1) ^ m, block, last)
        (before,) = yield [(last, ("ring", 1))]
        return before

    halo_job = net.spawn(last_rows())
    before, out_rows_here = net.until(halo_job, out_job)
    upstream_job.held = True
    weights = in_job.result.reshape(net.count, part + 8, 3 * channels)
    out_job = net.spawn(net.blocks(out_rows_here))

    mix_job = net.do(
        lambda *x: mixer_forward(x[:TEAM], x[TEAM], x[TEAM + 1]),
        *hidden_job.result, before, weights,
    )
    (normed, mixed, gated, conv, mixer_in, in_own, gain_one, gain_two, taps, keeps) = net.until(
        mix_job
    )
    mixer_job = net.spawn(net.blocks(mixer_in))
    mixer_blocks, out_blocks = net.until(mixer_job, out_job)
    upstream_job.held = False
    project_job = net.do(
        lambda *x: out_project(
            x[:TEAM], x[TEAM : 2 * TEAM], x[2 * TEAM : 3 * TEAM], x[3 * TEAM], teams
        ),
        *mixer_blocks, *out_blocks, *hidden_job.result, gain_two,
    )
    resid, in_odd, in_even = net.until(project_job)
    upstream = net.until(upstream_job)

    ffn_job = net.do(
        lambda *x: ffn_block(x[0], x[1], x[2 : 2 + TEAM], x[2 + TEAM], x[3 + TEAM]),
        in_odd, in_even, *upstream[1::2], *upstream[0::2], pair_own, down_own,
    )
    act_odd, act_even, _, grads_even, pair_all, back_odd = net.until(ffn_job)
    pair_sum = reduce(pair_all)
    ffn_job = net.spawn(
        net.team_sum(
            back_odd,
            lambda arrived: (
                lambda *x: summed_parts(*x, True, "ffn_back"),
                (grads_even, pair_own, arrived),
            ),
        )
    )
    odd_job = net.do(lambda *x: product(*x, False, "ffn_output"), act_odd, down_own)
    net.step()
    output_job = net.spawn(
        net.team_sum(
            odd_job.result,
            lambda arrived: (
                lambda *x: summed_parts(*x, False, "ffn_output_sum"),
                (act_even, down_own, arrived),
            ),
            True,
        )
    )
    net.step()
    down_job = net.do(
        lambda *x: weight_grads(x[:2], x[2:], "down_grads"),
        act_odd, act_even, *upstream[1::2], *upstream[0::2],
    )
    ffn_grad = net.until(ffn_job)
    down_sum = reduce(down_job.result)

    output_job.held = True
    back_job = net.do(
        lambda *x: resid_back(x[:4], *x[4:7], x[7:], teams),
        *ffn_grad, resid, gain_two, cotangent, *out_blocks,
    )
    resid_grad, rounded, mixer_grad = net.until(back_job)
    output_job.held = True
    rounded_job = net.spawn(net.blocks(rounded))
    mixer_grad = net.until(net.do(net.exchange, mixer_grad)).reshape(TEAM * rows, channels)
    rounded_job.held = True
    gated_part, rim, taps_grad = net.until(
        net.do(conv_back, mixer_grad, mixed, gated, conv, taps, keeps)
    )
    rounded_job.held = False
    output_job.held = False

    def rim_steps():
        (returned,) = yield [(rim, ("back",))]
        return returned

    returned = net.until(net.spawn(rim_steps()))
    output_job.held = True
    mixed_grad, normed_odd, shares = net.until(
        net.do(
            lambda *x: mixer_back(*x, teams),
            gated_part, returned, mixer_grad, mixed, conv, normed, in_own,
        )
    )
    in_job = net.spawn(net.line_sum(shares))
    pair_job = net.do(net.exchange, pair_sum.reshape(TEAM, part, 2 * ffown))
    normed_job = net.spawn(
        net.team_sum(
            normed_odd,
            lambda arrived: (
                lambda *x: summed_parts(*x, True, "mixer_back_sum", True),
                (mixed_grad, in_own, arrived),
            ),
            span=2,
        )
    )
    low = (part + 15) // 16 * 16
    out_job = net.do(
        lambda *x: out_back(x[0], x[1 : 1 + TEAM], x[1 + TEAM], teams)[0],
        mixer_in, *net.until(rounded_job), taps_grad,
    )
    net.until(out_job)
    output_job.held = False
    net.need(down_sum)
    out_job = net.spawn(net.line_sum(out_job.result))
    in_grad = net.until(in_job).astype(NARROW)
    in_job = net.do(net.exchange, in_grad.reshape(TEAM, part, 3 * channels))
    finish_job = net.do(
        lambda *x: pair_finish(*x, teams),
        net.until(pair_job), gate_weight[0], up_weight[0], ffn_gain.reshape(part, 1),
    )
    in_grad = net.until(in_job)
    grad_gate, grad_up, grad_ffn_gain = net.until(finish_job)
    normed_grad, ffn_out, out_pack = net.until(normed_job, output_job, out_job)
    in_grad, grad_mixer_gain = in_finish(
        in_grad, in_weight[0], mixer_gain.reshape(part, 1), teams
    )

    def total(parts):
        return sum([part.astype(WIDE) for part in parts[1:]], parts[0])

    own_hidden = hidden_in.astype(WIDE)
    scale_one = scale_of(own_hidden)
    grad_hidden = resid_grad + norm_back(
        total(normed_grad), own_hidden * scale_one, scale_one, gain_one
    )
    hidden_out = (resid + total(ffn_out)).astype(NARROW)
    grad_out = out_pack[:part]
    grad_conv = lax.dynamic_slice(out_pack, (low, net.team * part), (3, part)).T
    return (
        hidden_out,
        grad_hidden,
        grad_mixer_gain,
        in_grad[None],
        grad_conv[None],
        grad_out[None],
        grad_ffn_gain,
        grad_gate[None],
        grad_up[None],
        down_sum.astype(WIDE)[None],
    )


def solution(mesh):
    tokens, wide, deep = P("dp", None), P(None, "dp"), P(None, "dp", None)
    return jax.shard_map(
        body,
        mesh=mesh,
        in_specs=(tokens, P("dp"), wide, deep, deep, deep, wide, deep, deep, deep, tokens),
        out_specs=(tokens, tokens, wide, deep, deep, deep, wide, deep, deep, deep),
        check_vma=False,
    )
```

```python
import jax
import jax.numpy as jnp
from jax import lax
from jax.experimental import pallas as pl
from jax.experimental.pallas import tpu as pltpu
from jax.sharding import PartitionSpec as P

epsilon = 1e-05
TEAM = 8
HALO = 16
WIDE = jnp.float32
NARROW = jnp.bfloat16


def dot(left, right, contract):
    return lax.dot_general(left, right, (contract, ((), ())), preferred_element_type=WIDE)


def fetch(pairs, sems):
    copies = [pltpu.make_async_copy(a, b, sems.at[i]) for i, (a, b) in enumerate(pairs)]
    for copy in copies:
        copy.start()
    return copies


def shape(kind, *sizes):
    return jax.ShapeDtypeStruct(sizes, kind)


def call(kernel, name, out_shape, operands, scratch=(), flops=0, in_place=False):
    places = {}
    if in_place:
        spec = pl.BlockSpec(memory_space=pl.ANY)
        places["in_specs"] = [spec] * len(operands) if in_place is True else in_place
    size = sum(x.size * x.dtype.itemsize for x in operands)
    return pl.pallas_call(
        kernel,
        out_shape=out_shape,
        scratch_shapes=list(scratch),
        compiler_params=pltpu.CompilerParams(vmem_limit_bytes=56 * 2**20),
        cost_estimate=pl.CostEstimate(flops=flops, bytes_accessed=size, transcendentals=0),
        name=name,
        **places,
    )(*operands)


class Job:
    def __init__(self, steps):
        self.steps = steps
        self.result = None
        self.open = True
        self.request = None
        self.held = False
        self.send(None)

    def send(self, value):
        try:
            self.request = self.steps.send(value)
        except StopIteration as stop:
            self.result, self.open, self.request = stop.value, False, None


class Net:
    def __init__(self):
        self.count = lax.axis_size("dp")
        self.teams = self.count // TEAM
        self.index = lax.axis_index("dp")
        self.place = self.index % TEAM
        self.team = self.index // TEAM
        self.core = self.index % 2
        self.peer = (self.index // 2) % 4
        self.jobs = []
        self.waiting = []
        self.gate = []
        self.extra = []

    def pairs(self, move):
        if move[0] == "swap":
            return [(i, i ^ move[1]) for i in range(self.count)]
        if move[0] == "ring":
            return [(i, (i + move[1] * TEAM) % self.count) for i in range(self.count)]
        if move[0] == "mixed":
            return [(i, i ^ (2 if i % 2 == 0 else 4)) for i in range(self.count)]
        return [(i, i - TEAM) for i in range(TEAM, self.count)]

    def do(self, call, *operands):
        def steps():
            (got,) = yield [(operands, ("call", call))]
            return got

        return self.spawn(steps())

    def spawn(self, steps):
        job = Job(steps)
        if job.open:
            self.jobs.append(job)
        return job

    def need(self, *values):
        self.extra.extend(values)

    def later(self, value):
        return lax.optimization_barrier((value, self.gate))[0]

    def step(self, times=1):
        for _ in range(times):
            self.one_step()

    def one_step(self):
        ready = [job for job in self.jobs if job.request is not None and not job.held]
        values = [move[0] for job in ready for move in job.request]
        self.raw = []
        if values or self.waiting:
            values, _ = lax.optimization_barrier((values, (self.gate, self.extra)))
            self.extra = []
            at = 0
            for job in ready:
                span = 1
                got = []
                moves = job.request
                for move in moves:
                    if len(move) > 2:
                        span = move[2]
                    if move[1][0] == "call":
                        got.append(move[1][1](*values[at]))
                    else:
                        got.append(lax.ppermute(values[at], "dp", self.pairs(move[1])))
                    at += 1
                job.request = None
                self.raw.extend(zip([move[1] for move in moves], got))
                self.waiting.append([span, job, got])
        for entry in self.waiting:
            entry[0] -= 1
        done = [entry for entry in self.waiting if entry[0] <= 0]
        self.waiting = [entry for entry in self.waiting if entry[0] > 0]
        results = lax.optimization_barrier([entry[2] for entry in done])
        self.gate = results
        for (_, job, _), got in zip(done, results):
            job.send(got)
        self.jobs = [job for job in self.jobs if job.open]

    def until(self, *jobs):
        while any(job.open for job in jobs):
            self.one_step()
        return [job.result for job in jobs] if len(jobs) > 1 else jobs[0].result


    def blocks(self, value):
        across, along, twin = yield [
            (value, ("swap", 2)),
            (value, ("swap", 4)),
            (value, ("swap", 1)),
        ]
        corner, across_twin, along_twin = yield [
            (jnp.where(self.core == 0, along, across), ("mixed",)),
            (across, ("swap", 1)),
            (along, ("swap", 1)),
        ]
        (corner_twin,) = yield [(corner, ("swap", 1))]
        return [value, twin, across, across_twin, along, along_twin, corner, corner_twin]

    def blocks_direct(self, value):
        found = yield [(value, ("swap", mask)) for mask in (2, 4, 6, 1)]
        twins = yield [(block, ("swap", 1)) for block in found[:3]]
        return [value, found[3], found[0], twins[0], found[1], twins[1], found[2], twins[2]]

    def team_sum(self, odd, fold, split=False, span=1):
        (arrived,) = yield [(odd, ("swap", 1))]
        call, operands = fold(arrived)
        (parts,) = yield [(operands, ("call", call))]
        sends = [(part, ("swap", mask), span) for part, mask in zip(parts[1:], (6, 2, 4))]
        if split:
            corner = yield sends[:1]
            return [parts[0]] + corner + (yield sends[1:])
        moved = yield sends
        return [parts[0]] + moved

    def exchange(self, blocks):
        groups = [[base + q for q in range(TEAM)] for base in range(0, self.count, TEAM)]
        return lax.all_to_all(blocks, "dp", 0, 0, axis_index_groups=groups, tiled=True)

    def line_both(self, value):
        teams = self.teams
        found, up, down = {0: value}, value, value
        for step in range(1, teams // 2 + 1):
            moves = [(up, ("ring", 1))]
            if step < teams - step:
                moves.append((down, ("ring", teams - 1)))
            got = yield moves
            found[step], up = got[0], got[0]
            if len(got) > 1:
                found[teams - step], down = got[1], got[1]
        return jnp.concatenate([found[k] for k in range(teams)], 0)

    def line_send(self, parts, span=1):
        return (yield [(part, ("ring", k + 1), span) for k, part in enumerate(parts)])

    def line_sum(self, shares):
        total = shares[-1].astype(NARROW)
        for share in reversed(shares[:-1]):
            (got,) = yield [(total, ("ring", 1))]
            total = share + got.astype(WIDE)
            total = total if share is shares[0] else total.astype(NARROW)
        return total


def scale_of(values):
    return lax.rsqrt(jnp.mean(values * values, axis=1, keepdims=True) + epsilon)


def norm_back(upstream, normed, scaler, gain):
    scaled = upstream * gain
    return scaler * (scaled - normed * jnp.mean(scaled * normed, axis=1, keepdims=True))


def where_am_i():
    index = lax.axis_index("dp")
    return index % TEAM, index // TEAM


def at(start, size, step=16):
    return pl.ds(pl.multiple_of(start, step), size)


def summed_parts(left, right, arrived, turned, name, relative=False):
    rows, width = arrived.shape[0] // 4, arrived.shape[1]
    deep = left.shape[1]
    contract = ((1,), (1,)) if turned else ((1,), (0,))

    def kernel(left_in, right_in, arrived_in, own, corner, across, along, left, right, arrived, sems):
        place, _ = where_am_i()
        copies = [(right_in, right), (arrived_in, arrived)]
        for k in range(4):
            source = left_in
            if relative:
                source = left_in.at[at((place ^ (2 * k)) * rows, rows), :]
            else:
                source = left_in.at[k * rows : (k + 1) * rows, :]
            copies.append((source, left.at[k * rows : (k + 1) * rows, :]))
        for copy in fetch(copies, sems):
            copy.wait()
        total = dot(left[...], right[...], contract) + arrived[...].astype(WIDE)
        for k, out in ((3, corner), (1, across), (2, along), (0, own)):
            out[...] = total[k * rows : (k + 1) * rows].astype(out.dtype)

    outs = (shape(WIDE, rows, width),) + (shape(NARROW, rows, width),) * 3
    return call(
        kernel,
        name,
        outs,
        (left, right, arrived),
        [
            pltpu.VMEM((4 * rows, deep), NARROW),
            pltpu.VMEM(right.shape, NARROW),
            pltpu.VMEM(arrived.shape, NARROW),
            pltpu.SemaphoreType.DMA((6,)),
        ],
        8 * rows * deep * width,
        in_place=True,
    )


def pieces(ffpart, even, own):
    runs = []
    for z in range(own // ffpart):
        for start, stop in ((0, even), (even, own)):
            low, high = max(z * ffpart, start), min((z + 1) * ffpart, stop)
            if low < high:
                at_gate = low if start == 0 else 2 * even + low - even
                at_up = even + low if start == 0 else own + low
                runs.append((z, low, high, at_gate, at_up))
    return runs


def in_prepare(weight, gains, marks, taps, teams):
    part, width = weight.shape
    features = width // 3
    channels = features // TEAM
    slots = max(128, TEAM * part) // part

    def kernel(weight, gain_one, gain_two, marks, taps, out, wide, small):
        index = lax.axis_index("dp")
        whole = weight[...].astype(WIDE)
        small[...] = jnp.zeros_like(small)
        for slot in range(slots):
            mine = lax.rem(index, slots) == slot
            for row, gain in enumerate((gain_one, gain_two)):
                value = gain[...].astype(WIDE)
                value = jnp.where(mine, value, jnp.zeros_like(value))
                small[row : row + 1, slot * part : (slot + 1) * part] = value
        small[0:1, 2 * channels :] = marks[...].astype(WIDE)
        for slot in range(teams):
            value = taps[...].astype(WIDE)
            value = jnp.where(index // TEAM == slot, value, jnp.zeros_like(value))
            for k in range(3):
                to = k * channels + slot * part
                small[2:3, to : to + part] = value[k : k + 1, :]
        for p in range(TEAM):
            for k in range(3):
                for z in range(teams):
                    source = k * features + (z * TEAM + p) * part
                    to = k * channels + z * part
                    wide[:, to : to + part] = whole[:, source : source + part]
            out[p, :part, :] = wide[...].astype(NARROW)
            out[p, part:, :] = small[...].astype(NARROW)

    return call(
        kernel,
        "in_prepare",
        shape(NARROW, TEAM, part + 8, 3 * channels),
        (weight, *gains, marks, taps),
        [pltpu.VMEM((part, 3 * channels), WIDE), pltpu.VMEM((8, 3 * channels), WIDE)],
    )


def in_finish(blocks, weight, gain, teams):
    part, width = weight.shape
    features = width // 3
    channels = features // TEAM

    def kernel(blocks, weight, gain, out, gain_grad):
        for p in range(TEAM):
            block = blocks[p].astype(WIDE)
            for k in range(3):
                for z in range(teams):
                    to = k * features + (z * TEAM + p) * part
                    source = k * channels + z * part
                    out[:, to : to + part] = block[:, source : source + part]
        product = jnp.sum(weight[...].astype(WIDE) * out[...], axis=1, keepdims=True)
        gain_grad[...] = (product / gain[...].astype(WIDE)).reshape(1, part)

    outs = (shape(WIDE, part, width), shape(WIDE, 1, part))
    return call(kernel, "in_finish", outs, (blocks, weight, gain))


def pair_prepare(gate, up, teams):
    part, inner = gate.shape
    own = inner // TEAM
    ffpart = own // teams
    even = own // 128 * 128
    runs = pieces(ffpart, even, own)

    def kernel(gate, up, out, wide):
        gates, ups = gate[...].astype(WIDE), up[...].astype(WIDE)
        for p in range(TEAM):
            for z, low, high, at_gate, at_up in runs:
                source = (z * TEAM + p) * ffpart + low - z * ffpart
                size = high - low
                wide[:, at_gate : at_gate + size] = gates[:, source : source + size]
                wide[:, at_up : at_up + size] = ups[:, source : source + size]
            out[p] = wide[...].astype(NARROW)

    out = shape(NARROW, TEAM, part, 2 * own)
    scratch = [pltpu.VMEM((part, 2 * own), WIDE)]
    return call(kernel, "pair_prepare", out, (gate, up), scratch)


def pair_finish(blocks, gate, up, gain, teams):
    part, inner = gate.shape
    own = inner // TEAM
    ffpart = own // teams
    even = own // 128 * 128
    runs = pieces(ffpart, even, own)

    def kernel(blocks, gate, up, gain, gate_grad, up_grad, gain_grad):
        for p in range(TEAM):
            block = blocks[p].astype(WIDE)
            for z, low, high, at_gate, at_up in runs:
                to = (z * TEAM + p) * ffpart + low - z * ffpart
                size = high - low
                gate_grad[:, to : to + size] = block[:, at_gate : at_gate + size]
                up_grad[:, to : to + size] = block[:, at_up : at_up + size]
        product = gate[...].astype(WIDE) * gate_grad[...] + up[...].astype(WIDE) * up_grad[...]
        total = jnp.sum(product, axis=1, keepdims=True) / gain[...].astype(WIDE)
        gain_grad[...] = total.reshape(1, part)

    outs = (shape(WIDE, part, inner), shape(WIDE, part, inner), shape(WIDE, 1, part))
    return call(kernel, "pair_finish", outs, (blocks, gate, up, gain))


def mixer_forward(blocks, before, weights):
    rows, features = blocks[0].shape
    tokens = TEAM * rows
    count, _, channels = weights.shape
    channels = channels // 3
    teams = count // TEAM
    share, part = features // teams, features // count

    def kernel(*refs):
        blocks, (before, weights), refs = refs[:TEAM], refs[TEAM : TEAM + 2], refs[TEAM + 2 :]
        normed, mixed, gated, conv, mixer_in, in_own, gain, gain_two, taps, keeps = refs[:10]
        hs, small, sems = refs[10:]
        place, team = where_am_i()
        copies = [(weights.at[:, part:, :], small)]
        for d in range(count):
            to = in_own.at[d * part : (d + 1) * part, :]
            copies.append((weights.at[d, :part, :], to))
        for m in range(TEAM):
            copies.append((blocks[m], hs.at[at(HALO + (place ^ m) * rows, rows), :]))
        copies.append((before, hs.at[:HALO, :]))
        for copy in fetch(copies, sems):
            copy.wait()
        first = hs[:HALO, :]
        hs[:HALO, :] = jnp.where(team > 0, first, jnp.zeros_like(first))
        total = jnp.zeros((1, 3 * channels), WIDE)
        gain[...] = jnp.zeros_like(gain)
        gain_two[...] = jnp.zeros_like(gain_two)
        span = max(share, 128)
        for z in range(teams):
            both = sum(small[z * TEAM + p].astype(WIDE) for p in range(TEAM))
            one, two = both[0:1], both[1:2]
            total = total + small[z * TEAM + place].astype(WIDE)[2:3]
            to = slice(z * share // span * span, z * share // span * span + span)
            gain[:, to] = gain[:, to] + one[:, :span]
            gain_two[:, to] = gain_two[:, to] + two[:, :span]
        taps[...] = jnp.zeros_like(taps)
        for k in range(3):
            taps[k : k + 1, :] = total[:, k * channels : (k + 1) * channels]
        marks = [
            1.0 - small[team * TEAM + p].astype(WIDE)[0:1, 2 * channels :] for p in range(TEAM)
        ]
        keep = jnp.concatenate([mark.reshape(rows, 1) for mark in marks], 0)
        keeps[8:, 0:1] = keep
        before_team = lax.rem(team + teams - 1, teams) * TEAM + TEAM - 1
        last = 1.0 - small[before_team].astype(WIDE)[0:1, 3 * channels - 1 :]
        keeps[7:8, 0:1] = last
        keeps[8:, 1:2] = keep * keeps[7 : 7 + tokens, 0:1]
        scale = gain[...]

        def norm(start, size):
            values = hs[at(start, size), :].astype(WIDE)
            values = values * scale_of(values) * scale
            normed[at(start, size), :] = values.astype(NARROW)

        norm(0, HALO)

        @pl.loop(0, TEAM)
        def _(step):
            norm(HALO + step * rows, rows)

        mixed[...] = dot(normed[...], in_own[...], ((1,), (0,)))
        gated[...] = (mixed[:, :channels] * mixed[:, 2 * channels :]).astype(NARROW).astype(WIDE)
        conv_out = (
            taps[2:3, :] * gated[HALO:, :]
            + taps[1:2, :] * (keeps[8:, 0:1] * gated[HALO - 1 : HALO - 1 + tokens, :])
            + taps[0:1, :] * (keeps[8:, 1:2] * gated[HALO - 2 : HALO - 2 + tokens, :])
        )
        conv[...] = conv_out
        mixer_in[...] = (mixed[HALO:, channels : 2 * channels] * conv_out).astype(NARROW)

    outs = (
        shape(NARROW, HALO + tokens, features),
        shape(WIDE, HALO + tokens, 3 * channels),
        shape(WIDE, HALO + tokens, channels),
        shape(WIDE, tokens, channels),
        shape(NARROW, tokens, channels),
        shape(NARROW, features, 3 * channels),
        shape(WIDE, 1, features),
        shape(WIDE, 1, features),
        shape(WIDE, 8, channels),
        shape(WIDE, 8 + tokens, 2),
    )
    return call(
        kernel,
        "mixer_forward",
        outs,
        (*blocks, before, weights),
        [
            pltpu.VMEM((HALO + tokens, features), NARROW),
            pltpu.VMEM((count, 8, 3 * channels), NARROW),
            pltpu.SemaphoreType.DMA((count + TEAM + 2,)),
        ],
        2 * tokens * features * 3 * channels,
        in_place=True,
    )


def out_rows(blocks, whole, teams):
    place, team = where_am_i()
    channels = blocks[0].shape[0]
    share = channels // teams
    copies = []
    for m, block in enumerate(blocks):
        for k in range(teams):
            to = (place ^ m) * channels + lax.rem(team - k + teams, teams) * share
            copies.append((block.at[k * share : (k + 1) * share, :], whole.at[at(to, share, 8), :]))
    return copies


def out_project(mixer_blocks, out_blocks, hidden_blocks, gain, teams):
    rows, features = hidden_blocks[0].shape
    tokens, channels = mixer_blocks[0].shape

    def kernel(*refs):
        mixer_in, out_in, hidden_in = [refs[k * TEAM : (k + 1) * TEAM] for k in range(3)]
        gain, resid, odd, even, mixer, turned, out, hidden, sems = refs[3 * TEAM :]
        place, _ = where_am_i()
        copies = out_rows(out_in, out, teams)
        for m in range(TEAM):
            to = mixer.at[:, at((place ^ m) * channels, channels, 128)]
            copies.append((mixer_in[m], to))
        first = len(copies)
        copies += [(hidden_in[m], hidden.at[m]) for m in range(TEAM)]
        copies = fetch(copies, sems)
        for copy in copies[:first]:
            copy.wait()
        for half, side in ((1, odd), (0, even)):
            for k in range(TEAM // 2):
                source = mixer[at((place ^ (2 * k + half)) * rows, rows), :]
                turned[k * rows : (k + 1) * rows, :] = source
            product = dot(turned[...], out[...], ((1,), (0,)))
            if half == 1:
                for copy in copies[first:]:
                    copy.wait()
            for k in range(TEAM // 2):
                span = slice(k * rows, (k + 1) * rows)
                total = hidden[2 * k + half].astype(WIDE) + product[span]
                side[span, :] = (total * scale_of(total) * gain[...]).astype(NARROW)
                if k + half == 0:
                    resid[...] = total

    outs = (shape(WIDE, rows, features),) + (shape(NARROW, tokens // 2, features),) * 2
    any_place, in_vmem = pl.BlockSpec(memory_space=pl.ANY), pl.BlockSpec(memory_space=pltpu.VMEM)
    return call(
        kernel,
        "out_project",
        outs,
        (*mixer_blocks, *out_blocks, *hidden_blocks, gain),
        [
            pltpu.VMEM((tokens, features), NARROW),
            pltpu.VMEM((tokens // 2, features), NARROW),
            pltpu.VMEM((features, features), NARROW),
            pltpu.VMEM((TEAM, rows, features), NARROW),
            pltpu.SemaphoreType.DMA((TEAM * teams + 2 * TEAM,)),
        ],
        2 * tokens * features * features,
        in_place=[any_place] * (3 * TEAM) + [in_vmem],
    )


def ffn_parts(gate, up, grad):
    sigmoid = 1.0 / (1.0 + jnp.exp(-gate))
    scaled = gate * sigmoid
    gate_grad = grad * up * sigmoid * (1.0 + gate * (1.0 - sigmoid))
    return scaled * up, gate_grad, grad * scaled


def ffn_block(odd, even, upstream, pair, down):
    count = len(upstream)
    rows, features = upstream[0].shape
    own = down.shape[0]
    units = own // 128 * 128
    width = own - units
    half = odd.shape[0]

    def kernel(odd_in, even_in, *refs):
        g_in, (pair_in, down_in), refs = refs[:count], refs[count : count + 2], refs[count + 2 :]
        acts, grads, weight, back = refs[:2], refs[2:4], refs[4], refs[5]
        xs, gs, pair, down, last, all_grads, sems = refs[6:]
        first = [(odd_in, xs.at[:half, :]), (pair_in, pair)]
        second = [(g_in[k], gs.at[k * rows : (k + 1) * rows, :]) for k in range(count)]
        second += [(down_in, down), (even_in, xs.at[half:, :])]
        copies = fetch(first + second, sems)
        for copy in copies[:2]:
            copy.wait()
        for side in range(2):
            span = slice(side * half, (side + 1) * half)
            act, grad_out = acts[side], grads[side]
            x = xs[span, :]
            gate = dot(x, pair[:, :units], ((1,), (0,)))
            up = dot(x, pair[:, units : 2 * units], ((1,), (0,)))
            if side == 0:
                for copy in copies[2:]:
                    copy.wait()
                last[:width, :] = down[units:, :]
                last[width:, :] = down[units:, :]
            g = gs[span, :]
            grad = dot(g, down[:units, :], ((1,), (1,)))
            value, gate_grad, up_grad = ffn_parts(gate, up, grad)
            act[:, :units] = value.astype(NARROW)
            all_grads[span, :units] = gate_grad.astype(NARROW)
            all_grads[span, units : 2 * units] = up_grad.astype(NARROW)
            both = dot(x, pair[:, 2 * units :], ((1,), (0,)))
            turned = pltpu.roll(both, width, 1)
            lower = lax.broadcasted_iota(jnp.int32, both.shape, 1) < width
            grad = dot(g, last[...], ((1,), (1,)))
            value, gate_grad, up_grad = ffn_parts(
                jnp.where(lower, both, turned), jnp.where(lower, turned, both), grad
            )
            act[:, units:] = value[:, :width].astype(NARROW)
            all_grads[span, 2 * units :] = jnp.where(lower, gate_grad, up_grad).astype(NARROW)
            grad_out[...] = all_grads[span, :]
        back[...] = dot(all_grads[:half, :], pair[...], ((1,), (1,))).astype(NARROW)
        for start in range(0, features, 256):
            total = dot(xs[:, start : start + 256], all_grads[...], ((0,), (0,)))
            weight[start : start + 256, :] = total.astype(NARROW)

    outs = (shape(NARROW, half, own),) * 2 + (shape(NARROW, half, 2 * own),) * 2
    return call(
        kernel,
        "ffn",
        outs + (shape(NARROW, features, 2 * own), shape(NARROW, half, features)),
        (odd, even, *upstream, pair, down),
        [
            pltpu.VMEM((2 * half, features), NARROW),
            pltpu.VMEM((2 * half, features), NARROW),
            pltpu.VMEM((features, 2 * own), NARROW),
            pltpu.VMEM((own, features), NARROW),
            pltpu.VMEM((2 * width, features), NARROW),
            pltpu.VMEM((2 * half, 2 * own), NARROW),
            pltpu.SemaphoreType.DMA((count + 4,)),
        ],
        20 * half * features * own,
        in_place=True,
    )


def product(left, right, turned, name):
    contract = ((1,), (1,)) if turned else ((1,), (0,))

    def kernel(left, right, out):
        out[...] = dot(left[...], right[...], contract).astype(NARROW)

    rows, wide = left.shape[0], right.shape[0 if turned else 1]
    return call(kernel, name, shape(NARROW, rows, wide), (left, right), flops=2 * rows * right.size)


def weight_grads(lefts, rights, name):
    deep, wide = lefts[0].shape[1], rights[0].shape[1]
    tokens = sum(left.shape[0] for left in lefts)

    def kernel(*refs):
        ins, (out, left, right, sems) = refs[: len(lefts) + len(rights)], refs[-4:]
        pairs = []
        for blocks, whole in ((ins[: len(lefts)], left), (ins[len(lefts) :], right)):
            row = 0
            for block in blocks:
                pairs.append((block, whole.at[row : row + block.shape[0], :]))
                row += block.shape[0]
        for copy in fetch(pairs, sems):
            copy.wait()
        for start in range(0, deep, 256):
            stop = min(start + 256, deep)
            total = dot(left[:, start:stop], right[...], ((0,), (0,)))
            out[start:stop, :] = total.astype(NARROW)

    return call(
        kernel,
        name,
        shape(NARROW, deep, wide),
        (*lefts, *rights),
        [
            pltpu.VMEM((tokens, deep), NARROW),
            pltpu.VMEM((tokens, wide), NARROW),
            pltpu.SemaphoreType.DMA((len(lefts) + len(rights),)),
        ],
        2 * tokens * deep * wide,
        in_place=True,
    )


def resid_back(parts, resid, gain, upstream, out_blocks, teams):
    rows, features = resid.shape
    channels = features // TEAM

    def kernel(own, corner, across, along, resid, gain, upstream, *refs):
        out_in, (resid_grad, rounded, mixer_grad, out, sems) = refs[:TEAM], refs[TEAM:]
        copies = fetch(out_rows(out_in, out, teams), sems)
        grad = own[...] + sum(part[...].astype(WIDE) for part in (corner, across, along))
        values = resid[...]
        scale = scale_of(values)
        grad = upstream[...].astype(WIDE) + norm_back(grad, values * scale, scale, gain[...])
        resid_grad[...] = grad
        rounded[...] = grad.astype(NARROW)
        for copy in copies:
            copy.wait()
        product = dot(rounded[...], out[...], ((1,), (1,))).astype(NARROW)
        for p in range(TEAM):
            mixer_grad[p] = product[:, p * channels : (p + 1) * channels]

    outs = (
        shape(WIDE, rows, features),
        shape(NARROW, rows, features),
        shape(NARROW, TEAM, rows, channels),
    )
    any_place, in_vmem = pl.BlockSpec(memory_space=pl.ANY), pl.BlockSpec(memory_space=pltpu.VMEM)
    return call(
        kernel,
        "resid_back",
        outs,
        (*parts, resid, gain, upstream, *out_blocks),
        [
            pltpu.VMEM((features, features), NARROW),
            pltpu.SemaphoreType.DMA((TEAM * teams,)),
        ],
        2 * rows * features * features,
        in_place=[in_vmem] * 7 + [any_place] * TEAM,
    )


def conv_back(mixer_grad, mixed, gated, conv, taps, keeps):
    tokens, channels = conv.shape

    def kernel(mixer_grad, mixed, gated, conv, taps, keeps, part, rim, taps_grad, ones, twos):
        grad = mixer_grad[...].astype(WIDE)
        conv_grad = grad * mixed[HALO:, channels : 2 * channels]
        one, two = keeps[8:, 0:1] * conv_grad, keeps[8:, 1:2] * conv_grad
        zeros = jnp.zeros((8, channels), WIDE)
        taps_grad[...] = zeros
        for k, (left, back) in enumerate(((two, 2), (one, 1), (conv_grad, 0))):
            product = left * gated[HALO - back : HALO - back + tokens, :]
            taps_grad[k : k + 1, :] = jnp.sum(product, axis=0, keepdims=True)
        ones[:tokens, :] = taps[1:2, :] * one
        twos[:tokens, :] = taps[0:1, :] * two
        ones[tokens:, :] = zeros
        twos[tokens:, :] = zeros
        rim[...] = zeros
        rim[6:7, :] = twos[0:1, :]
        rim[7:8, :] = twos[1:2, :] + ones[0:1, :]
        part[...] = taps[2:3, :] * conv_grad + ones[1 : tokens + 1, :] + twos[2 : tokens + 2, :]

    outs = (shape(WIDE, tokens, channels), shape(WIDE, 8, channels), shape(WIDE, 8, channels))
    scratch = [pltpu.VMEM((tokens + 8, channels), WIDE)] * 2
    return call(
        kernel, "conv_back", outs, (mixer_grad, mixed, gated, conv, taps, keeps), scratch
    )


def mixer_back(part, returned, mixer_grad, mixed, conv, normed, in_own, teams):
    tokens, channels = conv.shape
    features = in_own.shape[0]
    rows, share = tokens // TEAM, features // teams

    def kernel(*refs):
        part, returned, mixer_grad, mixed, conv, normed, in_own, grads, odd = refs[:9]
        shares, (side, whole, weight) = refs[9 : 9 + teams], refs[9 + teams :]
        place, team = where_am_i()
        whole[...] = part[...]
        whole[tokens - 8 :, :] = part[tokens - 8 :, :] + returned[...]
        gated_grad = whole[...]
        grads[:, :channels] = (gated_grad * mixed[HALO:, 2 * channels :]).astype(NARROW)
        grads[:, channels : 2 * channels] = (
            mixer_grad[...].astype(WIDE) * conv[...]
        ).astype(NARROW)
        grads[:, 2 * channels :] = (gated_grad * mixed[HALO:, :channels]).astype(NARROW)
        for chip in range(TEAM // 2):
            at_place = place ^ (2 * chip + 1)
            side[chip * rows : (chip + 1) * rows, :] = grads[at(at_place * rows, rows), :]
        step = features // 4
        for start in range(0, features, step):
            span = slice(start, start + step)
            weight[span, :] = dot(normed[HALO:, span], grads[...], ((0,), (0,)))
        for k in range(teams):
            owner = lax.rem(team + k, teams)
            shares[k][...] = weight[at(owner * share, share), :].astype(shares[k].dtype)
        odd[...] = dot(side[...], in_own[...], ((1,), (1,))).astype(NARROW)

    outs = (shape(NARROW, tokens, 3 * channels), shape(NARROW, tokens // 2, features))
    outs += tuple(
        shape(NARROW if k == teams - 1 else WIDE, share, 3 * channels) for k in range(teams)
    )
    grads, odd, *shares = call(
        kernel,
        "mixer_back",
        outs,
        (part, returned, mixer_grad, mixed, conv, normed, in_own),
        [
            pltpu.VMEM((tokens // 2, 3 * channels), NARROW),
            pltpu.VMEM((tokens, channels), WIDE),
            pltpu.VMEM((features, 3 * channels), WIDE),
        ],
        3 * tokens * features * 3 * channels,
    )
    return grads, odd, shares


def out_back(mixer_in, blocks, taps_grad, teams):
    rows, features = blocks[0].shape
    channels = mixer_in.shape[1]
    share = channels // teams
    low = (share + 15) // 16 * 16

    def kernel(*refs):
        mixer_in, blocks, taps_grad = refs[0], refs[1 : 1 + TEAM], refs[1 + TEAM]
        shares, (total,) = refs[2 + TEAM : 2 + TEAM + teams], refs[2 + TEAM + teams :]
        place, team = where_am_i()
        total[...] = sum(
            dot(mixer_in[at((place ^ m) * rows, rows), :], blocks[m][...], ((0,), (0,)))
            for m in range(TEAM)
        )
        for k in range(teams):
            owner = lax.rem(team + k, teams)
            kind = shares[k].dtype
            shares[k][...] = jnp.zeros_like(shares[k])
            shares[k][:share, :] = total[at(owner * share, share, 8), :].astype(kind)
            shares[k][low : low + 8, :channels] = taps_grad[...].astype(kind)

    outs = tuple(
        shape(NARROW if k == teams - 1 else WIDE, low + 16, features) for k in range(teams)
    )
    return call(
        kernel,
        "out_back",
        outs,
        (mixer_in, *blocks, taps_grad),
        [pltpu.VMEM((channels, features), WIDE)],
        2 * TEAM * rows * channels * features,
    ), low


def body(
    hidden_in,
    seq_start,
    mixer_gain,
    in_weight,
    conv_weight,
    out_weight,
    ffn_gain,
    gate_weight,
    up_weight,
    down_weight,
    cotangent,
):
    net = Net()
    teams = net.teams
    rows, features = hidden_in.shape
    inner = gate_weight.shape[2]
    part = features // net.count
    ffpart = inner // net.count
    channels = features // TEAM
    ffown = inner // TEAM
    line = [[p + TEAM * z for z in range(teams)] for p in range(TEAM)]


    def gather(value):
        return lax.all_gather(value, "dp", axis=0, tiled=True, axis_index_groups=line)

    def reduce(value):
        return lax.psum_scatter(
            value, "dp", scatter_dimension=0, tiled=True, axis_index_groups=line
        )

    down_own = gather(down_weight[0])
    hidden_job = net.spawn(net.blocks_direct(hidden_in))
    sent = in_prepare(
        in_weight[0],
        (mixer_gain, ffn_gain),
        seq_start.reshape(1, rows),
        conv_weight[0].T,
        teams,
    )
    net.need(sent)
    got_job = net.do(net.exchange, sent)
    pair_job = net.do(lambda *x: pair_prepare(*x, teams), gate_weight[0], up_weight[0])
    net.step()
    out_job = net.spawn(net.line_both(out_weight[0]))
    pair_job = net.do(net.exchange, pair_job.result)
    in_job = net.do(gather, got_job.result.reshape(TEAM * (part + 8), 3 * channels))
    net.until(pair_job, in_job, hidden_job)
    pair_own = gather(pair_job.result.reshape(TEAM * part, 2 * ffown))
    upstream_job = net.spawn(net.blocks(cotangent))

    def last_rows():
        last = hidden_job.result[0][-HALO:]
        for m in range(1, TEAM):
            block = hidden_job.result[m][-HALO:]
            last = jnp.where(net.place == (TEAM - 1) ^ m, block, last)
        (before,) = yield [(last, ("ring", 1))]
        return before

    halo_job = net.spawn(last_rows())
    before, out_rows_here = net.until(halo_job, out_job)
    upstream_job.held = True
    weights = in_job.result.reshape(net.count, part + 8, 3 * channels)
    out_job = net.spawn(net.blocks(out_rows_here))

    mix_job = net.do(
        lambda *x: mixer_forward(x[:TEAM], x[TEAM], x[TEAM + 1]),
        *hidden_job.result, before, weights,
    )
    (normed, mixed, gated, conv, mixer_in, in_own, gain_one, gain_two, taps, keeps) = net.until(
        mix_job
    )
    mixer_job = net.spawn(net.blocks(mixer_in))
    mixer_blocks, out_blocks = net.until(mixer_job, out_job)
    upstream_job.held = False
    project_job = net.do(
        lambda *x: out_project(
            x[:TEAM], x[TEAM : 2 * TEAM], x[2 * TEAM : 3 * TEAM], x[3 * TEAM], teams
        ),
        *mixer_blocks, *out_blocks, *hidden_job.result, gain_two,
    )
    resid, in_odd, in_even = net.until(project_job)
    upstream = net.until(upstream_job)

    ffn_job = net.do(
        lambda *x: ffn_block(x[0], x[1], x[2 : 2 + TEAM], x[2 + TEAM], x[3 + TEAM]),
        in_odd, in_even, *upstream[1::2], *upstream[0::2], pair_own, down_own,
    )
    act_odd, act_even, _, grads_even, pair_all, back_odd = net.until(ffn_job)
    pair_sum = reduce(pair_all)
    ffn_job = net.spawn(
        net.team_sum(
            back_odd,
            lambda arrived: (
                lambda *x: summed_parts(*x, True, "ffn_back"),
                (grads_even, pair_own, arrived),
            ),
        )
    )
    odd_job = net.do(lambda *x: product(*x, False, "ffn_output"), act_odd, down_own)
    net.step()
    output_job = net.spawn(
        net.team_sum(
            odd_job.result,
            lambda arrived: (
                lambda *x: summed_parts(*x, False, "ffn_output_sum"),
                (act_even, down_own, arrived),
            ),
            True,
        )
    )
    net.step()
    down_job = net.do(
        lambda *x: weight_grads(x[:2], x[2:], "down_grads"),
        act_odd, act_even, *upstream[1::2], *upstream[0::2],
    )
    ffn_grad = net.until(ffn_job)
    down_sum = reduce(down_job.result)

    output_job.held = True
    back_job = net.do(
        lambda *x: resid_back(x[:4], *x[4:7], x[7:], teams),
        *ffn_grad, resid, gain_two, cotangent, *out_blocks,
    )
    resid_grad, rounded, mixer_grad = net.until(back_job)
    output_job.held = True
    rounded_job = net.spawn(net.blocks(rounded))
    mixer_grad = net.until(net.do(net.exchange, mixer_grad)).reshape(TEAM * rows, channels)
    rounded_job.held = True
    gated_part, rim, taps_grad = net.until(
        net.do(conv_back, mixer_grad, mixed, gated, conv, taps, keeps)
    )
    rounded_job.held = False
    output_job.held = False

    def rim_steps():
        (returned,) = yield [(rim, ("back",))]
        return returned

    returned = net.until(net.spawn(rim_steps()))
    output_job.held = True
    mixed_grad, normed_odd, shares = net.until(
        net.do(
            lambda *x: mixer_back(*x, teams),
            gated_part, returned, mixer_grad, mixed, conv, normed, in_own,
        )
    )
    in_job = net.spawn(net.line_sum(shares))
    pair_job = net.do(net.exchange, pair_sum.reshape(TEAM, part, 2 * ffown))
    normed_job = net.spawn(
        net.team_sum(
            normed_odd,
            lambda arrived: (
                lambda *x: summed_parts(*x, True, "mixer_back_sum", True),
                (mixed_grad, in_own, arrived),
            ),
            span=2,
        )
    )
    low = (part + 15) // 16 * 16
    out_job = net.do(
        lambda *x: out_back(x[0], x[1 : 1 + TEAM], x[1 + TEAM], teams)[0],
        mixer_in, *net.until(rounded_job), taps_grad,
    )
    net.until(out_job)
    output_job.held = False
    net.need(down_sum)
    out_job = net.spawn(net.line_sum(out_job.result))
    in_grad = net.until(in_job).astype(NARROW)
    in_job = net.do(net.exchange, in_grad.reshape(TEAM, part, 3 * channels))
    finish_job = net.do(
        lambda *x: pair_finish(*x, teams),
        net.until(pair_job), gate_weight[0], up_weight[0], ffn_gain.reshape(part, 1),
    )
    in_grad = net.until(in_job)
    grad_gate, grad_up, grad_ffn_gain = net.until(finish_job)
    normed_grad, ffn_out, out_pack = net.until(normed_job, output_job, out_job)
    in_grad, grad_mixer_gain = in_finish(
        in_grad, in_weight[0], mixer_gain.reshape(part, 1), teams
    )

    def total(parts):
        return sum([part.astype(WIDE) for part in parts[1:]], parts[0])

    own_hidden = hidden_in.astype(WIDE)
    scale_one = scale_of(own_hidden)
    grad_hidden = resid_grad + norm_back(
        total(normed_grad), own_hidden * scale_one, scale_one, gain_one
    )
    hidden_out = (resid + total(ffn_out)).astype(NARROW)
    grad_out = out_pack[:part]
    grad_conv = lax.dynamic_slice(out_pack, (low, net.team * part), (3, part)).T
    return (
        hidden_out,
        grad_hidden,
        grad_mixer_gain,
        in_grad[None],
        grad_conv[None],
        grad_out[None],
        grad_ffn_gain,
        grad_gate[None],
        grad_up[None],
        down_sum.astype(WIDE)[None],
    )


def solution(mesh):
    tokens, wide, deep = P("dp", None), P(None, "dp"), P(None, "dp", None)
    return jax.shard_map(
        body,
        mesh=mesh,
        in_specs=(tokens, P("dp"), wide, deep, deep, deep, wide, deep, deep, deep, tokens),
        out_specs=(tokens, tokens, wide, deep, deep, deep, wide, deep, deep, deep),
        check_vma=False,
    )
```

```python
import jax
import jax.numpy as jnp
from jax import lax
from jax.experimental import pallas as pl
from jax.experimental.pallas import tpu as pltpu
from jax.sharding import PartitionSpec as P

epsilon = 1e-05
TEAM = 8
HALO = 16
WIDE = jnp.float32
NARROW = jnp.bfloat16


def dot(left, right, contract):
    return lax.dot_general(left, right, (contract, ((), ())), preferred_element_type=WIDE)


def fetch(pairs, sems):
    copies = [pltpu.make_async_copy(a, b, sems.at[i]) for i, (a, b) in enumerate(pairs)]
    for copy in copies:
        copy.start()
    return copies


def shape(kind, *sizes):
    return jax.ShapeDtypeStruct(sizes, kind)


def call(kernel, name, out_shape, operands, scratch=(), flops=0, in_place=False):
    places = {}
    if in_place:
        spec = pl.BlockSpec(memory_space=pl.ANY)
        places["in_specs"] = [spec] * len(operands) if in_place is True else in_place
    size = sum(x.size * x.dtype.itemsize for x in operands)
    return pl.pallas_call(
        kernel,
        out_shape=out_shape,
        scratch_shapes=list(scratch),
        compiler_params=pltpu.CompilerParams(vmem_limit_bytes=52 * 2**20),
        cost_estimate=pl.CostEstimate(flops=flops, bytes_accessed=size, transcendentals=0),
        name=name,
        **places,
    )(*operands)


class Job:
    def __init__(self, steps):
        self.steps = steps
        self.result = None
        self.open = True
        self.request = None
        self.held = False
        self.send(None)

    def send(self, value):
        try:
            self.request = self.steps.send(value)
        except StopIteration as stop:
            self.result, self.open, self.request = stop.value, False, None


class Net:
    def __init__(self):
        self.count = lax.axis_size("dp")
        self.teams = self.count // TEAM
        self.index = lax.axis_index("dp")
        self.place = self.index % TEAM
        self.team = self.index // TEAM
        self.core = self.index % 2
        self.peer = (self.index // 2) % 4
        self.jobs = []
        self.waiting = []
        self.gate = []
        self.extra = []

    def pairs(self, move):
        if move[0] == "swap":
            return [(i, i ^ move[1]) for i in range(self.count)]
        if move[0] == "ring":
            return [(i, (i + move[1] * TEAM) % self.count) for i in range(self.count)]
        if move[0] == "mixed":
            return [(i, i ^ (2 if i % 2 == 0 else 4)) for i in range(self.count)]
        return [(i, i - TEAM) for i in range(TEAM, self.count)]

    def do(self, call, *operands, span=1):
        def steps():
            (got,) = yield [(operands, ("call", call), span)]
            return got

        return self.spawn(steps())

    def spawn(self, steps):
        job = Job(steps)
        if job.open:
            self.jobs.append(job)
        return job

    def need(self, *values):
        self.extra.extend(values)

    def later(self, value):
        return lax.optimization_barrier((value, self.gate))[0]

    def step(self, times=1):
        for _ in range(times):
            self.one_step()

    def one_step(self):
        ready = [job for job in self.jobs if job.request is not None and not job.held]
        values = [move[0] for job in ready for move in job.request]
        self.raw = []
        if values or self.waiting:
            values, _ = lax.optimization_barrier((values, (self.gate, self.extra)))
            self.extra = []
            at = 0
            for job in ready:
                span = 1
                got = []
                moves = job.request
                for move in moves:
                    if len(move) > 2:
                        span = move[2]
                    if move[1][0] == "call":
                        got.append(move[1][1](*values[at]))
                    else:
                        got.append(lax.ppermute(values[at], "dp", self.pairs(move[1])))
                    at += 1
                job.request = None
                self.raw.extend(zip([move[1] for move in moves], got))
                self.waiting.append([span, job, got])
        for entry in self.waiting:
            entry[0] -= 1
        done = [entry for entry in self.waiting if entry[0] <= 0]
        self.waiting = [entry for entry in self.waiting if entry[0] > 0]
        results = lax.optimization_barrier([entry[2] for entry in done])
        self.gate = results
        for (_, job, _), got in zip(done, results):
            job.send(got)
        self.jobs = [job for job in self.jobs if job.open]

    def until(self, *jobs):
        while any(job.open for job in jobs):
            self.one_step()
        return [job.result for job in jobs] if len(jobs) > 1 else jobs[0].result


    def blocks(self, value):
        across, along, twin = yield [
            (value, ("swap", 2)),
            (value, ("swap", 4)),
            (value, ("swap", 1)),
        ]
        corner, across_twin, along_twin = yield [
            (jnp.where(self.core == 0, along, across), ("mixed",)),
            (across, ("swap", 1)),
            (along, ("swap", 1)),
        ]
        (corner_twin,) = yield [(corner, ("swap", 1))]
        return [value, twin, across, across_twin, along, along_twin, corner, corner_twin]

    def blocks_direct(self, value):
        found = yield [(value, ("swap", mask)) for mask in (2, 4, 6, 1)]
        twins = yield [(block, ("swap", 1)) for block in found[:3]]
        return [value, found[3], found[0], twins[0], found[1], twins[1], found[2], twins[2]]

    def team_sum(self, odd, fold, split=False, span=1):
        (arrived,) = yield [(odd, ("swap", 1))]
        call, operands = fold(arrived)
        (parts,) = yield [(operands, ("call", call))]
        sends = [(part, ("swap", mask), span) for part, mask in zip(parts[1:], (6, 2, 4))]
        if split:
            corner = yield sends[:1]
            return [parts[0]] + corner + (yield sends[1:])
        moved = yield sends
        return [parts[0]] + moved

    def exchange(self, blocks):
        groups = [[base + q for q in range(TEAM)] for base in range(0, self.count, TEAM)]
        return lax.all_to_all(blocks, "dp", 0, 0, axis_index_groups=groups, tiled=True)

    def line_both(self, value):
        teams = self.teams
        found, up, down = {0: value}, value, value
        for step in range(1, teams // 2 + 1):
            moves = [(up, ("ring", 1))]
            if step < teams - step:
                moves.append((down, ("ring", teams - 1)))
            got = yield moves
            found[step], up = got[0], got[0]
            if len(got) > 1:
                found[teams - step], down = got[1], got[1]
        return jnp.concatenate([found[k] for k in range(teams)], 0)

    def line_send(self, parts, span=1):
        return (yield [(part, ("ring", k + 1), span) for k, part in enumerate(parts)])

    def line_sum(self, shares):
        total = shares[-1].astype(NARROW)
        for share in reversed(shares[:-1]):
            (got,) = yield [(total, ("ring", 1))]
            total = share + got.astype(WIDE)
            total = total if share is shares[0] else total.astype(NARROW)
        return total


def scale_of(values):
    return lax.rsqrt(jnp.mean(values * values, axis=1, keepdims=True) + epsilon)


def norm_back(upstream, normed, scaler, gain):
    scaled = upstream * gain
    return scaler * (scaled - normed * jnp.mean(scaled * normed, axis=1, keepdims=True))


def where_am_i():
    index = lax.axis_index("dp")
    return index % TEAM, index // TEAM


def at(start, size, step=16):
    return pl.ds(pl.multiple_of(start, step), size)


def summed_parts(left, right, arrived, turned, name, relative=False):
    rows, width = arrived.shape[0] // 4, arrived.shape[1]
    deep = left.shape[1]
    contract = ((1,), (1,)) if turned else ((1,), (0,))

    def kernel(left_in, right_in, arrived_in, own, corner, across, along, left, right, arrived, sems):
        place, _ = where_am_i()
        copies = [(right_in, right), (arrived_in, arrived)]
        for k in range(4):
            source = left_in
            if relative:
                source = left_in.at[at((place ^ (2 * k)) * rows, rows), :]
            else:
                source = left_in.at[k * rows : (k + 1) * rows, :]
            copies.append((source, left.at[k * rows : (k + 1) * rows, :]))
        for copy in fetch(copies, sems):
            copy.wait()
        total = dot(left[...], right[...], contract) + arrived[...].astype(WIDE)
        for k, out in ((3, corner), (1, across), (2, along), (0, own)):
            out[...] = total[k * rows : (k + 1) * rows].astype(out.dtype)

    outs = (shape(WIDE, rows, width),) + (shape(NARROW, rows, width),) * 3
    return call(
        kernel,
        name,
        outs,
        (left, right, arrived),
        [
            pltpu.VMEM((4 * rows, deep), NARROW),
            pltpu.VMEM(right.shape, NARROW),
            pltpu.VMEM(arrived.shape, NARROW),
            pltpu.SemaphoreType.DMA((6,)),
        ],
        8 * rows * deep * width,
        in_place=True,
    )


def pieces(ffpart, even, own):
    runs = []
    for z in range(own // ffpart):
        for start, stop in ((0, even), (even, own)):
            low, high = max(z * ffpart, start), min((z + 1) * ffpart, stop)
            if low < high:
                at_gate = low if start == 0 else 2 * even + low - even
                at_up = even + low if start == 0 else own + low
                runs.append((z, low, high, at_gate, at_up))
    return runs


def in_prepare(weight, gains, marks, taps, teams):
    part, width = weight.shape
    features = width // 3
    channels = features // TEAM
    slots = max(128, TEAM * part) // part

    def kernel(weight, gain_one, gain_two, marks, taps, out, wide, small):
        index = lax.axis_index("dp")
        whole = weight[...].astype(WIDE)
        small[...] = jnp.zeros_like(small)
        for slot in range(slots):
            mine = lax.rem(index, slots) == slot
            for row, gain in enumerate((gain_one, gain_two)):
                value = gain[...].astype(WIDE)
                value = jnp.where(mine, value, jnp.zeros_like(value))
                small[row : row + 1, slot * part : (slot + 1) * part] = value
        small[0:1, 2 * channels :] = marks[...].astype(WIDE)
        for slot in range(teams):
            value = taps[...].astype(WIDE)
            value = jnp.where(index // TEAM == slot, value, jnp.zeros_like(value))
            for k in range(3):
                to = k * channels + slot * part
                small[2:3, to : to + part] = value[k : k + 1, :]
        for p in range(TEAM):
            for k in range(3):
                for z in range(teams):
                    source = k * features + (z * TEAM + p) * part
                    to = k * channels + z * part
                    wide[:, to : to + part] = whole[:, source : source + part]
            out[p, :part, :] = wide[...].astype(NARROW)
            out[p, part:, :] = small[...].astype(NARROW)

    return call(
        kernel,
        "in_prepare",
        shape(NARROW, TEAM, part + 8, 3 * channels),
        (weight, *gains, marks, taps),
        [pltpu.VMEM((part, 3 * channels), WIDE), pltpu.VMEM((8, 3 * channels), WIDE)],
    )


def in_finish(blocks, weight, gain, teams):
    part, width = weight.shape
    features = width // 3
    channels = features // TEAM

    def kernel(blocks, weight, gain, out, gain_grad):
        for p in range(TEAM):
            block = blocks[p].astype(WIDE)
            for k in range(3):
                for z in range(teams):
                    to = k * features + (z * TEAM + p) * part
                    source = k * channels + z * part
                    out[:, to : to + part] = block[:, source : source + part]
        product = jnp.sum(weight[...].astype(WIDE) * out[...], axis=1, keepdims=True)
        gain_grad[...] = (product / gain[...].astype(WIDE)).reshape(1, part)

    outs = (shape(WIDE, part, width), shape(WIDE, 1, part))
    return call(kernel, "in_finish", outs, (blocks, weight, gain))


def pair_prepare(gate, up, teams):
    part, inner = gate.shape
    own = inner // TEAM
    ffpart = own // teams
    even = own // 128 * 128
    runs = pieces(ffpart, even, own)

    def kernel(gate, up, out, wide):
        gates, ups = gate[...].astype(WIDE), up[...].astype(WIDE)
        for p in range(TEAM):
            for z, low, high, at_gate, at_up in runs:
                source = (z * TEAM + p) * ffpart + low - z * ffpart
                size = high - low
                wide[:, at_gate : at_gate + size] = gates[:, source : source + size]
                wide[:, at_up : at_up + size] = ups[:, source : source + size]
            out[p] = wide[...].astype(NARROW)

    out = shape(NARROW, TEAM, part, 2 * own)
    scratch = [pltpu.VMEM((part, 2 * own), WIDE)]
    return call(kernel, "pair_prepare", out, (gate, up), scratch)


def pair_finish(blocks, gate, up, gain, teams):
    part, inner = gate.shape
    own = inner // TEAM
    ffpart = own // teams
    even = own // 128 * 128
    runs = pieces(ffpart, even, own)

    def kernel(blocks, gate, up, gain, gate_grad, up_grad, gain_grad):
        for p in range(TEAM):
            block = blocks[p].astype(WIDE)
            for z, low, high, at_gate, at_up in runs:
                to = (z * TEAM + p) * ffpart + low - z * ffpart
                size = high - low
                gate_grad[:, to : to + size] = block[:, at_gate : at_gate + size]
                up_grad[:, to : to + size] = block[:, at_up : at_up + size]
        product = gate[...].astype(WIDE) * gate_grad[...] + up[...].astype(WIDE) * up_grad[...]
        total = jnp.sum(product, axis=1, keepdims=True) / gain[...].astype(WIDE)
        gain_grad[...] = total.reshape(1, part)

    outs = (shape(WIDE, part, inner), shape(WIDE, part, inner), shape(WIDE, 1, part))
    return call(kernel, "pair_finish", outs, (blocks, gate, up, gain))


def mixer_forward(blocks, before, weights):
    rows, features = blocks[0].shape
    tokens = TEAM * rows
    count, _, channels = weights.shape
    channels = channels // 3
    teams = count // TEAM
    share, part = features // teams, features // count

    def kernel(*refs):
        blocks, (before, weights), refs = refs[:TEAM], refs[TEAM : TEAM + 2], refs[TEAM + 2 :]
        normed, mixed, gated, conv, mixer_in, in_own, gain, gain_two, taps, keeps = refs[:10]
        hs, small, sems = refs[10:]
        place, team = where_am_i()
        copies = [(weights.at[:, part:, :], small)]
        for d in range(count):
            to = in_own.at[d * part : (d + 1) * part, :]
            copies.append((weights.at[d, :part, :], to))
        for m in range(TEAM):
            copies.append((blocks[m], hs.at[at(HALO + (place ^ m) * rows, rows), :]))
        copies.append((before, hs.at[:HALO, :]))
        for copy in fetch(copies, sems):
            copy.wait()
        first = hs[:HALO, :]
        hs[:HALO, :] = jnp.where(team > 0, first, jnp.zeros_like(first))
        total = jnp.zeros((1, 3 * channels), WIDE)
        gain[...] = jnp.zeros_like(gain)
        gain_two[...] = jnp.zeros_like(gain_two)
        span = max(share, 128)
        for z in range(teams):
            both = sum(small[z * TEAM + p].astype(WIDE) for p in range(TEAM))
            one, two = both[0:1], both[1:2]
            total = total + small[z * TEAM + place].astype(WIDE)[2:3]
            to = slice(z * share // span * span, z * share // span * span + span)
            gain[:, to] = gain[:, to] + one[:, :span]
            gain_two[:, to] = gain_two[:, to] + two[:, :span]
        taps[...] = jnp.zeros_like(taps)
        for k in range(3):
            taps[k : k + 1, :] = total[:, k * channels : (k + 1) * channels]
        marks = [
            1.0 - small[team * TEAM + p].astype(WIDE)[0:1, 2 * channels :] for p in range(TEAM)
        ]
        keep = jnp.concatenate([mark.reshape(rows, 1) for mark in marks], 0)
        keeps[8:, 0:1] = keep
        before_team = lax.rem(team + teams - 1, teams) * TEAM + TEAM - 1
        last = 1.0 - small[before_team].astype(WIDE)[0:1, 3 * channels - 1 :]
        keeps[7:8, 0:1] = last
        keeps[8:, 1:2] = keep * keeps[7 : 7 + tokens, 0:1]
        scale = gain[...]

        def norm(start, size):
            values = hs[at(start, size), :].astype(WIDE)
            values = values * scale_of(values) * scale
            normed[at(start, size), :] = values.astype(NARROW)

        norm(0, HALO)

        @pl.loop(0, TEAM)
        def _(step):
            norm(HALO + step * rows, rows)

        mixed[...] = dot(normed[...], in_own[...], ((1,), (0,)))
        gated[...] = (mixed[:, :channels] * mixed[:, 2 * channels :]).astype(NARROW).astype(WIDE)
        conv_out = (
            taps[2:3, :] * gated[HALO:, :]
            + taps[1:2, :] * (keeps[8:, 0:1] * gated[HALO - 1 : HALO - 1 + tokens, :])
            + taps[0:1, :] * (keeps[8:, 1:2] * gated[HALO - 2 : HALO - 2 + tokens, :])
        )
        conv[...] = conv_out
        mixer_in[...] = (mixed[HALO:, channels : 2 * channels] * conv_out).astype(NARROW)

    outs = (
        shape(NARROW, HALO + tokens, features),
        shape(WIDE, HALO + tokens, 3 * channels),
        shape(WIDE, HALO + tokens, channels),
        shape(WIDE, tokens, channels),
        shape(NARROW, tokens, channels),
        shape(NARROW, features, 3 * channels),
        shape(WIDE, 1, features),
        shape(WIDE, 1, features),
        shape(WIDE, 8, channels),
        shape(WIDE, 8 + tokens, 2),
    )
    return call(
        kernel,
        "mixer_forward",
        outs,
        (*blocks, before, weights),
        [
            pltpu.VMEM((HALO + tokens, features), NARROW),
            pltpu.VMEM((count, 8, 3 * channels), NARROW),
            pltpu.SemaphoreType.DMA((count + TEAM + 2,)),
        ],
        2 * tokens * features * 3 * channels,
        in_place=True,
    )


def out_rows(blocks, whole, teams):
    place, team = where_am_i()
    channels = blocks[0].shape[0]
    share = channels // teams
    copies = []
    for m, block in enumerate(blocks):
        for k in range(teams):
            to = (place ^ m) * channels + lax.rem(team - k + teams, teams) * share
            copies.append((block.at[k * share : (k + 1) * share, :], whole.at[at(to, share, 8), :]))
    return copies


def out_project(mixer_blocks, out_blocks, hidden_blocks, gain, teams):
    rows, features = hidden_blocks[0].shape
    tokens, channels = mixer_blocks[0].shape

    def kernel(*refs):
        mixer_in, out_in, hidden_in = [refs[k * TEAM : (k + 1) * TEAM] for k in range(3)]
        gain, resid, odd, even, mixer, turned, out, hidden, sems = refs[3 * TEAM :]
        place, _ = where_am_i()
        copies = out_rows(out_in, out, teams)
        for m in range(TEAM):
            to = mixer.at[:, at((place ^ m) * channels, channels, 128)]
            copies.append((mixer_in[m], to))
        first = len(copies)
        copies += [(hidden_in[m], hidden.at[m]) for m in range(TEAM)]
        copies = fetch(copies, sems)
        for copy in copies[:first]:
            copy.wait()
        for half, side in ((1, odd), (0, even)):
            for k in range(TEAM // 2):
                source = mixer[at((place ^ (2 * k + half)) * rows, rows), :]
                turned[k * rows : (k + 1) * rows, :] = source
            product = dot(turned[...], out[...], ((1,), (0,)))
            if half == 1:
                for copy in copies[first:]:
                    copy.wait()
            for k in range(TEAM // 2):
                span = slice(k * rows, (k + 1) * rows)
                total = hidden[2 * k + half].astype(WIDE) + product[span]
                side[span, :] = (total * scale_of(total) * gain[...]).astype(NARROW)
                if k + half == 0:
                    resid[...] = total

    outs = (shape(WIDE, rows, features),) + (shape(NARROW, tokens // 2, features),) * 2
    any_place, in_vmem = pl.BlockSpec(memory_space=pl.ANY), pl.BlockSpec(memory_space=pltpu.VMEM)
    return call(
        kernel,
        "out_project",
        outs,
        (*mixer_blocks, *out_blocks, *hidden_blocks, gain),
        [
            pltpu.VMEM((tokens, features), NARROW),
            pltpu.VMEM((tokens // 2, features), NARROW),
            pltpu.VMEM((features, features), NARROW),
            pltpu.VMEM((TEAM, rows, features), NARROW),
            pltpu.SemaphoreType.DMA((TEAM * teams + 2 * TEAM,)),
        ],
        2 * tokens * features * features,
        in_place=[any_place] * (3 * TEAM) + [in_vmem],
    )


def ffn_parts(gate, up, grad):
    sigmoid = 1.0 / (1.0 + jnp.exp(-gate))
    scaled = gate * sigmoid
    gate_grad = grad * up * sigmoid * (1.0 + gate * (1.0 - sigmoid))
    return scaled * up, gate_grad, grad * scaled


def ffn_block(odd, even, upstream, pair, down):
    count = len(upstream)
    rows, features = upstream[0].shape
    own = down.shape[0]
    units = own // 128 * 128
    width = own - units
    half = odd.shape[0]

    def kernel(odd_in, even_in, *refs):
        g_in, (pair_in, down_in), refs = refs[:count], refs[count : count + 2], refs[count + 2 :]
        acts, grads, weight, back = refs[:2], refs[2:4], refs[4], refs[5]
        xs, gs, pair, down, last, all_grads, sems = refs[6:]
        first = [(odd_in, xs.at[:half, :]), (pair_in, pair)]
        second = [(g_in[k], gs.at[k * rows : (k + 1) * rows, :]) for k in range(count)]
        second += [(down_in, down), (even_in, xs.at[half:, :])]
        copies = fetch(first + second, sems)
        for copy in copies[:2]:
            copy.wait()
        for side in range(2):
            span = slice(side * half, (side + 1) * half)
            act, grad_out = acts[side], grads[side]
            x = xs[span, :]
            gate = dot(x, pair[:, :units], ((1,), (0,)))
            up = dot(x, pair[:, units : 2 * units], ((1,), (0,)))
            if side == 0:
                for copy in copies[2:]:
                    copy.wait()
                last[:width, :] = down[units:, :]
                last[width:, :] = down[units:, :]
            g = gs[span, :]
            grad = dot(g, down[:units, :], ((1,), (1,)))
            value, gate_grad, up_grad = ffn_parts(gate, up, grad)
            act[:, :units] = value.astype(NARROW)
            all_grads[span, :units] = gate_grad.astype(NARROW)
            all_grads[span, units : 2 * units] = up_grad.astype(NARROW)
            both = dot(x, pair[:, 2 * units :], ((1,), (0,)))
            turned = pltpu.roll(both, width, 1)
            lower = lax.broadcasted_iota(jnp.int32, both.shape, 1) < width
            grad = dot(g, last[...], ((1,), (1,)))
            value, gate_grad, up_grad = ffn_parts(
                jnp.where(lower, both, turned), jnp.where(lower, turned, both), grad
            )
            act[:, units:] = value[:, :width].astype(NARROW)
            all_grads[span, 2 * units :] = jnp.where(lower, gate_grad, up_grad).astype(NARROW)
            grad_out[...] = all_grads[span, :]
        back[...] = dot(all_grads[:half, :], pair[...], ((1,), (1,))).astype(NARROW)
        for start in range(0, features, 256):
            total = dot(xs[:, start : start + 256], all_grads[...], ((0,), (0,)))
            weight[start : start + 256, :] = total.astype(NARROW)

    outs = (shape(NARROW, half, own),) * 2 + (shape(NARROW, half, 2 * own),) * 2
    return call(
        kernel,
        "ffn",
        outs + (shape(NARROW, features, 2 * own), shape(NARROW, half, features)),
        (odd, even, *upstream, pair, down),
        [
            pltpu.VMEM((2 * half, features), NARROW),
            pltpu.VMEM((2 * half, features), NARROW),
            pltpu.VMEM((features, 2 * own), NARROW),
            pltpu.VMEM((own, features), NARROW),
            pltpu.VMEM((2 * width, features), NARROW),
            pltpu.VMEM((2 * half, 2 * own), NARROW),
            pltpu.SemaphoreType.DMA((count + 4,)),
        ],
        20 * half * features * own,
        in_place=True,
    )


def product(left, right, turned, name):
    contract = ((1,), (1,)) if turned else ((1,), (0,))

    def kernel(left, right, out):
        out[...] = dot(left[...], right[...], contract).astype(NARROW)

    rows, wide = left.shape[0], right.shape[0 if turned else 1]
    return call(kernel, name, shape(NARROW, rows, wide), (left, right), flops=2 * rows * right.size)


def weight_grads(lefts, rights, name):
    deep, wide = lefts[0].shape[1], rights[0].shape[1]
    tokens = sum(left.shape[0] for left in lefts)

    def kernel(*refs):
        ins, (out, left, right, sems) = refs[: len(lefts) + len(rights)], refs[-4:]
        pairs = []
        for blocks, whole in ((ins[: len(lefts)], left), (ins[len(lefts) :], right)):
            row = 0
            for block in blocks:
                pairs.append((block, whole.at[row : row + block.shape[0], :]))
                row += block.shape[0]
        for copy in fetch(pairs, sems):
            copy.wait()
        for start in range(0, deep, 256):
            stop = min(start + 256, deep)
            total = dot(left[:, start:stop], right[...], ((0,), (0,)))
            out[start:stop, :] = total.astype(NARROW)

    return call(
        kernel,
        name,
        shape(NARROW, deep, wide),
        (*lefts, *rights),
        [
            pltpu.VMEM((tokens, deep), NARROW),
            pltpu.VMEM((tokens, wide), NARROW),
            pltpu.SemaphoreType.DMA((len(lefts) + len(rights),)),
        ],
        2 * tokens * deep * wide,
        in_place=True,
    )


def resid_back(parts, resid, gain, upstream, out_blocks, teams):
    rows, features = resid.shape
    channels = features // TEAM

    def kernel(own, corner, across, along, resid, gain, upstream, *refs):
        out_in, (resid_grad, rounded, mixer_grad, out, sems) = refs[:TEAM], refs[TEAM:]
        copies = fetch(out_rows(out_in, out, teams), sems)
        grad = own[...] + sum(part[...].astype(WIDE) for part in (corner, across, along))
        values = resid[...]
        scale = scale_of(values)
        grad = upstream[...].astype(WIDE) + norm_back(grad, values * scale, scale, gain[...])
        resid_grad[...] = grad
        rounded[...] = grad.astype(NARROW)
        for copy in copies:
            copy.wait()
        product = dot(rounded[...], out[...], ((1,), (1,))).astype(NARROW)
        for p in range(TEAM):
            mixer_grad[p] = product[:, p * channels : (p + 1) * channels]

    outs = (
        shape(WIDE, rows, features),
        shape(NARROW, rows, features),
        shape(NARROW, TEAM, rows, channels),
    )
    any_place, in_vmem = pl.BlockSpec(memory_space=pl.ANY), pl.BlockSpec(memory_space=pltpu.VMEM)
    return call(
        kernel,
        "resid_back",
        outs,
        (*parts, resid, gain, upstream, *out_blocks),
        [
            pltpu.VMEM((features, features), NARROW),
            pltpu.SemaphoreType.DMA((TEAM * teams,)),
        ],
        2 * rows * features * features,
        in_place=[in_vmem] * 7 + [any_place] * TEAM,
    )


def conv_back(mixer_grad, mixed, gated, conv, taps, keeps):
    tokens, channels = conv.shape

    def kernel(mixer_grad, mixed, gated, conv, taps, keeps, part, rim, taps_grad, ones, twos):
        grad = mixer_grad[...].astype(WIDE)
        conv_grad = grad * mixed[HALO:, channels : 2 * channels]
        one, two = keeps[8:, 0:1] * conv_grad, keeps[8:, 1:2] * conv_grad
        zeros = jnp.zeros((8, channels), WIDE)
        taps_grad[...] = zeros
        for k, (left, back) in enumerate(((two, 2), (one, 1), (conv_grad, 0))):
            product = left * gated[HALO - back : HALO - back + tokens, :]
            taps_grad[k : k + 1, :] = jnp.sum(product, axis=0, keepdims=True)
        ones[:tokens, :] = taps[1:2, :] * one
        twos[:tokens, :] = taps[0:1, :] * two
        ones[tokens:, :] = zeros
        twos[tokens:, :] = zeros
        rim[...] = zeros
        rim[6:7, :] = twos[0:1, :]
        rim[7:8, :] = twos[1:2, :] + ones[0:1, :]
        part[...] = taps[2:3, :] * conv_grad + ones[1 : tokens + 1, :] + twos[2 : tokens + 2, :]

    outs = (shape(WIDE, tokens, channels), shape(WIDE, 8, channels), shape(WIDE, 8, channels))
    scratch = [pltpu.VMEM((tokens + 8, channels), WIDE)] * 2
    return call(
        kernel, "conv_back", outs, (mixer_grad, mixed, gated, conv, taps, keeps), scratch
    )


def mixer_back(part, returned, mixer_grad, mixed, conv, normed, in_own, teams):
    tokens, channels = conv.shape
    features = in_own.shape[0]
    rows, share = tokens // TEAM, features // teams

    def kernel(*refs):
        part, returned, mixer_grad, mixed, conv, normed, in_own, grads, odd = refs[:9]
        shares, (side, whole, weight) = refs[9 : 9 + teams], refs[9 + teams :]
        place, team = where_am_i()
        whole[...] = part[...]
        whole[tokens - 8 :, :] = part[tokens - 8 :, :] + returned[...]
        gated_grad = whole[...]
        grads[:, :channels] = (gated_grad * mixed[HALO:, 2 * channels :]).astype(NARROW)
        grads[:, channels : 2 * channels] = (
            mixer_grad[...].astype(WIDE) * conv[...]
        ).astype(NARROW)
        grads[:, 2 * channels :] = (gated_grad * mixed[HALO:, :channels]).astype(NARROW)
        for chip in range(TEAM // 2):
            at_place = place ^ (2 * chip + 1)
            side[chip * rows : (chip + 1) * rows, :] = grads[at(at_place * rows, rows), :]
        step = features // 4
        for start in range(0, features, step):
            span = slice(start, start + step)
            weight[span, :] = dot(normed[HALO:, span], grads[...], ((0,), (0,)))
        for k in range(teams):
            owner = lax.rem(team + k, teams)
            shares[k][...] = weight[at(owner * share, share), :].astype(shares[k].dtype)
        odd[...] = dot(side[...], in_own[...], ((1,), (1,))).astype(NARROW)

    outs = (shape(NARROW, tokens, 3 * channels), shape(NARROW, tokens // 2, features))
    outs += tuple(
        shape(NARROW if k == teams - 1 else WIDE, share, 3 * channels) for k in range(teams)
    )
    grads, odd, *shares = call(
        kernel,
        "mixer_back",
        outs,
        (part, returned, mixer_grad, mixed, conv, normed, in_own),
        [
            pltpu.VMEM((tokens // 2, 3 * channels), NARROW),
            pltpu.VMEM((tokens, channels), WIDE),
            pltpu.VMEM((features, 3 * channels), WIDE),
        ],
        3 * tokens * features * 3 * channels,
    )
    return grads, odd, shares


def out_back(mixer_in, blocks, taps_grad, teams):
    rows, features = blocks[0].shape
    channels = mixer_in.shape[1]
    share = channels // teams
    low = (share + 15) // 16 * 16

    def kernel(*refs):
        mixer_in, blocks, taps_grad = refs[0], refs[1 : 1 + TEAM], refs[1 + TEAM]
        shares, (total,) = refs[2 + TEAM : 2 + TEAM + teams], refs[2 + TEAM + teams :]
        place, team = where_am_i()
        total[...] = sum(
            dot(mixer_in[at((place ^ m) * rows, rows), :], blocks[m][...], ((0,), (0,)))
            for m in range(TEAM)
        )
        for k in range(teams):
            owner = lax.rem(team + k, teams)
            kind = shares[k].dtype
            shares[k][...] = jnp.zeros_like(shares[k])
            shares[k][:share, :] = total[at(owner * share, share, 8), :].astype(kind)
            shares[k][low : low + 8, :channels] = taps_grad[...].astype(kind)

    outs = tuple(
        shape(NARROW if k == teams - 1 else WIDE, low + 16, features) for k in range(teams)
    )
    return call(
        kernel,
        "out_back",
        outs,
        (mixer_in, *blocks, taps_grad),
        [pltpu.VMEM((channels, features), WIDE)],
        2 * TEAM * rows * channels * features,
    ), low


def body(
    hidden_in,
    seq_start,
    mixer_gain,
    in_weight,
    conv_weight,
    out_weight,
    ffn_gain,
    gate_weight,
    up_weight,
    down_weight,
    cotangent,
):
    net = Net()
    teams = net.teams
    rows, features = hidden_in.shape
    inner = gate_weight.shape[2]
    part = features // net.count
    ffpart = inner // net.count
    channels = features // TEAM
    ffown = inner // TEAM
    line = [[p + TEAM * z for z in range(teams)] for p in range(TEAM)]


    def gather(value):
        return lax.all_gather(value, "dp", axis=0, tiled=True, axis_index_groups=line)

    def reduce(value):
        return lax.psum_scatter(
            value, "dp", scatter_dimension=0, tiled=True, axis_index_groups=line
        )

    down_own = gather(down_weight[0])
    hidden_job = net.spawn(net.blocks_direct(hidden_in))
    sent = in_prepare(
        in_weight[0],
        (mixer_gain, ffn_gain),
        seq_start.reshape(1, rows),
        conv_weight[0].T,
        teams,
    )
    net.need(sent)
    got_job = net.do(net.exchange, sent)
    pair_job = net.do(lambda *x: pair_prepare(*x, teams), gate_weight[0], up_weight[0])
    net.step()
    out_job = net.spawn(net.line_both(out_weight[0]))
    pair_job = net.do(net.exchange, pair_job.result)
    in_job = net.do(gather, got_job.result.reshape(TEAM * (part + 8), 3 * channels))
    net.until(pair_job, in_job, hidden_job)
    pair_own = gather(pair_job.result.reshape(TEAM * part, 2 * ffown))
    upstream_job = net.spawn(net.blocks(cotangent))

    def last_rows():
        last = hidden_job.result[0][-HALO:]
        for m in range(1, TEAM):
            block = hidden_job.result[m][-HALO:]
            last = jnp.where(net.place == (TEAM - 1) ^ m, block, last)
        (before,) = yield [(last, ("ring", 1))]
        return before

    halo_job = net.spawn(last_rows())
    before, out_rows_here = net.until(halo_job, out_job)
    upstream_job.held = True
    weights = in_job.result.reshape(net.count, part + 8, 3 * channels)
    out_job = net.spawn(net.blocks(out_rows_here))

    mix_job = net.do(
        lambda *x: mixer_forward(x[:TEAM], x[TEAM], x[TEAM + 1]),
        *hidden_job.result, before, weights,
    )
    (normed, mixed, gated, conv, mixer_in, in_own, gain_one, gain_two, taps, keeps) = net.until(
        mix_job
    )
    mixer_job = net.spawn(net.blocks(mixer_in))
    mixer_blocks, out_blocks = net.until(mixer_job, out_job)
    upstream_job.held = False
    project_job = net.do(
        lambda *x: out_project(
            x[:TEAM], x[TEAM : 2 * TEAM], x[2 * TEAM : 3 * TEAM], x[3 * TEAM], teams
        ),
        *mixer_blocks, *out_blocks, *hidden_job.result, gain_two,
    )
    resid, in_odd, in_even = net.until(project_job)
    upstream = net.until(upstream_job)

    ffn_job = net.do(
        lambda *x: ffn_block(x[0], x[1], x[2 : 2 + TEAM], x[2 + TEAM], x[3 + TEAM]),
        in_odd, in_even, *upstream[1::2], *upstream[0::2], pair_own, down_own,
    )
    act_odd, act_even, _, grads_even, pair_all, back_odd = net.until(ffn_job)
    pair_sum = reduce(pair_all)
    ffn_job = net.spawn(
        net.team_sum(
            back_odd,
            lambda arrived: (
                lambda *x: summed_parts(*x, True, "ffn_back"),
                (grads_even, pair_own, arrived),
            ),
        )
    )
    odd_job = net.do(lambda *x: product(*x, False, "ffn_output"), act_odd, down_own)
    net.step()
    output_job = net.spawn(
        net.team_sum(
            odd_job.result,
            lambda arrived: (
                lambda *x: summed_parts(*x, False, "ffn_output_sum"),
                (act_even, down_own, arrived),
            ),
            True,
        )
    )
    net.step()
    down_job = net.do(
        lambda *x: weight_grads(x[:2], x[2:], "down_grads"),
        act_odd, act_even, *upstream[1::2], *upstream[0::2],
    )
    ffn_grad = net.until(ffn_job)
    down_sum = reduce(down_job.result)

    output_job.held = True
    back_job = net.do(
        lambda *x: resid_back(x[:4], *x[4:7], x[7:], teams),
        *ffn_grad, resid, gain_two, cotangent, *out_blocks,
    )
    resid_grad, rounded, mixer_grad = net.until(back_job)
    output_job.held = True
    rounded_job = net.spawn(net.blocks(rounded))
    mixer_grad = net.until(net.do(net.exchange, mixer_grad)).reshape(TEAM * rows, channels)
    rounded_job.held = True
    gated_part, rim, taps_grad = net.until(
        net.do(conv_back, mixer_grad, mixed, gated, conv, taps, keeps)
    )
    rounded_job.held = False
    output_job.held = False

    def rim_steps():
        (returned,) = yield [(rim, ("back",))]
        return returned

    returned = net.until(net.spawn(rim_steps()))
    output_job.held = True
    mixed_grad, normed_odd, shares = net.until(
        net.do(
            lambda *x: mixer_back(*x, teams),
            gated_part, returned, mixer_grad, mixed, conv, normed, in_own,
        )
    )
    in_job = net.spawn(net.line_sum(shares))
    pair_job = net.do(net.exchange, pair_sum.reshape(TEAM, part, 2 * ffown), span=2)
    normed_job = net.spawn(
        net.team_sum(
            normed_odd,
            lambda arrived: (
                lambda *x: summed_parts(*x, True, "mixer_back_sum", True),
                (mixed_grad, in_own, arrived),
            ),
            span=2,
        )
    )
    low = (part + 15) // 16 * 16
    out_job = net.do(
        lambda *x: out_back(x[0], x[1 : 1 + TEAM], x[1 + TEAM], teams)[0],
        mixer_in, *net.until(rounded_job), taps_grad,
    )
    net.until(out_job)
    output_job.held = False
    net.need(down_sum)
    out_job = net.spawn(net.line_sum(out_job.result))
    in_grad = net.until(in_job).astype(NARROW)
    in_job = net.do(net.exchange, in_grad.reshape(TEAM, part, 3 * channels))
    finish_job = net.do(
        lambda *x: pair_finish(*x, teams),
        net.until(pair_job), gate_weight[0], up_weight[0], ffn_gain.reshape(part, 1),
    )
    in_grad = net.until(in_job)
    grad_gate, grad_up, grad_ffn_gain = net.until(finish_job)
    normed_grad, ffn_out, out_pack = net.until(normed_job, output_job, out_job)
    in_grad, grad_mixer_gain = in_finish(
        in_grad, in_weight[0], mixer_gain.reshape(part, 1), teams
    )

    def total(parts):
        return sum([part.astype(WIDE) for part in parts[1:]], parts[0])

    own_hidden = hidden_in.astype(WIDE)
    scale_one = scale_of(own_hidden)
    grad_hidden = resid_grad + norm_back(
        total(normed_grad), own_hidden * scale_one, scale_one, gain_one
    )
    hidden_out = (resid + total(ffn_out)).astype(NARROW)
    grad_out = out_pack[:part]
    grad_conv = lax.dynamic_slice(out_pack, (low, net.team * part), (3, part)).T
    return (
        hidden_out,
        grad_hidden,
        grad_mixer_gain,
        in_grad[None],
        grad_conv[None],
        grad_out[None],
        grad_ffn_gain,
        grad_gate[None],
        grad_up[None],
        down_sum.astype(WIDE)[None],
    )


def solution(mesh):
    tokens, wide, deep = P("dp", None), P(None, "dp"), P(None, "dp", None)
    return jax.shard_map(
        body,
        mesh=mesh,
        in_specs=(tokens, P("dp"), wide, deep, deep, deep, wide, deep, deep, deep, tokens),
        out_specs=(tokens, tokens, wide, deep, deep, deep, wide, deep, deep, deep),
        check_vma=False,
    )
```
